256 devices in a mesh: seq: 64 (over z, y, x_hi), mdl: 4 (over x_lo, core).
Axes of the slice: x: 4 (x_hi: 2, x_lo: 2; x = x_hi * 2 + x_lo), y: 4, z: 8, core: 2. Of those that a mesh axis runs over, the one named last changes fastest.
Arguments:
- tokens: bfloat16 [16384, 2048], P('seq', 'mdl'), may hold values from -6 to 6
- norm_gain: bfloat16 [2048], P('mdl'), may hold values from 0.099609375 to 1.8984375
- w_query: bfloat16 [2048, 2048], P('seq', 'mdl'), may hold values from -0.125 to 0.125
- key_matrix: bfloat16 [2048, 1024], P('seq', 'mdl'), may hold values from -0.125 to 0.125
- value_matrix: bfloat16 [2048, 1024], P('seq', 'mdl'), may hold values from -0.125 to 0.125
- w_gate: bfloat16 [2048, 2048], P('seq', 'mdl'), may hold values from -0.125 to 0.125
- q_gain: float32 [128], replicated, may hold values from 0.6 to 8
- k_gain: float32 [128], replicated, may hold values from 0.6 to 8
- w_out: bfloat16 [2048, 2048], P('mdl', 'seq'), may hold values from -0.125 to 0.125
- prompt_lengths: int32 [64], replicated, may hold values from 1 to 512, as said below
- segment_ids: int32 [16384], P('seq'), may hold values from 0 to 63, as said below
- tenant_ranges: int32 [4, 2], replicated, may hold values from 0 to 64, as said below
- key_mask: int32 [16384], P('seq'), may hold values 0 or 1
- cache_slot: int32 [64], replicated, may hold values from 0 to 63, each once
Outputs:
- layer_out: bfloat16 [16384, 2048], P('seq', 'mdl')
- cache_keys: bfloat16 [64, 512, 1024], P('seq', None, 'mdl')
- cache_values: bfloat16 [64, 512, 1024], P('seq', None, 'mdl')
The draws below stay inside these ranges and needn't reach their ends.
Inputs may be any that keep to these rules, and one draw needn't show every extreme that they name: `prompt_lengths`: the lengths sum to 16384 and one of them equals 512. `segment_ids`: request r holds the prompt_lengths[r] consecutive tokens that follow those of requests 0 to r - 1. `tenant_ranges`: each row (lo, hi) has lo < hi; the rows increase and do not intersect; the first lo is 0 and the last hi is 64; request lo of a tenant is its shared prompt. `cache_slot`: each slot belongs to one request.
All inputs are finite; a program needn't handle non-finite values. No bound on the sum of `key_mask` on one device may be relied on, other than what follows from the above.
Results may differ from the reference program's by a relative error of at most 0.012.
The reference program's roundings to bfloat16 on the way count: a program that leaves them out, or rounds other values in their place, can miss the bound.
Values may be sent and summed in bfloat16 or wider, within the bound.
A program may use at most 128 MiB of HBM per device.

```python
import math
import jax
import jax.numpy as jnp
from jax import lax

MODEL_WIDTH = 2048
QUERY_HEADS = 16
KEY_VALUE_HEADS = 8
HEAD_SIZE = 128
TENANTS = 4
STREAM_TOKENS = 16384
REQ = 64
LMAX = 512


def pack_lengths(key):
    base = jax.random.fold_in(key, 11)
    weight_key, place_key = jax.random.split(base)
    weights = jax.random.randint(weight_key, (REQ - 1,), 32, 65)
    spare = STREAM_TOKENS - LMAX - (REQ - 1)
    shares = spare * weights // jnp.sum(weights)
    leftover = spare - jnp.sum(shares)
    order = jnp.arange(REQ - 1)
    others = 1 + shares + (order < leftover).astype(jnp.int32)
    place = jax.random.randint(place_key, (), 0, REQ)
    index = jnp.arange(REQ)
    before = others[jnp.clip(index - 1, 0, REQ - 2)]
    after = others[jnp.clip(index, 0, REQ - 2)]
    return jnp.where(index < place, after, jnp.where(index == place, LMAX, before)).astype(jnp.int32)


def draw_prompt_lengths(key, part):
    return pack_lengths(key)


def draw_segment_ids(key, part):
    lengths = pack_lengths(key)
    ends = jnp.cumsum(lengths)
    positions = jnp.arange(STREAM_TOKENS)
    return jnp.sum((positions[:, None] >= ends[None, :]).astype(jnp.int32), axis=1).astype(jnp.int32)


def draw_tenant_ranges(key, part):
    picked = jax.random.permutation(jax.random.fold_in(key, 23), REQ - 1)[:2 * TENANTS - 2] + 1
    inner = jnp.sort(picked).astype(jnp.int32)
    bounds = jnp.concatenate([jnp.zeros((1,), jnp.int32), inner, jnp.full((1,), REQ, jnp.int32)])
    return bounds.reshape(TENANTS, 2)


def draw_q_gain(key, part):
    inner_key = jax.random.fold_in(key, 31)
    return jax.random.uniform(inner_key, (HEAD_SIZE,), jnp.float32, 0.6, 1.6)


def draw_k_gain(key, part):
    inner_key = jax.random.fold_in(key, 37)
    return jax.random.uniform(inner_key, (HEAD_SIZE,), jnp.float32, 0.6, 1.6)


def plant(result, own_key, smallest, largest):
    dims = result.shape
    index_at = [jax.random.randint(jax.random.fold_in(own_key, axis), (), 0, dims[axis]) for axis in range(len(dims))]
    result = result.at[tuple(index_at)].set(smallest)
    longest = dims.index(max(dims))
    index_at[longest] = (index_at[longest] + 1) % dims[longest]
    return result.at[tuple(index_at)].set(largest)


def level_of(stream_key, shape, pieces, smallest, high):
    loudness, own = 1.0, jax.random.fold_in(stream_key, 6)
    for axis_at, parts in pieces:
        steps = jnp.exp(jax.random.uniform(jax.random.fold_in(own, axis_at), (parts,), jnp.float32, smallest / len(pieces), high / len(pieces)))
        loudness = loudness * jnp.repeat(steps, shape[axis_at] // parts).reshape([-1 if axis == axis_at else 1 for axis in range(len(shape))])
    return loudness


def scatter_about(key, dims, width, bound, cuts=(), kind=jnp.bfloat16):
    drawn = width * jax.random.normal(key, dims, jnp.float32)
    if cuts:
        drawn = drawn * level_of(key, dims, cuts, -0.22, 0.18)
    return jnp.clip(drawn, -bound, bound).astype(kind)


def setup_inputs(seed: int = 0) -> dict:
    keys = jax.random.split(jax.random.key(seed), 15)
    return {
        "tokens": scatter_about(keys[0], (STREAM_TOKENS, MODEL_WIDTH), 1.0, 6.0, ((0, 64), (1, 4))),
        "norm_gain": jnp.clip(1.0 + 0.18 * jax.random.normal(keys[1], (MODEL_WIDTH,), jnp.float32), 0.099609375, 1.8984375).astype(jnp.bfloat16),
        "w_query": scatter_about(keys[2], (MODEL_WIDTH, QUERY_HEADS * HEAD_SIZE), MODEL_WIDTH ** -0.5, 0.125, ((0, 64), (1, 4))),
        "key_matrix": scatter_about(keys[3], (MODEL_WIDTH, KEY_VALUE_HEADS * HEAD_SIZE), MODEL_WIDTH ** -0.5, 0.125, ((0, 64), (1, 4))),
        "value_matrix": scatter_about(keys[4], (MODEL_WIDTH, KEY_VALUE_HEADS * HEAD_SIZE), MODEL_WIDTH ** -0.5, 0.125, ((0, 64), (1, 4))),
        "w_gate": scatter_about(keys[5], (MODEL_WIDTH, QUERY_HEADS * HEAD_SIZE), MODEL_WIDTH ** -0.5, 0.125, ((0, 64), (1, 4))),
        "q_gain": draw_q_gain(jax.random.fold_in(keys[14], 71), 0),
        "k_gain": draw_k_gain(jax.random.fold_in(keys[14], 71), 0),
        "w_out": scatter_about(keys[8], (QUERY_HEADS * HEAD_SIZE, MODEL_WIDTH), (QUERY_HEADS * HEAD_SIZE) ** -0.5, 0.125, ((0, 4), (1, 64))),
        "prompt_lengths": draw_prompt_lengths(jax.random.fold_in(keys[14], 71), 0),
        "segment_ids": draw_segment_ids(jax.random.fold_in(keys[14], 71), 0),
        "tenant_ranges": draw_tenant_ranges(jax.random.fold_in(keys[14], 71), 0),
        "key_mask": plant((jax.random.randint(keys[12], (STREAM_TOKENS,), 0, 8) < 7).astype(jnp.int32), jax.random.fold_in(keys[12], 1), 0, 1),
        "cache_slot": jax.random.permutation(keys[13], REQ).astype(jnp.int32),
    }


epsilon = 1e-06
rope_base = 1000000.0
masked_score = -1e+30

def head_norm(values, gain_vector):
    return values * lax.rsqrt(lax.optimization_barrier(jnp.mean(values * values, axis=-1, keepdims=True)) + epsilon) * gain_vector

def rotate(values, position):
    half_width = values.shape[-1] // 2
    frequency = rope_base ** (-2.0 * jnp.arange(half_width, dtype=jnp.float32) / values.shape[-1])
    angles = position.astype(jnp.float32)[:, None] * frequency[None, :]
    cosine = jnp.cos(angles)[:, None, :]
    sine_part = jnp.sin(angles)[:, None, :]
    former = values[..., :half_width]
    latter = values[..., half_width:]
    return jnp.concatenate([former * cosine - latter * sine_part, latter * cosine + former * sine_part], axis=-1)

def token_tables(lengths, segments, ranges):
    request_count = lengths.shape[0]
    starts = jnp.cumsum(lengths) - lengths
    requests = jnp.arange(request_count, dtype=jnp.int32)
    member = (requests[:, None] > ranges[None, :, 0]) & (requests[:, None] < ranges[None, :, 1])
    shared_of = lax.optimization_barrier(jnp.sum(jnp.where(member, ranges[None, :, 0] + 3, 0), axis=1)) - 3
    onehot = segments[:, None] == requests[None, :]
    seg_start = lax.optimization_barrier(jnp.sum(jnp.where(onehot, starts[None, :], 0), axis=1))
    shared_req = lax.optimization_barrier(jnp.sum(jnp.where(onehot, shared_of[None, :], 0), axis=1))
    return (starts, seg_start, shared_req)

def reference(tokens, norm_gain, w_query, key_matrix, value_matrix, w_gate, q_gain, k_gain, w_out, prompt_lengths, segment_ids, tenant_ranges, key_mask, cache_slot):
    wide_tokens = tokens.astype(jnp.float32)
    normalized_input = (wide_tokens * lax.rsqrt(lax.optimization_barrier(jnp.mean(wide_tokens * wide_tokens, axis=1, keepdims=True)) + epsilon) * norm_gain.astype(jnp.float32)).astype(jnp.bfloat16)
    query_rows = jnp.dot(normalized_input, w_query, preferred_element_type=jnp.float32).reshape(STREAM_TOKENS, QUERY_HEADS, HEAD_SIZE)
    unprojected_keys = jnp.dot(normalized_input, key_matrix, preferred_element_type=jnp.float32).reshape(STREAM_TOKENS, KEY_VALUE_HEADS, HEAD_SIZE)
    every_value = jnp.dot(normalized_input, value_matrix, preferred_element_type=jnp.float32).astype(jnp.bfloat16)
    gate_logits = jnp.dot(normalized_input, w_gate, preferred_element_type=jnp.float32)
    starts, seg_start, shared_req = token_tables(prompt_lengths, segment_ids, tenant_ranges)
    position = jnp.arange(STREAM_TOKENS, dtype=jnp.int32) - seg_start
    query_rows = rotate(head_norm(query_rows, q_gain), position).astype(jnp.bfloat16)
    every_key = rotate(head_norm(unprojected_keys, k_gain), position).astype(jnp.bfloat16)
    key_tags = jnp.where(key_mask == 1, segment_ids, -2)
    query_group_width = QUERY_HEADS // KEY_VALUE_HEADS
    rows_per_block = math.gcd(STREAM_TOKENS, 512)
    scale_factor = HEAD_SIZE ** (-0.5)
    keys_wide = every_key.astype(jnp.float32)
    broad_values = every_value.astype(jnp.float32).reshape(STREAM_TOKENS, KEY_VALUE_HEADS, HEAD_SIZE)
    columns = jnp.arange(STREAM_TOKENS, dtype=jnp.int32)

    def attend_block(block_offset):
        block_of_queries = lax.dynamic_slice_in_dim(query_rows, block_offset, rows_per_block, 0).astype(jnp.float32).reshape(rows_per_block, KEY_VALUE_HEADS, query_group_width, HEAD_SIZE)
        row_ids = block_offset + jnp.arange(rows_per_block, dtype=jnp.int32)
        row_segs = lax.dynamic_slice_in_dim(segment_ids, block_offset, rows_per_block, 0)
        row_shared = lax.dynamic_slice_in_dim(shared_req, block_offset, rows_per_block, 0)
        visible = (columns[None, :] == row_ids[:, None]) | (columns[None, :] <= row_ids[:, None]) & ((key_tags[None, :] == row_segs[:, None]) | (key_tags[None, :] == row_shared[:, None]))
        allowed = visible[:, None, None, :]
        scores = jnp.einsum('qhgd,khd->qhgk', block_of_queries, keys_wide) * scale_factor
        scores = jnp.where(allowed, scores, masked_score)
        top_score = lax.optimization_barrier(jnp.max(scores, axis=-1, keepdims=True))
        raw_weights = jnp.where(allowed, jnp.exp(scores - top_score), 0.0)
        weights = lax.optimization_barrier(raw_weights.astype(jnp.bfloat16)).astype(jnp.float32)
        totals = lax.optimization_barrier(jnp.sum(raw_weights, axis=-1))
        summed = jnp.einsum('qhgk,khd->qhgd', weights, broad_values)
        return (summed / totals[..., None]).reshape(rows_per_block, QUERY_HEADS * HEAD_SIZE)
    block_starts = jnp.arange(0, STREAM_TOKENS, rows_per_block, dtype=jnp.int32)
    attended = lax.map(attend_block, block_starts).reshape(STREAM_TOKENS, QUERY_HEADS * HEAD_SIZE)
    gated_heads = (attended * jax.nn.sigmoid(gate_logits)).astype(jnp.bfloat16)
    layer_out = (wide_tokens + jnp.dot(gated_heads, w_out, preferred_element_type=jnp.float32)).astype(jnp.bfloat16)
    flat_keys = every_key.reshape(STREAM_TOKENS, KEY_VALUE_HEADS * HEAD_SIZE)
    request_ids = jnp.arange(REQ, dtype=jnp.int32)
    slot_owner = jnp.zeros((REQ,), jnp.int32).at[cache_slot].set(request_ids)
    offsets = jnp.arange(LMAX, dtype=jnp.int32)

    def fill_slot(slot_index):
        request = slot_owner[slot_index]
        source = jnp.clip(starts[request] + offsets, 0, STREAM_TOKENS - 1)
        in_window = (offsets < prompt_lengths[request])[:, None]
        keys_rows = jnp.where(in_window, jnp.take(flat_keys, source, axis=0), jnp.zeros((), jnp.bfloat16))
        values_rows = jnp.where(in_window, jnp.take(every_value, source, axis=0), jnp.zeros((), jnp.bfloat16))
        return (keys_rows, values_rows)
    cache_keys, cache_values = lax.map(fill_slot, request_ids)
    return (layer_out, cache_keys, cache_values)
```

```python
import jax
import jax.numpy as jnp
from jax import lax
from jax.sharding import PartitionSpec as P

HEAD_SIZE = 128
LMAX = 512
KEY_BLOCK = 256


epsilon = 1e-06
rope_base = 1000000.0
masked_score = -1e30


def head_norm(values, gain_vector):
    return (
        values
        * lax.rsqrt(jnp.mean(values * values, axis=-1, keepdims=True) + epsilon)
        * gain_vector
    )


def rotate(values, position):
    half_width = values.shape[-1] // 2
    frequency = rope_base ** (-2.0 * jnp.arange(half_width, dtype=jnp.float32) / values.shape[-1])
    angles = position.astype(jnp.float32)[:, None] * frequency[None, :]
    cosine = jnp.cos(angles)[:, None, :]
    sine_part = jnp.sin(angles)[:, None, :]
    former = values[..., :half_width]
    latter = values[..., half_width:]
    return jnp.concatenate(
        [former * cosine - latter * sine_part, latter * cosine + former * sine_part], axis=-1
    )


def body(
    tokens,
    norm_gain,
    w_query,
    key_matrix,
    value_matrix,
    w_gate,
    q_gain,
    k_gain,
    w_out,
    prompt_lengths,
    segment_ids,
    tenant_ranges,
    key_mask,
    cache_slot,
):
    local_rows = tokens.shape[0]
    weight_rows = w_query.shape[0]
    q_cols = w_query.shape[1]
    kv_cols = key_matrix.shape[1]
    g_cols = w_gate.shape[1]
    seq_size = lax.axis_size("seq")
    stream = local_rows * seq_size
    request_count = prompt_lengths.shape[0]

    mask_cols = local_rows // weight_rows
    mask_block = key_mask.astype(jnp.bfloat16).reshape(weight_rows, mask_cols)
    mask_block = jnp.pad(mask_block, ((0, 0), (0, 128 - mask_cols)))
    packed = jnp.concatenate(
        [w_query, key_matrix, value_matrix, w_gate, w_out.T, mask_block], axis=1
    )
    gathered = lax.all_gather(packed, "seq", axis=0, tiled=True)
    proj_cols = q_cols + 2 * kv_cols + g_cols
    w_proj = gathered[:, :proj_cols]
    w_out_t = gathered[:, proj_cols : proj_cols + w_out.shape[0]]
    all_mask = gathered[:, proj_cols + w_out.shape[0] : proj_cols + w_out.shape[0] + mask_cols]
    all_mask = all_mask.reshape(stream)

    wide_tokens = tokens.astype(jnp.float32)
    full_width = tokens.shape[1] * lax.axis_size("mdl")
    square_total = lax.psum(jnp.sum(wide_tokens * wide_tokens, axis=1), "mdl")
    scaled = (
        wide_tokens
        * lax.rsqrt(square_total / full_width + epsilon)[:, None]
        * norm_gain.astype(jnp.float32)
    )
    normalized_input = lax.all_gather(scaled.astype(jnp.bfloat16), "mdl", axis=1, tiled=True)
    projected = jnp.dot(normalized_input, w_proj, preferred_element_type=jnp.float32)
    query_rows = projected[:, :q_cols]
    unprojected_keys = projected[:, q_cols : q_cols + kv_cols]
    values_raw = projected[:, q_cols + kv_cols : q_cols + 2 * kv_cols]
    gate_logits = projected[:, q_cols + 2 * kv_cols :]

    device_seq = lax.axis_index("seq")
    token_ids = device_seq * local_rows + jnp.arange(local_rows, dtype=jnp.int32)
    starts = jnp.cumsum(prompt_lengths) - prompt_lengths
    ends = starts + prompt_lengths
    requests = jnp.arange(request_count, dtype=jnp.int32)
    member = (requests[:, None] > tenant_ranges[None, :, 0]) & (
        requests[:, None] < tenant_ranges[None, :, 1]
    )
    shared_of = jnp.sum(jnp.where(member, tenant_ranges[None, :, 0] + 3, 0), axis=1) - 3
    onehot = segment_ids[:, None] == requests[None, :]
    seg_start = jnp.sum(jnp.where(onehot, starts[None, :], 0), axis=1)
    shared_req = jnp.sum(jnp.where(onehot, shared_of[None, :], 0), axis=1)
    position = token_ids - seg_start

    query_heads = q_cols // HEAD_SIZE
    kv_heads = kv_cols // HEAD_SIZE
    group = query_heads // kv_heads
    q_rot = (
        rotate(head_norm(query_rows.reshape(local_rows, query_heads, HEAD_SIZE), q_gain), position)
        .astype(jnp.bfloat16)
        .reshape(local_rows, kv_heads, group, HEAD_SIZE)
    )
    k_rot = (
        rotate(head_norm(unprojected_keys.reshape(local_rows, kv_heads, HEAD_SIZE), k_gain), position)
        .astype(jnp.bfloat16)
        .reshape(local_rows, kv_cols)
    )
    values_flat = values_raw.astype(jnp.bfloat16)
    kv_local = jnp.concatenate([k_rot, values_flat], axis=1)
    kv_all = lax.all_gather(kv_local, "seq", axis=0, tiled=True)

    n_blocks = stream // KEY_BLOCK
    block_ids = jnp.arange(n_blocks, dtype=jnp.int32)
    last_block = (device_seq * local_rows + local_rows - 1) // KEY_BLOCK
    first_block = jnp.min(seg_start) // KEY_BLOCK
    needed = (block_ids >= first_block) & (block_ids <= last_block)
    lo = tenant_ranges[:, 0]
    hi = tenant_ranges[:, 1]
    used = jnp.any(
        (segment_ids[:, None] > lo[None, :]) & (segment_ids[:, None] < hi[None, :]), axis=0
    )
    lo_start = jnp.sum(jnp.where(requests[None, :] == lo[:, None], starts[None, :], 0), axis=1)
    lo_end = jnp.sum(jnp.where(requests[None, :] == lo[:, None], ends[None, :], 0), axis=1)
    in_prompt = (
        used[:, None]
        & (block_ids[None, :] >= (lo_start // KEY_BLOCK)[:, None])
        & (block_ids[None, :] <= ((lo_end - 1) // KEY_BLOCK)[:, None])
    )
    needed = needed | jnp.any(in_prompt, axis=0)
    n_needed = jnp.sum(needed.astype(jnp.int32))
    (block_list,) = jnp.nonzero(needed, size=n_blocks, fill_value=0)
    block_list = block_list.astype(jnp.int32)

    row_segs = segment_ids
    row_shared = shared_req
    scale_factor = HEAD_SIZE ** (-0.5)
    head_shape = (local_rows, kv_heads, group)

    def key_block(i, loop_state):
        old_top, old_totals, old_summed = loop_state
        block = block_list[i]
        offset = block * KEY_BLOCK
        kv_part = lax.dynamic_slice_in_dim(kv_all, offset, KEY_BLOCK, 0)
        keys_part = kv_part[:, :kv_cols].reshape(KEY_BLOCK, kv_heads, HEAD_SIZE)
        values_part = kv_part[:, kv_cols:].reshape(KEY_BLOCK, kv_heads, HEAD_SIZE)
        mask_part = lax.dynamic_slice_in_dim(all_mask, offset, KEY_BLOCK, 0)
        columns = offset + jnp.arange(KEY_BLOCK, dtype=jnp.int32)
        col_segs = jnp.sum((columns[:, None] >= ends[None, :]).astype(jnp.int32), axis=1)
        live = mask_part == 1
        own = col_segs[None, :] == row_segs[:, None]
        other = col_segs[None, :] == row_shared[:, None]
        earlier = columns[None, :] <= token_ids[:, None]
        diagonal = columns[None, :] == token_ids[:, None]
        visible = diagonal | (earlier & live[None, :] & (own | other))
        allowed = visible[:, None, None, :]
        scores = (
            jnp.einsum("qhgd,khd->qhgk", q_rot, keys_part, preferred_element_type=jnp.float32)
            * scale_factor
        )
        scores = jnp.where(allowed, scores, masked_score)
        new_top = jnp.maximum(old_top, jnp.max(scores, axis=-1))
        factor = jnp.exp(old_top - new_top)
        raw_weights = jnp.where(allowed, jnp.exp(scores - new_top[..., None]), 0.0)
        new_totals = old_totals * factor + jnp.sum(raw_weights, axis=-1)
        new_summed = old_summed * factor[..., None] + jnp.einsum(
            "qhgk,khd->qhgd",
            raw_weights.astype(jnp.bfloat16),
            values_part,
            preferred_element_type=jnp.float32,
        )
        return (new_top, new_totals, new_summed)

    start_state = (
        jnp.full(head_shape, masked_score, jnp.float32),
        jnp.zeros(head_shape, jnp.float32),
        jnp.zeros(head_shape + (HEAD_SIZE,), jnp.float32),
    )
    top_now, totals, summed = lax.fori_loop(0, n_needed, key_block, start_state)

    my_request = jnp.sum(jnp.where(cache_slot == device_seq, requests, 0))
    my_start = jnp.sum(jnp.where(requests == my_request, starts, 0))
    my_length = jnp.sum(jnp.where(requests == my_request, prompt_lengths, 0))
    offsets = jnp.arange(LMAX, dtype=jnp.int32)
    wanted = my_start + offsets
    in_window = ((wanted < stream) & (offsets < my_length))[:, None]
    source = jnp.clip(wanted, 0, stream - 1)
    cache_rows = jnp.where(in_window, jnp.take(kv_all, source, axis=0), jnp.zeros((), jnp.bfloat16))
    cache_k = cache_rows[:, :kv_cols]
    cache_v = cache_rows[:, kv_cols:]

    attended = (summed / totals[..., None]).reshape(local_rows, query_heads * HEAD_SIZE)
    gated_heads = (attended * jax.nn.sigmoid(gate_logits)).astype(jnp.bfloat16)
    partial_out = lax.dot_general(
        gated_heads,
        w_out_t,
        (((1,), (1,)), ((), ())),
        preferred_element_type=jnp.float32,
    )
    branch_sum = lax.psum_scatter(
        partial_out.astype(jnp.bfloat16), "mdl", scatter_dimension=1, tiled=True
    ).astype(jnp.float32)
    layer_out = (wide_tokens + branch_sum).astype(jnp.bfloat16)
    return (layer_out, cache_k[None], cache_v[None])


def solution(mesh):
    placed = (
        P("seq", "mdl"),
        P("mdl"),
        P("seq", "mdl"),
        P("seq", "mdl"),
        P("seq", "mdl"),
        P("seq", "mdl"),
        P(),
        P(),
        P("mdl", "seq"),
        P(),
        P("seq"),
        P(),
        P("seq"),
        P(),
    )
    return jax.shard_map(
        body,
        mesh=mesh,
        in_specs=placed,
        out_specs=(P("seq", "mdl"), P("seq", None, "mdl"), P("seq", None, "mdl")),
        check_vma=False,
    )
```

```python
import jax
import jax.numpy as jnp
from jax import lax
from jax.sharding import Mesh
from jax.sharding import PartitionSpec as P

HEAD_SIZE = 128
LMAX = 512
KEY_BLOCK = 256


epsilon = 1e-06
rope_base = 1000000.0
masked_score = -1e30


def head_norm(values, gain_vector):
    return (
        values
        * lax.rsqrt(jnp.mean(values * values, axis=-1, keepdims=True) + epsilon)
        * gain_vector
    )


def rotate(values, position):
    half_width = values.shape[-1] // 2
    frequency = rope_base ** (-2.0 * jnp.arange(half_width, dtype=jnp.float32) / values.shape[-1])
    angles = position.astype(jnp.float32)[:, None] * frequency[None, :]
    cosine = jnp.cos(angles)[:, None, :]
    sine_part = jnp.sin(angles)[:, None, :]
    former = values[..., :half_width]
    latter = values[..., half_width:]
    return jnp.concatenate(
        [former * cosine - latter * sine_part, latter * cosine + former * sine_part], axis=-1
    )


SEQ_PARTS = ("z", "y", "xh")


def gather_seq(x):
    for name in reversed(SEQ_PARTS):
        x = lax.all_gather(x, name, axis=0, tiled=True)
    return x


def body(
    tokens,
    norm_gain,
    w_query,
    key_matrix,
    value_matrix,
    w_gate,
    q_gain,
    k_gain,
    w_out,
    prompt_lengths,
    segment_ids,
    tenant_ranges,
    key_mask,
    cache_slot,
):
    local_rows = tokens.shape[0]
    weight_rows = w_query.shape[0]
    q_cols = w_query.shape[1]
    kv_cols = key_matrix.shape[1]
    g_cols = w_gate.shape[1]
    seq_size = lax.axis_size(SEQ_PARTS)
    stream = local_rows * seq_size
    request_count = prompt_lengths.shape[0]

    mask_cols = local_rows // weight_rows
    mask_block = key_mask.astype(jnp.bfloat16).reshape(weight_rows, mask_cols)
    mask_block = jnp.pad(mask_block, ((0, 0), (0, 128 - mask_cols)))
    packed = jnp.concatenate(
        [w_query, key_matrix, value_matrix, w_gate, w_out.T, mask_block], axis=1
    )
    gathered = gather_seq(packed)
    proj_cols = q_cols + 2 * kv_cols + g_cols
    w_proj = gathered[:, :proj_cols]
    w_out_t = gathered[:, proj_cols : proj_cols + w_out.shape[0]]
    all_mask = gathered[:, proj_cols + w_out.shape[0] : proj_cols + w_out.shape[0] + mask_cols]
    all_mask = all_mask.reshape(stream)

    wide_tokens = tokens.astype(jnp.float32)
    full_width = tokens.shape[1] * lax.axis_size("mdl")
    square_total = lax.psum(jnp.sum(wide_tokens * wide_tokens, axis=1), "mdl")
    scaled = (
        wide_tokens
        * lax.rsqrt(square_total / full_width + epsilon)[:, None]
        * norm_gain.astype(jnp.float32)
    )
    normalized_input = lax.all_gather(scaled.astype(jnp.bfloat16), "mdl", axis=1, tiled=True)
    projected = jnp.dot(normalized_input, w_proj, preferred_element_type=jnp.float32)
    query_rows = projected[:, :q_cols]
    unprojected_keys = projected[:, q_cols : q_cols + kv_cols]
    values_raw = projected[:, q_cols + kv_cols : q_cols + 2 * kv_cols]
    gate_logits = projected[:, q_cols + 2 * kv_cols :]

    device_seq = lax.axis_index(SEQ_PARTS)
    token_ids = device_seq * local_rows + jnp.arange(local_rows, dtype=jnp.int32)
    starts = jnp.cumsum(prompt_lengths) - prompt_lengths
    ends = starts + prompt_lengths
    requests = jnp.arange(request_count, dtype=jnp.int32)
    member = (requests[:, None] > tenant_ranges[None, :, 0]) & (
        requests[:, None] < tenant_ranges[None, :, 1]
    )
    shared_of = jnp.sum(jnp.where(member, tenant_ranges[None, :, 0] + 3, 0), axis=1) - 3
    onehot = segment_ids[:, None] == requests[None, :]
    seg_start = jnp.sum(jnp.where(onehot, starts[None, :], 0), axis=1)
    shared_req = jnp.sum(jnp.where(onehot, shared_of[None, :], 0), axis=1)
    position = token_ids - seg_start

    query_heads = q_cols // HEAD_SIZE
    kv_heads = kv_cols // HEAD_SIZE
    group = query_heads // kv_heads
    q_rot = (
        rotate(head_norm(query_rows.reshape(local_rows, query_heads, HEAD_SIZE), q_gain), position)
        .astype(jnp.bfloat16)
        .reshape(local_rows, kv_heads, group, HEAD_SIZE)
    )
    k_rot = (
        rotate(head_norm(unprojected_keys.reshape(local_rows, kv_heads, HEAD_SIZE), k_gain), position)
        .astype(jnp.bfloat16)
        .reshape(local_rows, kv_cols)
    )
    values_flat = values_raw.astype(jnp.bfloat16)
    kv_local = jnp.concatenate([k_rot, values_flat], axis=1)
    kv_all = gather_seq(kv_local)

    n_blocks = stream // KEY_BLOCK
    block_ids = jnp.arange(n_blocks, dtype=jnp.int32)
    last_block = (device_seq * local_rows + local_rows - 1) // KEY_BLOCK
    first_block = jnp.min(seg_start) // KEY_BLOCK
    needed = (block_ids >= first_block) & (block_ids <= last_block)
    lo = tenant_ranges[:, 0]
    hi = tenant_ranges[:, 1]
    used = jnp.any(
        (segment_ids[:, None] > lo[None, :]) & (segment_ids[:, None] < hi[None, :]), axis=0
    )
    lo_start = jnp.sum(jnp.where(requests[None, :] == lo[:, None], starts[None, :], 0), axis=1)
    lo_end = jnp.sum(jnp.where(requests[None, :] == lo[:, None], ends[None, :], 0), axis=1)
    in_prompt = (
        used[:, None]
        & (block_ids[None, :] >= (lo_start // KEY_BLOCK)[:, None])
        & (block_ids[None, :] <= ((lo_end - 1) // KEY_BLOCK)[:, None])
    )
    needed = needed | jnp.any(in_prompt, axis=0)
    n_needed = jnp.sum(needed.astype(jnp.int32))
    (block_list,) = jnp.nonzero(needed, size=n_blocks, fill_value=0)
    block_list = block_list.astype(jnp.int32)

    row_segs = segment_ids
    row_shared = shared_req
    scale_factor = HEAD_SIZE ** (-0.5)
    head_shape = (local_rows, kv_heads, group)

    def key_block(i, loop_state):
        old_top, old_totals, old_summed = loop_state
        block = block_list[i]
        offset = block * KEY_BLOCK
        kv_part = lax.dynamic_slice_in_dim(kv_all, offset, KEY_BLOCK, 0)
        keys_part = kv_part[:, :kv_cols].reshape(KEY_BLOCK, kv_heads, HEAD_SIZE)
        values_part = kv_part[:, kv_cols:].reshape(KEY_BLOCK, kv_heads, HEAD_SIZE)
        mask_part = lax.dynamic_slice_in_dim(all_mask, offset, KEY_BLOCK, 0)
        columns = offset + jnp.arange(KEY_BLOCK, dtype=jnp.int32)
        col_segs = jnp.sum((columns[:, None] >= ends[None, :]).astype(jnp.int32), axis=1)
        live = mask_part == 1
        own = col_segs[None, :] == row_segs[:, None]
        other = col_segs[None, :] == row_shared[:, None]
        earlier = columns[None, :] <= token_ids[:, None]
        diagonal = columns[None, :] == token_ids[:, None]
        visible = diagonal | (earlier & live[None, :] & (own | other))
        allowed = visible[:, None, None, :]
        scores = (
            jnp.einsum("qhgd,khd->qhgk", q_rot, keys_part, preferred_element_type=jnp.float32)
            * scale_factor
        )
        scores = jnp.where(allowed, scores, masked_score)
        new_top = jnp.maximum(old_top, jnp.max(scores, axis=-1))
        factor = jnp.exp(old_top - new_top)
        raw_weights = jnp.where(allowed, jnp.exp(scores - new_top[..., None]), 0.0)
        new_totals = old_totals * factor + jnp.sum(raw_weights, axis=-1)
        new_summed = old_summed * factor[..., None] + jnp.einsum(
            "qhgk,khd->qhgd",
            raw_weights.astype(jnp.bfloat16),
            values_part,
            preferred_element_type=jnp.float32,
        )
        return (new_top, new_totals, new_summed)

    start_state = (
        jnp.full(head_shape, masked_score, jnp.float32),
        jnp.zeros(head_shape, jnp.float32),
        jnp.zeros(head_shape + (HEAD_SIZE,), jnp.float32),
    )
    top_now, totals, summed = lax.fori_loop(0, n_needed, key_block, start_state)

    my_request = jnp.sum(jnp.where(cache_slot == device_seq, requests, 0))
    my_start = jnp.sum(jnp.where(requests == my_request, starts, 0))
    my_length = jnp.sum(jnp.where(requests == my_request, prompt_lengths, 0))
    offsets = jnp.arange(LMAX, dtype=jnp.int32)
    wanted = my_start + offsets
    in_window = ((wanted < stream) & (offsets < my_length))[:, None]
    source = jnp.clip(wanted, 0, stream - 1)
    cache_rows = jnp.where(in_window, jnp.take(kv_all, source, axis=0), jnp.zeros((), jnp.bfloat16))
    cache_k = cache_rows[:, :kv_cols]
    cache_v = cache_rows[:, kv_cols:]

    attended = (summed / totals[..., None]).reshape(local_rows, query_heads * HEAD_SIZE)
    gated_heads = (attended * jax.nn.sigmoid(gate_logits)).astype(jnp.bfloat16)
    partial_out = lax.dot_general(
        gated_heads,
        w_out_t,
        (((1,), (1,)), ((), ())),
        preferred_element_type=jnp.float32,
    )
    branch_sum = lax.psum_scatter(
        partial_out.astype(jnp.bfloat16), "mdl", scatter_dimension=1, tiled=True
    ).astype(jnp.float32)
    layer_out = (wide_tokens + branch_sum).astype(jnp.bfloat16)
    return (layer_out, cache_k[None], cache_v[None])


def solution(mesh):
    seq = SEQ_PARTS
    split = Mesh(mesh.devices.reshape(8, 4, 2, mesh.shape["mdl"]), SEQ_PARTS + ("mdl",))
    placed = (
        P(seq, "mdl"),
        P("mdl"),
        P(seq, "mdl"),
        P(seq, "mdl"),
        P(seq, "mdl"),
        P(seq, "mdl"),
        P(),
        P(),
        P("mdl", seq),
        P(),
        P(seq),
        P(),
        P(seq),
        P(),
    )
    return jax.shard_map(
        body,
        mesh=split,
        in_specs=placed,
        out_specs=(P(seq, "mdl"), P(seq, None, "mdl"), P(seq, None, "mdl")),
        check_vma=False,
    )
```

```python
import jax
import jax.numpy as jnp
from jax import lax
from jax.sharding import Mesh
from jax.sharding import PartitionSpec as P

HEAD_SIZE = 128
LMAX = 512
KEY_BLOCK = 256


epsilon = 1e-06
rope_base = 1000000.0
masked_score = -1e30


def head_norm(values, gain_vector):
    return (
        values
        * lax.rsqrt(jnp.mean(values * values, axis=-1, keepdims=True) + epsilon)
        * gain_vector
    )


def rotate(values, position):
    half_width = values.shape[-1] // 2
    frequency = rope_base ** (-2.0 * jnp.arange(half_width, dtype=jnp.float32) / values.shape[-1])
    angles = position.astype(jnp.float32)[:, None] * frequency[None, :]
    cosine = jnp.cos(angles)[:, None, :]
    sine_part = jnp.sin(angles)[:, None, :]
    former = values[..., :half_width]
    latter = values[..., half_width:]
    return jnp.concatenate(
        [former * cosine - latter * sine_part, latter * cosine + former * sine_part], axis=-1
    )


SEQ_PARTS = ("z", "y", "xh")


def gather_seq(x):
    for name in reversed(SEQ_PARTS):
        x = lax.all_gather(x, name, axis=0, tiled=True)
    return x


def gather_z_xh(x):
    x = lax.all_gather(x, "z", axis=0, tiled=True)
    return lax.all_gather(x, "xh", axis=0, tiled=True)


def ring_y(x):
    ny = 4
    right = [(i, (i + 1) % ny) for i in range(ny)]
    left = [(i, (i - 1) % ny) for i in range(ny)]
    from_minus = lax.ppermute(x, "y", right)
    from_plus = lax.ppermute(x, "y", left)
    half = x.shape[0] // 2
    opp_a = lax.ppermute(from_minus[:half], "y", right)
    opp_b = lax.ppermute(from_plus[half:], "y", left)
    opposite = jnp.concatenate([opp_a, opp_b], axis=0)
    return jnp.stack([x, from_plus, opposite, from_minus])


def body(
    tokens,
    norm_gain,
    w_query,
    key_matrix,
    value_matrix,
    w_gate,
    q_gain,
    k_gain,
    w_out,
    prompt_lengths,
    segment_ids,
    tenant_ranges,
    key_mask,
    cache_slot,
):
    local_rows = tokens.shape[0]
    weight_rows = w_query.shape[0]
    q_cols = w_query.shape[1]
    kv_cols = key_matrix.shape[1]
    g_cols = w_gate.shape[1]
    seq_size = lax.axis_size(SEQ_PARTS)
    stream = local_rows * seq_size
    request_count = prompt_lengths.shape[0]

    mask_cols = local_rows // weight_rows
    mask_block = key_mask.astype(jnp.bfloat16).reshape(weight_rows, mask_cols)
    mask_block = jnp.pad(mask_block, ((0, 0), (0, 128 - mask_cols)))
    gate_part = gather_z_xh(w_gate)
    packed = jnp.concatenate([w_query, key_matrix, value_matrix, w_out.T, mask_block], axis=1)
    packed, gate_part = lax.optimization_barrier((packed, gate_part))
    gate_ring = ring_y(gate_part)
    gathered = gather_seq(packed)
    proj_cols = q_cols + 2 * kv_cols
    w_proj = gathered[:, :proj_cols]
    w_out_t = gathered[:, proj_cols : proj_cols + w_out.shape[0]]
    all_mask = gathered[:, proj_cols + w_out.shape[0] : proj_cols + w_out.shape[0] + mask_cols]
    all_mask = all_mask.reshape(stream)
    w_gate_perm = gate_ring.reshape(-1, g_cols)

    wide_tokens = tokens.astype(jnp.float32)
    full_width = tokens.shape[1] * lax.axis_size("mdl")
    square_total = lax.psum(jnp.sum(wide_tokens * wide_tokens, axis=1), "mdl")
    scaled = (
        wide_tokens
        * lax.rsqrt(square_total / full_width + epsilon)[:, None]
        * norm_gain.astype(jnp.float32)
    )
    normalized_input = lax.all_gather(scaled.astype(jnp.bfloat16), "mdl", axis=1, tiled=True)
    projected = jnp.dot(normalized_input, w_proj, preferred_element_type=jnp.float32)
    query_rows = projected[:, :q_cols]
    unprojected_keys = projected[:, q_cols : q_cols + kv_cols]
    values_raw = projected[:, q_cols + kv_cols : q_cols + 2 * kv_cols]
    my_y = lax.axis_index("y")
    input_perm = normalized_input.reshape(local_rows, 8, 4, 2, weight_rows)
    input_perm = jnp.roll(input_perm, -my_y, axis=2)
    input_perm = input_perm.transpose(0, 2, 3, 1, 4).reshape(local_rows, -1)
    gate_logits = jnp.dot(input_perm, w_gate_perm, preferred_element_type=jnp.float32)

    device_seq = lax.axis_index(SEQ_PARTS)
    token_ids = device_seq * local_rows + jnp.arange(local_rows, dtype=jnp.int32)
    starts = jnp.cumsum(prompt_lengths) - prompt_lengths
    ends = starts + prompt_lengths
    requests = jnp.arange(request_count, dtype=jnp.int32)
    member = (requests[:, None] > tenant_ranges[None, :, 0]) & (
        requests[:, None] < tenant_ranges[None, :, 1]
    )
    shared_of = jnp.sum(jnp.where(member, tenant_ranges[None, :, 0] + 3, 0), axis=1) - 3
    onehot = segment_ids[:, None] == requests[None, :]
    seg_start = jnp.sum(jnp.where(onehot, starts[None, :], 0), axis=1)
    shared_req = jnp.sum(jnp.where(onehot, shared_of[None, :], 0), axis=1)
    position = token_ids - seg_start

    query_heads = q_cols // HEAD_SIZE
    kv_heads = kv_cols // HEAD_SIZE
    group = query_heads // kv_heads
    q_rot = (
        rotate(head_norm(query_rows.reshape(local_rows, query_heads, HEAD_SIZE), q_gain), position)
        .astype(jnp.bfloat16)
        .reshape(local_rows, kv_heads, group, HEAD_SIZE)
    )
    k_rot = (
        rotate(head_norm(unprojected_keys.reshape(local_rows, kv_heads, HEAD_SIZE), k_gain), position)
        .astype(jnp.bfloat16)
        .reshape(local_rows, kv_cols)
    )
    values_flat = values_raw.astype(jnp.bfloat16)
    v_part = gather_z_xh(values_flat)
    k_rot, v_part = lax.optimization_barrier((k_rot, v_part))
    v_ring = ring_y(v_part)
    k_all = gather_seq(k_rot)
    v_ring = v_ring.reshape(-1, kv_cols)

    def v_row_of(token):
        block = token // local_rows
        rel = (block // 2 % 4 - my_y) % 4
        place = (block % 2) * 8 + block // 8
        return (rel * 16 + place) * local_rows + token % local_rows

    n_blocks = stream // KEY_BLOCK
    block_ids = jnp.arange(n_blocks, dtype=jnp.int32)
    last_block = (device_seq * local_rows + local_rows - 1) // KEY_BLOCK
    first_block = jnp.min(seg_start) // KEY_BLOCK
    needed = (block_ids >= first_block) & (block_ids <= last_block)
    lo = tenant_ranges[:, 0]
    hi = tenant_ranges[:, 1]
    used = jnp.any(
        (segment_ids[:, None] > lo[None, :]) & (segment_ids[:, None] < hi[None, :]), axis=0
    )
    lo_start = jnp.sum(jnp.where(requests[None, :] == lo[:, None], starts[None, :], 0), axis=1)
    lo_end = jnp.sum(jnp.where(requests[None, :] == lo[:, None], ends[None, :], 0), axis=1)
    in_prompt = (
        used[:, None]
        & (block_ids[None, :] >= (lo_start // KEY_BLOCK)[:, None])
        & (block_ids[None, :] <= ((lo_end - 1) // KEY_BLOCK)[:, None])
    )
    needed = needed | jnp.any(in_prompt, axis=0)
    n_needed = jnp.sum(needed.astype(jnp.int32))
    (block_list,) = jnp.nonzero(needed, size=n_blocks, fill_value=0)
    block_list = block_list.astype(jnp.int32)

    row_segs = segment_ids
    row_shared = shared_req
    scale_factor = HEAD_SIZE ** (-0.5)
    head_shape = (local_rows, kv_heads, group)

    def key_block(i, loop_state):
        old_top, old_totals, old_summed = loop_state
        block = block_list[i]
        offset = block * KEY_BLOCK
        keys_part = lax.dynamic_slice_in_dim(k_all, offset, KEY_BLOCK, 0).reshape(
            KEY_BLOCK, kv_heads, HEAD_SIZE
        )
        values_part = lax.dynamic_slice_in_dim(v_ring, v_row_of(offset), KEY_BLOCK, 0).reshape(
            KEY_BLOCK, kv_heads, HEAD_SIZE
        )
        mask_part = lax.dynamic_slice_in_dim(all_mask, offset, KEY_BLOCK, 0)
        columns = offset + jnp.arange(KEY_BLOCK, dtype=jnp.int32)
        col_segs = jnp.sum((columns[:, None] >= ends[None, :]).astype(jnp.int32), axis=1)
        live = mask_part == 1
        own = col_segs[None, :] == row_segs[:, None]
        other = col_segs[None, :] == row_shared[:, None]
        earlier = columns[None, :] <= token_ids[:, None]
        diagonal = columns[None, :] == token_ids[:, None]
        visible = diagonal | (earlier & live[None, :] & (own | other))
        allowed = visible[:, None, None, :]
        scores = (
            jnp.einsum("qhgd,khd->qhgk", q_rot, keys_part, preferred_element_type=jnp.float32)
            * scale_factor
        )
        scores = jnp.where(allowed, scores, masked_score)
        new_top = jnp.maximum(old_top, jnp.max(scores, axis=-1))
        factor = jnp.exp(old_top - new_top)
        raw_weights = jnp.where(allowed, jnp.exp(scores - new_top[..., None]), 0.0)
        new_totals = old_totals * factor + jnp.sum(raw_weights, axis=-1)
        new_summed = old_summed * factor[..., None] + jnp.einsum(
            "qhgk,khd->qhgd",
            raw_weights.astype(jnp.bfloat16),
            values_part,
            preferred_element_type=jnp.float32,
        )
        return (new_top, new_totals, new_summed)

    start_state = (
        jnp.full(head_shape, masked_score, jnp.float32),
        jnp.zeros(head_shape, jnp.float32),
        jnp.zeros(head_shape + (HEAD_SIZE,), jnp.float32),
    )
    top_now, totals, summed = lax.fori_loop(0, n_needed, key_block, start_state)

    my_request = jnp.sum(jnp.where(cache_slot == device_seq, requests, 0))
    my_start = jnp.sum(jnp.where(requests == my_request, starts, 0))
    my_length = jnp.sum(jnp.where(requests == my_request, prompt_lengths, 0))
    offsets = jnp.arange(LMAX, dtype=jnp.int32)
    wanted = my_start + offsets
    in_window = ((wanted < stream) & (offsets < my_length))[:, None]
    source = jnp.clip(wanted, 0, stream - 1)
    zero = jnp.zeros((), jnp.bfloat16)
    cache_k = jnp.where(in_window, jnp.take(k_all, source, axis=0), zero)
    cache_v = jnp.where(in_window, jnp.take(v_ring, v_row_of(source), axis=0), zero)

    attended = (summed / totals[..., None]).reshape(local_rows, query_heads * HEAD_SIZE)
    gated_heads = (attended * jax.nn.sigmoid(gate_logits)).astype(jnp.bfloat16)
    partial_out = lax.dot_general(
        gated_heads,
        w_out_t,
        (((1,), (1,)), ((), ())),
        preferred_element_type=jnp.float32,
    )
    branch_sum = lax.psum_scatter(
        partial_out.astype(jnp.bfloat16), "mdl", scatter_dimension=1, tiled=True
    ).astype(jnp.float32)
    layer_out = (wide_tokens + branch_sum).astype(jnp.bfloat16)
    return (layer_out, cache_k[None], cache_v[None])


def solution(mesh):
    seq = SEQ_PARTS
    split = Mesh(mesh.devices.reshape(8, 4, 2, mesh.shape["mdl"]), SEQ_PARTS + ("mdl",))
    placed = (
        P(seq, "mdl"),
        P("mdl"),
        P(seq, "mdl"),
        P(seq, "mdl"),
        P(seq, "mdl"),
        P(seq, "mdl"),
        P(),
        P(),
        P("mdl", seq),
        P(),
        P(seq),
        P(),
        P(seq),
        P(),
    )
    return jax.shard_map(
        body,
        mesh=split,
        in_specs=placed,
        out_specs=(P(seq, "mdl"), P(seq, None, "mdl"), P(seq, None, "mdl")),
        check_vma=False,
    )
```

```python
import jax
import jax.numpy as jnp
from jax import lax
from jax.sharding import Mesh
from jax.sharding import PartitionSpec as P

HEAD_SIZE = 128
LMAX = 512
KEY_BLOCK = 256


epsilon = 1e-06
rope_base = 1000000.0
masked_score = -1e30


def head_norm(values, gain_vector):
    return (
        values
        * lax.rsqrt(jnp.mean(values * values, axis=-1, keepdims=True) + epsilon)
        * gain_vector
    )


def rotate(values, position):
    half_width = values.shape[-1] // 2
    frequency = rope_base ** (-2.0 * jnp.arange(half_width, dtype=jnp.float32) / values.shape[-1])
    angles = position.astype(jnp.float32)[:, None] * frequency[None, :]
    cosine = jnp.cos(angles)[:, None, :]
    sine_part = jnp.sin(angles)[:, None, :]
    former = values[..., :half_width]
    latter = values[..., half_width:]
    return jnp.concatenate(
        [former * cosine - latter * sine_part, latter * cosine + former * sine_part], axis=-1
    )


SEQ_PARTS = ("z", "y", "xh")


def gather_seq(x):
    for name in reversed(SEQ_PARTS):
        x = lax.all_gather(x, name, axis=0, tiled=True)
    return x


def gather_xh_z(x):
    x = lax.all_gather(x, "xh", axis=0, tiled=True)
    return lax.all_gather(x, "z", axis=0, tiled=True)


def ring_y(x):
    ny = 4
    right = [(i, (i + 1) % ny) for i in range(ny)]
    left = [(i, (i - 1) % ny) for i in range(ny)]
    from_minus = lax.ppermute(x, "y", right)
    from_plus = lax.ppermute(x, "y", left)
    half = x.shape[0] // 2
    opp_a = lax.ppermute(from_minus[:half], "y", right)
    opp_b = lax.ppermute(from_plus[half:], "y", left)
    opposite = jnp.concatenate([opp_a, opp_b], axis=0)
    return jnp.stack([x, from_plus, opposite, from_minus])


def body(
    tokens,
    norm_gain,
    w_query,
    key_matrix,
    value_matrix,
    w_gate,
    q_gain,
    k_gain,
    w_out,
    prompt_lengths,
    segment_ids,
    tenant_ranges,
    key_mask,
    cache_slot,
):
    local_rows = tokens.shape[0]
    weight_rows = w_query.shape[0]
    q_cols = w_query.shape[1]
    kv_cols = key_matrix.shape[1]
    g_cols = w_gate.shape[1]
    seq_size = lax.axis_size(SEQ_PARTS)
    stream = local_rows * seq_size
    request_count = prompt_lengths.shape[0]

    mask_cols = local_rows // weight_rows
    mask_block = key_mask.astype(jnp.bfloat16).reshape(weight_rows, mask_cols)
    mask_block = jnp.pad(mask_block, ((0, 0), (0, 128 - mask_cols)))
    packed = jnp.concatenate([w_query, key_matrix, value_matrix, w_out.T, mask_block], axis=1)
    packed = lax.all_gather(packed, "xh", axis=0, tiled=True)
    packed = lax.all_gather(packed, "y", axis=0, tiled=True)
    packed, gate_in = lax.optimization_barrier((packed, w_gate))
    gate_ring = ring_y(gather_xh_z(gate_in))
    gathered = lax.all_gather(packed, "z", axis=0, tiled=True)
    proj_cols = q_cols + 2 * kv_cols
    w_proj = gathered[:, :proj_cols]
    w_out_t = gathered[:, proj_cols : proj_cols + w_out.shape[0]]
    all_mask = gathered[:, proj_cols + w_out.shape[0] : proj_cols + w_out.shape[0] + mask_cols]
    all_mask = all_mask.reshape(stream)
    w_gate_perm = gate_ring.reshape(-1, g_cols)

    wide_tokens = tokens.astype(jnp.float32)
    full_width = tokens.shape[1] * lax.axis_size("mdl")
    square_total = lax.psum(jnp.sum(wide_tokens * wide_tokens, axis=1), "mdl")
    scaled = (
        wide_tokens
        * lax.rsqrt(square_total / full_width + epsilon)[:, None]
        * norm_gain.astype(jnp.float32)
    )
    normalized_input = lax.all_gather(scaled.astype(jnp.bfloat16), "mdl", axis=1, tiled=True)
    projected = jnp.dot(normalized_input, w_proj, preferred_element_type=jnp.float32)
    query_rows = projected[:, :q_cols]
    unprojected_keys = projected[:, q_cols : q_cols + kv_cols]
    values_raw = projected[:, q_cols + kv_cols : q_cols + 2 * kv_cols]
    my_y = lax.axis_index("y")
    input_perm = normalized_input.reshape(local_rows, 8, 4, 2, weight_rows)
    input_perm = jnp.roll(input_perm, -my_y, axis=2)
    input_perm = input_perm.transpose(0, 2, 1, 3, 4).reshape(local_rows, -1)
    gate_logits = jnp.dot(input_perm, w_gate_perm, preferred_element_type=jnp.float32)

    device_seq = lax.axis_index(SEQ_PARTS)
    token_ids = device_seq * local_rows + jnp.arange(local_rows, dtype=jnp.int32)
    starts = jnp.cumsum(prompt_lengths) - prompt_lengths
    ends = starts + prompt_lengths
    requests = jnp.arange(request_count, dtype=jnp.int32)
    member = (requests[:, None] > tenant_ranges[None, :, 0]) & (
        requests[:, None] < tenant_ranges[None, :, 1]
    )
    shared_of = jnp.sum(jnp.where(member, tenant_ranges[None, :, 0] + 3, 0), axis=1) - 3
    onehot = segment_ids[:, None] == requests[None, :]
    seg_start = jnp.sum(jnp.where(onehot, starts[None, :], 0), axis=1)
    shared_req = jnp.sum(jnp.where(onehot, shared_of[None, :], 0), axis=1)
    position = token_ids - seg_start

    query_heads = q_cols // HEAD_SIZE
    kv_heads = kv_cols // HEAD_SIZE
    group = query_heads // kv_heads
    q_rot = (
        rotate(head_norm(query_rows.reshape(local_rows, query_heads, HEAD_SIZE), q_gain), position)
        .astype(jnp.bfloat16)
        .reshape(local_rows, kv_heads, group, HEAD_SIZE)
    )
    k_rot = (
        rotate(head_norm(unprojected_keys.reshape(local_rows, kv_heads, HEAD_SIZE), k_gain), position)
        .astype(jnp.bfloat16)
        .reshape(local_rows, kv_cols)
    )
    values_flat = values_raw.astype(jnp.bfloat16)
    v_part = gather_xh_z(values_flat)
    k_rot, v_part = lax.optimization_barrier((k_rot, v_part))
    v_ring = ring_y(v_part)
    k_all = gather_seq(k_rot)
    v_ring = v_ring.reshape(-1, kv_cols)

    def v_row_of(token):
        block = token // local_rows
        rel = (block // 2 % 4 - my_y) % 4
        place = (block // 8) * 2 + block % 2
        return (rel * 16 + place) * local_rows + token % local_rows

    n_blocks = stream // KEY_BLOCK
    block_ids = jnp.arange(n_blocks, dtype=jnp.int32)
    last_block = (device_seq * local_rows + local_rows - 1) // KEY_BLOCK
    first_block = jnp.min(seg_start) // KEY_BLOCK
    needed = (block_ids >= first_block) & (block_ids <= last_block)
    lo = tenant_ranges[:, 0]
    hi = tenant_ranges[:, 1]
    used = jnp.any(
        (segment_ids[:, None] > lo[None, :]) & (segment_ids[:, None] < hi[None, :]), axis=0
    )
    lo_start = jnp.sum(jnp.where(requests[None, :] == lo[:, None], starts[None, :], 0), axis=1)
    lo_end = jnp.sum(jnp.where(requests[None, :] == lo[:, None], ends[None, :], 0), axis=1)
    in_prompt = (
        used[:, None]
        & (block_ids[None, :] >= (lo_start // KEY_BLOCK)[:, None])
        & (block_ids[None, :] <= ((lo_end - 1) // KEY_BLOCK)[:, None])
    )
    needed = needed | jnp.any(in_prompt, axis=0)
    n_needed = jnp.sum(needed.astype(jnp.int32))
    (block_list,) = jnp.nonzero(needed, size=n_blocks, fill_value=0)
    block_list = block_list.astype(jnp.int32)

    row_segs = segment_ids
    row_shared = shared_req
    scale_factor = HEAD_SIZE ** (-0.5)
    head_shape = (local_rows, kv_heads, group)

    def key_block(i, loop_state):
        old_top, old_totals, old_summed = loop_state
        block = block_list[i]
        offset = block * KEY_BLOCK
        keys_part = lax.dynamic_slice_in_dim(k_all, offset, KEY_BLOCK, 0).reshape(
            KEY_BLOCK, kv_heads, HEAD_SIZE
        )
        values_part = lax.dynamic_slice_in_dim(v_ring, v_row_of(offset), KEY_BLOCK, 0).reshape(
            KEY_BLOCK, kv_heads, HEAD_SIZE
        )
        mask_part = lax.dynamic_slice_in_dim(all_mask, offset, KEY_BLOCK, 0)
        columns = offset + jnp.arange(KEY_BLOCK, dtype=jnp.int32)
        col_segs = jnp.sum((columns[:, None] >= ends[None, :]).astype(jnp.int32), axis=1)
        live = mask_part == 1
        own = col_segs[None, :] == row_segs[:, None]
        other = col_segs[None, :] == row_shared[:, None]
        earlier = columns[None, :] <= token_ids[:, None]
        diagonal = columns[None, :] == token_ids[:, None]
        visible = diagonal | (earlier & live[None, :] & (own | other))
        allowed = visible[:, None, None, :]
        scores = (
            jnp.einsum("qhgd,khd->qhgk", q_rot, keys_part, preferred_element_type=jnp.float32)
            * scale_factor
        )
        scores = jnp.where(allowed, scores, masked_score)
        new_top = jnp.maximum(old_top, jnp.max(scores, axis=-1))
        factor = jnp.exp(old_top - new_top)
        raw_weights = jnp.where(allowed, jnp.exp(scores - new_top[..., None]), 0.0)
        new_totals = old_totals * factor + jnp.sum(raw_weights, axis=-1)
        new_summed = old_summed * factor[..., None] + jnp.einsum(
            "qhgk,khd->qhgd",
            raw_weights.astype(jnp.bfloat16),
            values_part,
            preferred_element_type=jnp.float32,
        )
        return (new_top, new_totals, new_summed)

    start_state = (
        jnp.full(head_shape, masked_score, jnp.float32),
        jnp.zeros(head_shape, jnp.float32),
        jnp.zeros(head_shape + (HEAD_SIZE,), jnp.float32),
    )
    top_now, totals, summed = lax.fori_loop(0, n_needed, key_block, start_state)

    my_request = jnp.sum(jnp.where(cache_slot == device_seq, requests, 0))
    my_start = jnp.sum(jnp.where(requests == my_request, starts, 0))
    my_length = jnp.sum(jnp.where(requests == my_request, prompt_lengths, 0))
    offsets = jnp.arange(LMAX, dtype=jnp.int32)
    wanted = my_start + offsets
    in_window = ((wanted < stream) & (offsets < my_length))[:, None]
    source = jnp.clip(wanted, 0, stream - 1)
    zero = jnp.zeros((), jnp.bfloat16)
    cache_k = jnp.where(in_window, jnp.take(k_all, source, axis=0), zero)
    cache_v = jnp.where(in_window, jnp.take(v_ring, v_row_of(source), axis=0), zero)

    attended = (summed / totals[..., None]).reshape(local_rows, query_heads * HEAD_SIZE)
    gated_heads = (attended * jax.nn.sigmoid(gate_logits)).astype(jnp.bfloat16)
    partial_out = lax.dot_general(
        gated_heads,
        w_out_t,
        (((1,), (1,)), ((), ())),
        preferred_element_type=jnp.float32,
    )
    mdl_index = lax.axis_index("mdl")
    n_mdl = lax.axis_size("mdl")
    x_lo = mdl_index // 2
    core = mdl_index % 2
    half = partial_out.shape[1] // 2
    quarter = half // 2
    mine = lax.dynamic_slice_in_dim(partial_out, x_lo * half, half, 1)
    theirs = lax.dynamic_slice_in_dim(partial_out, (1 - x_lo) * half, half, 1)
    across = lax.ppermute(
        theirs.astype(jnp.bfloat16), "mdl", [(m, m ^ 2) for m in range(n_mdl)]
    )
    half_sum = mine + across.astype(jnp.float32)
    mine = lax.dynamic_slice_in_dim(half_sum, core * quarter, quarter, 1)
    theirs = lax.dynamic_slice_in_dim(half_sum, (1 - core) * quarter, quarter, 1)
    branch_sum = mine + lax.ppermute(theirs, "mdl", [(m, m ^ 1) for m in range(n_mdl)])
    layer_out = (wide_tokens + branch_sum).astype(jnp.bfloat16)
    return (layer_out, cache_k[None], cache_v[None])


def solution(mesh):
    seq = SEQ_PARTS
    split = Mesh(mesh.devices.reshape(8, 4, 2, mesh.shape["mdl"]), SEQ_PARTS + ("mdl",))
    placed = (
        P(seq, "mdl"),
        P("mdl"),
        P(seq, "mdl"),
        P(seq, "mdl"),
        P(seq, "mdl"),
        P(seq, "mdl"),
        P(),
        P(),
        P("mdl", seq),
        P(),
        P(seq),
        P(),
        P(seq),
        P(),
    )
    return jax.shard_map(
        body,
        mesh=split,
        in_specs=placed,
        out_specs=(P(seq, "mdl"), P(seq, None, "mdl"), P(seq, None, "mdl")),
        check_vma=False,
    )
```

```python
import jax
import jax.numpy as jnp
from jax import lax
from jax.experimental import pallas as pl
from jax.experimental.pallas import tpu as pltpu
from jax.sharding import Mesh
from jax.sharding import PartitionSpec as P

HEAD_SIZE = 128
LMAX = 512
KEY_BLOCK = 256


epsilon = 1e-06
rope_base = 1000000.0
masked_score = -1e30


def head_norm(values, gain_vector):
    return (
        values
        * lax.rsqrt(jnp.mean(values * values, axis=-1, keepdims=True) + epsilon)
        * gain_vector
    )


def rotate(values, position):
    half_width = values.shape[-1] // 2
    frequency = rope_base ** (-2.0 * jnp.arange(half_width, dtype=jnp.float32) / values.shape[-1])
    angles = position.astype(jnp.float32)[:, None] * frequency[None, :]
    cosine = jnp.cos(angles)[:, None, :]
    sine_part = jnp.sin(angles)[:, None, :]
    former = values[..., :half_width]
    latter = values[..., half_width:]
    return jnp.concatenate(
        [former * cosine - latter * sine_part, latter * cosine + former * sine_part], axis=-1
    )


SEQ_PARTS = ("z", "y", "xh")
MESH_ID = pl.DeviceIdType.MESH
AXES = SEQ_PARTS + ("mdl",)


def _ring_kernel(x_ref, out_ref, send_sem, recv_sem, local_sem):
    ny = 4
    me = {name: lax.axis_index(name) for name in AXES}
    my_y = me["y"]

    def dev(yy):
        return tuple(yy if name == "y" else me[name] for name in AXES)

    plus = dev(lax.rem(my_y + 1, ny))
    minus = dev(lax.rem(my_y + ny - 1, ny))
    barrier = pltpu.get_barrier_semaphore()
    for d in (plus, minus):
        pl.semaphore_signal(barrier, inc=1, device_id=d, device_id_type=MESH_ID)
    pl.semaphore_wait(barrier, 2)

    rows = x_ref.shape[0]
    half = rows // 2
    to_minus = pltpu.make_async_remote_copy(
        src_ref=x_ref, dst_ref=out_ref.at[1], send_sem=send_sem.at[0], recv_sem=recv_sem.at[0],
        device_id=minus, device_id_type=MESH_ID)
    to_plus = pltpu.make_async_remote_copy(
        src_ref=x_ref, dst_ref=out_ref.at[3], send_sem=send_sem.at[1], recv_sem=recv_sem.at[1],
        device_id=plus, device_id_type=MESH_ID)
    own = pltpu.make_async_copy(x_ref, out_ref.at[0], local_sem.at[0])
    to_minus.start()
    to_plus.start()
    own.start()
    to_minus.wait_recv()
    on_minus = pltpu.make_async_remote_copy(
        src_ref=out_ref.at[1, pl.ds(0, half)], dst_ref=out_ref.at[2, pl.ds(0, half)],
        send_sem=send_sem.at[2], recv_sem=recv_sem.at[2], device_id=minus, device_id_type=MESH_ID)
    on_minus.start()
    to_plus.wait_recv()
    on_plus = pltpu.make_async_remote_copy(
        src_ref=out_ref.at[3, pl.ds(half, rows - half)], dst_ref=out_ref.at[2, pl.ds(half, rows - half)],
        send_sem=send_sem.at[3], recv_sem=recv_sem.at[3], device_id=plus, device_id_type=MESH_ID)
    on_plus.start()
    to_minus.wait_send()
    to_plus.wait_send()
    own.wait()
    on_minus.wait_send()
    on_plus.wait_send()
    on_minus.wait_recv()
    on_plus.wait_recv()


def ring_y_kernel(x, collective_id):
    rows, width = x.shape
    return pl.pallas_call(
        _ring_kernel,
        out_shape=jax.ShapeDtypeStruct((4, rows, width), x.dtype),
        in_specs=[pl.BlockSpec(memory_space=pl.ANY)],
        out_specs=pl.BlockSpec(memory_space=pl.ANY),
        scratch_shapes=[
            pltpu.SemaphoreType.DMA((4,)),
            pltpu.SemaphoreType.DMA((4,)),
            pltpu.SemaphoreType.DMA((1,)),
        ],
        compiler_params=pltpu.CompilerParams(collective_id=collective_id, has_side_effects=True),
    )(x)


def gather_seq(x):
    for name in reversed(SEQ_PARTS):
        x = lax.all_gather(x, name, axis=0, tiled=True)
    return x


def gather_xh_z(x):
    x = lax.all_gather(x, "xh", axis=0, tiled=True)
    return lax.all_gather(x, "z", axis=0, tiled=True)


def ring_y(x):
    ny = 4
    right = [(i, (i + 1) % ny) for i in range(ny)]
    left = [(i, (i - 1) % ny) for i in range(ny)]
    from_minus = lax.ppermute(x, "y", right)
    from_plus = lax.ppermute(x, "y", left)
    half = x.shape[0] // 2
    opp_a = lax.ppermute(from_minus[:half], "y", right)
    opp_b = lax.ppermute(from_plus[half:], "y", left)
    opposite = jnp.concatenate([opp_a, opp_b], axis=0)
    return jnp.stack([x, from_plus, opposite, from_minus])


def body(
    tokens,
    norm_gain,
    w_query,
    key_matrix,
    value_matrix,
    w_gate,
    q_gain,
    k_gain,
    w_out,
    prompt_lengths,
    segment_ids,
    tenant_ranges,
    key_mask,
    cache_slot,
):
    local_rows = tokens.shape[0]
    weight_rows = w_query.shape[0]
    q_cols = w_query.shape[1]
    kv_cols = key_matrix.shape[1]
    g_cols = w_gate.shape[1]
    seq_size = lax.axis_size(SEQ_PARTS)
    stream = local_rows * seq_size
    request_count = prompt_lengths.shape[0]

    mask_cols = local_rows // weight_rows
    mask_block = key_mask.astype(jnp.bfloat16).reshape(weight_rows, mask_cols)
    mask_block = jnp.pad(mask_block, ((0, 0), (0, 128 - mask_cols)))
    packed = jnp.concatenate([w_query, key_matrix, value_matrix, w_out.T, mask_block], axis=1)
    packed = lax.all_gather(packed, "xh", axis=0, tiled=True)
    packed = lax.all_gather(packed, "y", axis=0, tiled=True)
    packed, gate_in = lax.optimization_barrier((packed, w_gate))
    gate_ring = ring_y_kernel(gather_xh_z(gate_in), 1)
    gathered = lax.all_gather(packed, "z", axis=0, tiled=True)
    proj_cols = q_cols + 2 * kv_cols
    w_proj = gathered[:, :proj_cols]
    w_out_t = gathered[:, proj_cols : proj_cols + w_out.shape[0]]
    all_mask = gathered[:, proj_cols + w_out.shape[0] : proj_cols + w_out.shape[0] + mask_cols]
    all_mask = all_mask.reshape(stream)
    w_gate_perm = gate_ring.reshape(-1, g_cols)

    wide_tokens = tokens.astype(jnp.float32)
    full_width = tokens.shape[1] * lax.axis_size("mdl")
    square_total = lax.psum(jnp.sum(wide_tokens * wide_tokens, axis=1), "mdl")
    scaled = (
        wide_tokens
        * lax.rsqrt(square_total / full_width + epsilon)[:, None]
        * norm_gain.astype(jnp.float32)
    )
    normalized_input = lax.all_gather(scaled.astype(jnp.bfloat16), "mdl", axis=1, tiled=True)
    projected = jnp.dot(normalized_input, w_proj, preferred_element_type=jnp.float32)
    query_rows = projected[:, :q_cols]
    unprojected_keys = projected[:, q_cols : q_cols + kv_cols]
    values_raw = projected[:, q_cols + kv_cols : q_cols + 2 * kv_cols]
    my_y = lax.axis_index("y")
    input_perm = normalized_input.reshape(local_rows, 8, 4, 2, weight_rows)
    input_perm = jnp.roll(input_perm, -my_y, axis=2)
    input_perm = input_perm.transpose(0, 2, 1, 3, 4).reshape(local_rows, -1)
    gate_logits = jnp.dot(input_perm, w_gate_perm, preferred_element_type=jnp.float32)

    device_seq = lax.axis_index(SEQ_PARTS)
    token_ids = device_seq * local_rows + jnp.arange(local_rows, dtype=jnp.int32)
    starts = jnp.cumsum(prompt_lengths) - prompt_lengths
    ends = starts + prompt_lengths
    requests = jnp.arange(request_count, dtype=jnp.int32)
    member = (requests[:, None] > tenant_ranges[None, :, 0]) & (
        requests[:, None] < tenant_ranges[None, :, 1]
    )
    shared_of = jnp.sum(jnp.where(member, tenant_ranges[None, :, 0] + 3, 0), axis=1) - 3
    onehot = segment_ids[:, None] == requests[None, :]
    seg_start = jnp.sum(jnp.where(onehot, starts[None, :], 0), axis=1)
    shared_req = jnp.sum(jnp.where(onehot, shared_of[None, :], 0), axis=1)
    position = token_ids - seg_start

    query_heads = q_cols // HEAD_SIZE
    kv_heads = kv_cols // HEAD_SIZE
    group = query_heads // kv_heads
    q_rot = (
        rotate(head_norm(query_rows.reshape(local_rows, query_heads, HEAD_SIZE), q_gain), position)
        .astype(jnp.bfloat16)
        .reshape(local_rows, kv_heads, group, HEAD_SIZE)
    )
    k_rot = (
        rotate(head_norm(unprojected_keys.reshape(local_rows, kv_heads, HEAD_SIZE), k_gain), position)
        .astype(jnp.bfloat16)
        .reshape(local_rows, kv_cols)
    )
    values_flat = values_raw.astype(jnp.bfloat16)
    kv_pair = lax.all_gather(jnp.concatenate([k_rot, values_flat], axis=1), "xh", axis=0, tiled=True)
    v_part = lax.all_gather(kv_pair[:, kv_cols:], "z", axis=0, tiled=True)
    k_part = ring_y_kernel(kv_pair[:, :kv_cols], 2).reshape(-1, kv_cols)
    k_part, v_part = lax.optimization_barrier((k_part, v_part))
    k_all = lax.all_gather(k_part, "z", axis=0, tiled=True)
    v_ring = ring_y_kernel(v_part, 3).reshape(-1, kv_cols)

    def k_row_of(token):
        block = token // local_rows
        rel = (block // 2 % 4 - my_y) % 4
        place = ((block // 8) * 4 + rel) * 2 + block % 2
        return place * local_rows + token % local_rows

    def v_row_of(token):
        block = token // local_rows
        rel = (block // 2 % 4 - my_y) % 4
        place = (block // 8) * 2 + block % 2
        return (rel * 16 + place) * local_rows + token % local_rows

    n_blocks = stream // KEY_BLOCK
    block_ids = jnp.arange(n_blocks, dtype=jnp.int32)
    last_block = (device_seq * local_rows + local_rows - 1) // KEY_BLOCK
    first_block = jnp.min(seg_start) // KEY_BLOCK
    needed = (block_ids >= first_block) & (block_ids <= last_block)
    lo = tenant_ranges[:, 0]
    hi = tenant_ranges[:, 1]
    used = jnp.any(
        (segment_ids[:, None] > lo[None, :]) & (segment_ids[:, None] < hi[None, :]), axis=0
    )
    lo_start = jnp.sum(jnp.where(requests[None, :] == lo[:, None], starts[None, :], 0), axis=1)
    lo_end = jnp.sum(jnp.where(requests[None, :] == lo[:, None], ends[None, :], 0), axis=1)
    in_prompt = (
        used[:, None]
        & (block_ids[None, :] >= (lo_start // KEY_BLOCK)[:, None])
        & (block_ids[None, :] <= ((lo_end - 1) // KEY_BLOCK)[:, None])
    )
    needed = needed | jnp.any(in_prompt, axis=0)
    n_needed = jnp.sum(needed.astype(jnp.int32))
    (block_list,) = jnp.nonzero(needed, size=n_blocks, fill_value=0)
    block_list = block_list.astype(jnp.int32)

    row_segs = segment_ids
    row_shared = shared_req
    scale_factor = HEAD_SIZE ** (-0.5)
    head_shape = (local_rows, kv_heads, group)

    def key_block(i, loop_state):
        old_top, old_totals, old_summed = loop_state
        block = block_list[i]
        offset = block * KEY_BLOCK
        keys_part = lax.dynamic_slice_in_dim(k_all, k_row_of(offset), KEY_BLOCK, 0).reshape(
            KEY_BLOCK, kv_heads, HEAD_SIZE
        )
        values_part = lax.dynamic_slice_in_dim(v_ring, v_row_of(offset), KEY_BLOCK, 0).reshape(
            KEY_BLOCK, kv_heads, HEAD_SIZE
        )
        mask_part = lax.dynamic_slice_in_dim(all_mask, offset, KEY_BLOCK, 0)
        columns = offset + jnp.arange(KEY_BLOCK, dtype=jnp.int32)
        col_segs = jnp.sum((columns[:, None] >= ends[None, :]).astype(jnp.int32), axis=1)
        live = mask_part == 1
        own = col_segs[None, :] == row_segs[:, None]
        other = col_segs[None, :] == row_shared[:, None]
        earlier = columns[None, :] <= token_ids[:, None]
        diagonal = columns[None, :] == token_ids[:, None]
        visible = diagonal | (earlier & live[None, :] & (own | other))
        allowed = visible[:, None, None, :]
        scores = (
            jnp.einsum("qhgd,khd->qhgk", q_rot, keys_part, preferred_element_type=jnp.float32)
            * scale_factor
        )
        scores = jnp.where(allowed, scores, masked_score)
        new_top = jnp.maximum(old_top, jnp.max(scores, axis=-1))
        factor = jnp.exp(old_top - new_top)
        raw_weights = jnp.where(allowed, jnp.exp(scores - new_top[..., None]), 0.0)
        new_totals = old_totals * factor + jnp.sum(raw_weights, axis=-1)
        new_summed = old_summed * factor[..., None] + jnp.einsum(
            "qhgk,khd->qhgd",
            raw_weights.astype(jnp.bfloat16),
            values_part,
            preferred_element_type=jnp.float32,
        )
        return (new_top, new_totals, new_summed)

    start_state = (
        jnp.full(head_shape, masked_score, jnp.float32),
        jnp.zeros(head_shape, jnp.float32),
        jnp.zeros(head_shape + (HEAD_SIZE,), jnp.float32),
    )
    top_now, totals, summed = lax.fori_loop(0, n_needed, key_block, start_state)

    my_request = jnp.sum(jnp.where(cache_slot == device_seq, requests, 0))
    my_start = jnp.sum(jnp.where(requests == my_request, starts, 0))
    my_length = jnp.sum(jnp.where(requests == my_request, prompt_lengths, 0))
    offsets = jnp.arange(LMAX, dtype=jnp.int32)
    wanted = my_start + offsets
    in_window = ((wanted < stream) & (offsets < my_length))[:, None]
    source = jnp.clip(wanted, 0, stream - 1)
    zero = jnp.zeros((), jnp.bfloat16)
    cache_k = jnp.where(in_window, jnp.take(k_all, k_row_of(source), axis=0), zero)
    cache_v = jnp.where(in_window, jnp.take(v_ring, v_row_of(source), axis=0), zero)

    attended = (summed / totals[..., None]).reshape(local_rows, query_heads * HEAD_SIZE)
    gated_heads = (attended * jax.nn.sigmoid(gate_logits)).astype(jnp.bfloat16)
    partial_out = lax.dot_general(
        gated_heads,
        w_out_t,
        (((1,), (1,)), ((), ())),
        preferred_element_type=jnp.float32,
    )
    mdl_index = lax.axis_index("mdl")
    n_mdl = lax.axis_size("mdl")
    x_lo = mdl_index // 2
    core = mdl_index % 2
    half = partial_out.shape[1] // 2
    quarter = half // 2
    mine = lax.dynamic_slice_in_dim(partial_out, x_lo * half, half, 1)
    theirs = lax.dynamic_slice_in_dim(partial_out, (1 - x_lo) * half, half, 1)
    across = lax.ppermute(
        theirs.astype(jnp.bfloat16), "mdl", [(m, m ^ 2) for m in range(n_mdl)]
    )
    half_sum = mine + across.astype(jnp.float32)
    mine = lax.dynamic_slice_in_dim(half_sum, core * quarter, quarter, 1)
    theirs = lax.dynamic_slice_in_dim(half_sum, (1 - core) * quarter, quarter, 1)
    branch_sum = mine + lax.ppermute(theirs, "mdl", [(m, m ^ 1) for m in range(n_mdl)])
    layer_out = (wide_tokens + branch_sum).astype(jnp.bfloat16)
    return (layer_out, cache_k[None], cache_v[None])


def solution(mesh):
    seq = SEQ_PARTS
    split = Mesh(mesh.devices.reshape(8, 4, 2, mesh.shape["mdl"]), SEQ_PARTS + ("mdl",))
    placed = (
        P(seq, "mdl"),
        P("mdl"),
        P(seq, "mdl"),
        P(seq, "mdl"),
        P(seq, "mdl"),
        P(seq, "mdl"),
        P(),
        P(),
        P("mdl", seq),
        P(),
        P(seq),
        P(),
        P(seq),
        P(),
    )
    return jax.shard_map(
        body,
        mesh=split,
        in_specs=placed,
        out_specs=(P(seq, "mdl"), P(seq, None, "mdl"), P(seq, None, "mdl")),
        check_vma=False,
    )
```

```python
import jax
import jax.numpy as jnp
from jax import lax
from jax.experimental import pallas as pl
from jax.experimental.pallas import tpu as pltpu
from jax.sharding import Mesh
from jax.sharding import PartitionSpec as P

HEAD_SIZE = 128
LMAX = 512
KEY_BLOCK = 256


epsilon = 1e-06
rope_base = 1000000.0
masked_score = -1e30


def head_norm(values, gain_vector):
    return (
        values
        * lax.rsqrt(jnp.mean(values * values, axis=-1, keepdims=True) + epsilon)
        * gain_vector
    )


def rotate(values, position):
    half_width = values.shape[-1] // 2
    frequency = rope_base ** (-2.0 * jnp.arange(half_width, dtype=jnp.float32) / values.shape[-1])
    angles = position.astype(jnp.float32)[:, None] * frequency[None, :]
    cosine = jnp.cos(angles)[:, None, :]
    sine_part = jnp.sin(angles)[:, None, :]
    former = values[..., :half_width]
    latter = values[..., half_width:]
    return jnp.concatenate(
        [former * cosine - latter * sine_part, latter * cosine + former * sine_part], axis=-1
    )


SEQ_PARTS = ("z", "y", "xh")
MESH_ID = pl.DeviceIdType.MESH
AXES = SEQ_PARTS + ("mdl",)


def _ring_kernel(x_ref, out_ref, send_sem, recv_sem, local_sem):
    ny = 4
    me = {name: lax.axis_index(name) for name in AXES}
    my_y = me["y"]

    def dev(yy):
        return tuple(yy if name == "y" else me[name] for name in AXES)

    plus = dev(lax.rem(my_y + 1, ny))
    minus = dev(lax.rem(my_y + ny - 1, ny))
    barrier = pltpu.get_barrier_semaphore()
    for d in (plus, minus):
        pl.semaphore_signal(barrier, inc=1, device_id=d, device_id_type=MESH_ID)
    pl.semaphore_wait(barrier, 2)

    rows = x_ref.shape[0]
    half = rows // 2
    to_minus = pltpu.make_async_remote_copy(
        src_ref=x_ref, dst_ref=out_ref.at[1], send_sem=send_sem.at[0], recv_sem=recv_sem.at[0],
        device_id=minus, device_id_type=MESH_ID)
    to_plus = pltpu.make_async_remote_copy(
        src_ref=x_ref, dst_ref=out_ref.at[3], send_sem=send_sem.at[1], recv_sem=recv_sem.at[1],
        device_id=plus, device_id_type=MESH_ID)
    own = pltpu.make_async_copy(x_ref, out_ref.at[0], local_sem.at[0])
    to_minus.start()
    to_plus.start()
    own.start()
    to_minus.wait_recv()
    on_minus = pltpu.make_async_remote_copy(
        src_ref=out_ref.at[1, pl.ds(0, half)], dst_ref=out_ref.at[2, pl.ds(0, half)],
        send_sem=send_sem.at[2], recv_sem=recv_sem.at[2], device_id=minus, device_id_type=MESH_ID)
    on_minus.start()
    to_plus.wait_recv()
    on_plus = pltpu.make_async_remote_copy(
        src_ref=out_ref.at[3, pl.ds(half, rows - half)], dst_ref=out_ref.at[2, pl.ds(half, rows - half)],
        send_sem=send_sem.at[3], recv_sem=recv_sem.at[3], device_id=plus, device_id_type=MESH_ID)
    on_plus.start()
    to_minus.wait_send()
    to_plus.wait_send()
    own.wait()
    on_minus.wait_send()
    on_plus.wait_send()
    on_minus.wait_recv()
    on_plus.wait_recv()


def ring_y_kernel(x, collective_id):
    rows, width = x.shape
    return pl.pallas_call(
        _ring_kernel,
        out_shape=jax.ShapeDtypeStruct((4, rows, width), x.dtype),
        in_specs=[pl.BlockSpec(memory_space=pl.ANY)],
        out_specs=pl.BlockSpec(memory_space=pl.ANY),
        scratch_shapes=[
            pltpu.SemaphoreType.DMA((4,)),
            pltpu.SemaphoreType.DMA((4,)),
            pltpu.SemaphoreType.DMA((1,)),
        ],
        compiler_params=pltpu.CompilerParams(collective_id=collective_id, has_side_effects=True),
    )(x)


def gather_seq(x):
    for name in reversed(SEQ_PARTS):
        x = lax.all_gather(x, name, axis=0, tiled=True)
    return x


def gather_xh_z(x):
    x = lax.all_gather(x, "xh", axis=0, tiled=True)
    return lax.all_gather(x, "z", axis=0, tiled=True)


def ring_y(x):
    ny = 4
    right = [(i, (i + 1) % ny) for i in range(ny)]
    left = [(i, (i - 1) % ny) for i in range(ny)]
    from_minus = lax.ppermute(x, "y", right)
    from_plus = lax.ppermute(x, "y", left)
    half = x.shape[0] // 2
    opp_a = lax.ppermute(from_minus[:half], "y", right)
    opp_b = lax.ppermute(from_plus[half:], "y", left)
    opposite = jnp.concatenate([opp_a, opp_b], axis=0)
    return jnp.stack([x, from_plus, opposite, from_minus])


def gather_mdl(x):
    mdl_index = lax.axis_index("mdl")
    n_mdl = lax.axis_size("mdl")
    other = lax.ppermute(x, "mdl", [(m, m ^ 1) for m in range(n_mdl)])
    pair = jnp.where(
        mdl_index % 2 == 0,
        jnp.concatenate([x, other], axis=1),
        jnp.concatenate([other, x], axis=1),
    )
    other = lax.ppermute(pair, "mdl", [(m, m ^ 2) for m in range(n_mdl)])
    return jnp.where(
        mdl_index // 2 == 0,
        jnp.concatenate([pair, other], axis=1),
        jnp.concatenate([other, pair], axis=1),
    )


def body(
    tokens,
    norm_gain,
    w_query,
    key_matrix,
    value_matrix,
    w_gate,
    q_gain,
    k_gain,
    w_out,
    prompt_lengths,
    segment_ids,
    tenant_ranges,
    key_mask,
    cache_slot,
):
    local_rows = tokens.shape[0]
    weight_rows = w_query.shape[0]
    q_cols = w_query.shape[1]
    kv_cols = key_matrix.shape[1]
    g_cols = w_gate.shape[1]
    seq_size = lax.axis_size(SEQ_PARTS)
    stream = local_rows * seq_size
    request_count = prompt_lengths.shape[0]

    mask_cols = local_rows // weight_rows
    mask_block = key_mask.astype(jnp.bfloat16).reshape(weight_rows, mask_cols)
    mask_block = jnp.pad(mask_block, ((0, 0), (0, 128 - mask_cols)))
    packed = jnp.concatenate([w_query, key_matrix, value_matrix, w_out.T, mask_block], axis=1)
    packed = lax.all_gather(packed, "xh", axis=0, tiled=True)
    packed = lax.all_gather(packed, "y", axis=0, tiled=True)
    packed, gate_in = lax.optimization_barrier((packed, w_gate))
    gate_ring = ring_y_kernel(gather_xh_z(gate_in), 1)
    gathered = lax.all_gather(packed, "z", axis=0, tiled=True)
    gathered, gate_ring = lax.optimization_barrier((gathered, gate_ring))
    proj_cols = q_cols + 2 * kv_cols
    w_proj = gathered[:, :proj_cols]
    w_out_t = gathered[:, proj_cols : proj_cols + w_out.shape[0]]
    all_mask = gathered[:, proj_cols + w_out.shape[0] : proj_cols + w_out.shape[0] + mask_cols]
    all_mask = all_mask.reshape(stream)
    w_gate_perm = gate_ring.reshape(-1, g_cols)

    wide_tokens = tokens.astype(jnp.float32)
    full_width = tokens.shape[1] * lax.axis_size("mdl")
    square_total = lax.psum(jnp.sum(wide_tokens * wide_tokens, axis=1), "mdl")
    scaled = (
        wide_tokens
        * lax.rsqrt(square_total / full_width + epsilon)[:, None]
        * norm_gain.astype(jnp.float32)
    )
    normalized_input = gather_mdl(scaled.astype(jnp.bfloat16))
    projected = jnp.dot(normalized_input, w_proj, preferred_element_type=jnp.float32)
    query_rows = projected[:, :q_cols]
    unprojected_keys = projected[:, q_cols : q_cols + kv_cols]
    values_raw = projected[:, q_cols + kv_cols : q_cols + 2 * kv_cols]
    my_y = lax.axis_index("y")
    input_perm = normalized_input.reshape(local_rows, 8, 4, 2, weight_rows)
    input_perm = jnp.roll(input_perm, -my_y, axis=2)
    input_perm = input_perm.transpose(0, 2, 1, 3, 4).reshape(local_rows, -1)
    gate_logits = jnp.dot(input_perm, w_gate_perm, preferred_element_type=jnp.float32)

    device_seq = lax.axis_index(SEQ_PARTS)
    token_ids = device_seq * local_rows + jnp.arange(local_rows, dtype=jnp.int32)
    starts = jnp.cumsum(prompt_lengths) - prompt_lengths
    ends = starts + prompt_lengths
    requests = jnp.arange(request_count, dtype=jnp.int32)
    member = (requests[:, None] > tenant_ranges[None, :, 0]) & (
        requests[:, None] < tenant_ranges[None, :, 1]
    )
    shared_of = jnp.sum(jnp.where(member, tenant_ranges[None, :, 0] + 3, 0), axis=1) - 3
    onehot = segment_ids[:, None] == requests[None, :]
    seg_start = jnp.sum(jnp.where(onehot, starts[None, :], 0), axis=1)
    shared_req = jnp.sum(jnp.where(onehot, shared_of[None, :], 0), axis=1)
    position = token_ids - seg_start

    query_heads = q_cols // HEAD_SIZE
    kv_heads = kv_cols // HEAD_SIZE
    group = query_heads // kv_heads
    q_rot = (
        rotate(head_norm(query_rows.reshape(local_rows, query_heads, HEAD_SIZE), q_gain), position)
        .astype(jnp.bfloat16)
        .reshape(local_rows, kv_heads, group, HEAD_SIZE)
    )
    k_rot = (
        rotate(head_norm(unprojected_keys.reshape(local_rows, kv_heads, HEAD_SIZE), k_gain), position)
        .astype(jnp.bfloat16)
        .reshape(local_rows, kv_cols)
    )
    values_flat = values_raw.astype(jnp.bfloat16)
    kv_pair = lax.all_gather(jnp.concatenate([k_rot, values_flat], axis=1), "xh", axis=0, tiled=True)
    v_part = lax.all_gather(kv_pair[:, kv_cols:], "z", axis=0, tiled=True)
    k_part = ring_y_kernel(kv_pair[:, :kv_cols], 2).reshape(-1, kv_cols)
    k_part, v_part = lax.optimization_barrier((k_part, v_part))
    k_all = lax.all_gather(k_part, "z", axis=0, tiled=True)
    v_ring = ring_y_kernel(v_part, 3).reshape(-1, kv_cols)

    def k_row_of(token):
        block = token // local_rows
        rel = (block // 2 % 4 - my_y) % 4
        place = ((block // 8) * 4 + rel) * 2 + block % 2
        return place * local_rows + token % local_rows

    def v_row_of(token):
        block = token // local_rows
        rel = (block // 2 % 4 - my_y) % 4
        place = (block // 8) * 2 + block % 2
        return (rel * 16 + place) * local_rows + token % local_rows

    n_blocks = stream // KEY_BLOCK
    block_ids = jnp.arange(n_blocks, dtype=jnp.int32)
    last_block = (device_seq * local_rows + local_rows - 1) // KEY_BLOCK
    first_block = jnp.min(seg_start) // KEY_BLOCK
    needed = (block_ids >= first_block) & (block_ids <= last_block)
    lo = tenant_ranges[:, 0]
    hi = tenant_ranges[:, 1]
    used = jnp.any(
        (segment_ids[:, None] > lo[None, :]) & (segment_ids[:, None] < hi[None, :]), axis=0
    )
    lo_start = jnp.sum(jnp.where(requests[None, :] == lo[:, None], starts[None, :], 0), axis=1)
    lo_end = jnp.sum(jnp.where(requests[None, :] == lo[:, None], ends[None, :], 0), axis=1)
    in_prompt = (
        used[:, None]
        & (block_ids[None, :] >= (lo_start // KEY_BLOCK)[:, None])
        & (block_ids[None, :] <= ((lo_end - 1) // KEY_BLOCK)[:, None])
    )
    needed = needed | jnp.any(in_prompt, axis=0)
    n_needed = jnp.sum(needed.astype(jnp.int32))
    (block_list,) = jnp.nonzero(needed, size=n_blocks, fill_value=0)
    block_list = block_list.astype(jnp.int32)

    row_segs = segment_ids
    row_shared = shared_req
    scale_factor = HEAD_SIZE ** (-0.5)
    head_shape = (local_rows, kv_heads, group)

    def key_block(i, loop_state):
        old_top, old_totals, old_summed = loop_state
        block = block_list[i]
        offset = block * KEY_BLOCK
        keys_part = lax.dynamic_slice_in_dim(k_all, k_row_of(offset), KEY_BLOCK, 0).reshape(
            KEY_BLOCK, kv_heads, HEAD_SIZE
        )
        values_part = lax.dynamic_slice_in_dim(v_ring, v_row_of(offset), KEY_BLOCK, 0).reshape(
            KEY_BLOCK, kv_heads, HEAD_SIZE
        )
        mask_part = lax.dynamic_slice_in_dim(all_mask, offset, KEY_BLOCK, 0)
        columns = offset + jnp.arange(KEY_BLOCK, dtype=jnp.int32)
        col_segs = jnp.sum((columns[:, None] >= ends[None, :]).astype(jnp.int32), axis=1)
        live = mask_part == 1
        own = col_segs[None, :] == row_segs[:, None]
        other = col_segs[None, :] == row_shared[:, None]
        earlier = columns[None, :] <= token_ids[:, None]
        diagonal = columns[None, :] == token_ids[:, None]
        visible = diagonal | (earlier & live[None, :] & (own | other))
        allowed = visible[:, None, None, :]
        scores = (
            jnp.einsum("qhgd,khd->qhgk", q_rot, keys_part, preferred_element_type=jnp.float32)
            * scale_factor
        )
        scores = jnp.where(allowed, scores, masked_score)
        new_top = jnp.maximum(old_top, jnp.max(scores, axis=-1))
        factor = jnp.exp(old_top - new_top)
        raw_weights = jnp.where(allowed, jnp.exp(scores - new_top[..., None]), 0.0)
        new_totals = old_totals * factor + jnp.sum(raw_weights, axis=-1)
        new_summed = old_summed * factor[..., None] + jnp.einsum(
            "qhgk,khd->qhgd",
            raw_weights.astype(jnp.bfloat16),
            values_part,
            preferred_element_type=jnp.float32,
        )
        return (new_top, new_totals, new_summed)

    start_state = (
        jnp.full(head_shape, masked_score, jnp.float32),
        jnp.zeros(head_shape, jnp.float32),
        jnp.zeros(head_shape + (HEAD_SIZE,), jnp.float32),
    )
    top_now, totals, summed = lax.fori_loop(0, n_needed, key_block, start_state)

    my_request = jnp.sum(jnp.where(cache_slot == device_seq, requests, 0))
    my_start = jnp.sum(jnp.where(requests == my_request, starts, 0))
    my_length = jnp.sum(jnp.where(requests == my_request, prompt_lengths, 0))
    offsets = jnp.arange(LMAX, dtype=jnp.int32)
    wanted = my_start + offsets
    in_window = ((wanted < stream) & (offsets < my_length))[:, None]
    source = jnp.clip(wanted, 0, stream - 1)
    zero = jnp.zeros((), jnp.bfloat16)
    cache_k = jnp.where(in_window, jnp.take(k_all, k_row_of(source), axis=0), zero)
    cache_v = jnp.where(in_window, jnp.take(v_ring, v_row_of(source), axis=0), zero)

    attended = (summed / totals[..., None]).reshape(local_rows, query_heads * HEAD_SIZE)
    gated_heads = (attended * jax.nn.sigmoid(gate_logits)).astype(jnp.bfloat16)
    partial_out = lax.dot_general(
        gated_heads,
        w_out_t,
        (((1,), (1,)), ((), ())),
        preferred_element_type=jnp.float32,
    )
    mdl_index = lax.axis_index("mdl")
    n_mdl = lax.axis_size("mdl")
    x_lo = mdl_index // 2
    core = mdl_index % 2
    half = partial_out.shape[1] // 2
    quarter = half // 2
    mine = lax.dynamic_slice_in_dim(partial_out, x_lo * half, half, 1)
    theirs = lax.dynamic_slice_in_dim(partial_out, (1 - x_lo) * half, half, 1)
    across = lax.ppermute(
        theirs.astype(jnp.bfloat16), "mdl", [(m, m ^ 2) for m in range(n_mdl)]
    )
    half_sum = mine + across.astype(jnp.float32)
    mine = lax.dynamic_slice_in_dim(half_sum, core * quarter, quarter, 1)
    theirs = lax.dynamic_slice_in_dim(half_sum, (1 - core) * quarter, quarter, 1)
    branch_sum = mine + lax.ppermute(theirs, "mdl", [(m, m ^ 1) for m in range(n_mdl)])
    layer_out = (wide_tokens + branch_sum).astype(jnp.bfloat16)
    return (layer_out, cache_k[None], cache_v[None])


def solution(mesh):
    seq = SEQ_PARTS
    split = Mesh(mesh.devices.reshape(8, 4, 2, mesh.shape["mdl"]), SEQ_PARTS + ("mdl",))
    placed = (
        P(seq, "mdl"),
        P("mdl"),
        P(seq, "mdl"),
        P(seq, "mdl"),
        P(seq, "mdl"),
        P(seq, "mdl"),
        P(),
        P(),
        P("mdl", seq),
        P(),
        P(seq),
        P(),
        P(seq),
        P(),
    )
    return jax.shard_map(
        body,
        mesh=split,
        in_specs=placed,
        out_specs=(P(seq, "mdl"), P(seq, None, "mdl"), P(seq, None, "mdl")),
        check_vma=False,
    )
```

```python
import jax
import jax.numpy as jnp
from jax import lax
from jax.experimental import pallas as pl
from jax.experimental.pallas import tpu as pltpu
from jax.sharding import Mesh
from jax.sharding import PartitionSpec as P

HEAD_SIZE = 128
LMAX = 512
KEY_BLOCK = 256


epsilon = 1e-06
rope_base = 1000000.0
masked_score = -1e30


def head_norm(values, gain_vector):
    return (
        values
        * lax.rsqrt(jnp.mean(values * values, axis=-1, keepdims=True) + epsilon)
        * gain_vector
    )


def rotate(values, position):
    half_width = values.shape[-1] // 2
    frequency = rope_base ** (-2.0 * jnp.arange(half_width, dtype=jnp.float32) / values.shape[-1])
    angles = position.astype(jnp.float32)[:, None] * frequency[None, :]
    cosine = jnp.cos(angles)[:, None, :]
    sine_part = jnp.sin(angles)[:, None, :]
    former = values[..., :half_width]
    latter = values[..., half_width:]
    return jnp.concatenate(
        [former * cosine - latter * sine_part, latter * cosine + former * sine_part], axis=-1
    )


SEQ_PARTS = ("z", "y", "xh")
MESH_ID = pl.DeviceIdType.MESH
AXES = SEQ_PARTS + ("mdl",)
RING_CHUNKS = 4


def _ring_kernel(x_ref, out_ref, send_sem, recv_sem, local_sem):
    ny = 4
    me = {name: lax.axis_index(name) for name in AXES}
    my_y = me["y"]

    def dev(yy):
        return tuple(yy if name == "y" else me[name] for name in AXES)

    plus = dev(lax.rem(my_y + 1, ny))
    minus = dev(lax.rem(my_y + ny - 1, ny))
    barrier = pltpu.get_barrier_semaphore()
    for d in (plus, minus):
        pl.semaphore_signal(barrier, inc=1, device_id=d, device_id_type=MESH_ID)
    pl.semaphore_wait(barrier, 2)

    rows = x_ref.shape[0]
    n = RING_CHUNKS
    step = rows // n

    def rows_of(c):
        return pl.ds(c * step, step)

    def remote(src, dst, k, device):
        return pltpu.make_async_remote_copy(
            src_ref=src, dst_ref=dst, send_sem=send_sem.at[k], recv_sem=recv_sem.at[k],
            device_id=device, device_id_type=MESH_ID)

    to_minus = [remote(x_ref.at[rows_of(c)], out_ref.at[1, rows_of(c)], c, minus) for c in range(n)]
    to_plus = [
        remote(x_ref.at[rows_of(c)], out_ref.at[3, rows_of(c)], n + c, plus) for c in range(n)
    ]
    own = pltpu.make_async_copy(x_ref, out_ref.at[0], local_sem.at[0])
    for i in range(n):
        to_minus[i].start()
        to_plus[n - 1 - i].start()
    own.start()
    forwards = []
    for i in range(n // 2):
        c = i
        to_minus[c].wait_recv()
        f = remote(out_ref.at[1, rows_of(c)], out_ref.at[2, rows_of(c)], 2 * n + c, minus)
        f.start()
        forwards.append(f)
        c = n - 1 - i
        to_plus[c].wait_recv()
        f = remote(out_ref.at[3, rows_of(c)], out_ref.at[2, rows_of(c)], 2 * n + c, plus)
        f.start()
        forwards.append(f)
    for i in range(n // 2, n):
        to_minus[i].wait_recv()
        to_plus[n - 1 - i].wait_recv()
    for copy in to_minus + to_plus:
        copy.wait_send()
    own.wait()
    for f in forwards:
        f.wait_send()
    for f in forwards:
        f.wait_recv()


def ring_y_kernel(x, collective_id):
    rows, width = x.shape
    return pl.pallas_call(
        _ring_kernel,
        out_shape=jax.ShapeDtypeStruct((4, rows, width), x.dtype),
        in_specs=[pl.BlockSpec(memory_space=pl.ANY)],
        out_specs=pl.BlockSpec(memory_space=pl.ANY),
        scratch_shapes=[
            pltpu.SemaphoreType.DMA((3 * RING_CHUNKS,)),
            pltpu.SemaphoreType.DMA((3 * RING_CHUNKS,)),
            pltpu.SemaphoreType.DMA((1,)),
        ],
        compiler_params=pltpu.CompilerParams(collective_id=collective_id, has_side_effects=True),
    )(x)


def gather_seq(x):
    for name in reversed(SEQ_PARTS):
        x = lax.all_gather(x, name, axis=0, tiled=True)
    return x


def gather_xh_z(x):
    x = lax.all_gather(x, "xh", axis=0, tiled=True)
    return lax.all_gather(x, "z", axis=0, tiled=True)


def ring_y(x):
    ny = 4
    right = [(i, (i + 1) % ny) for i in range(ny)]
    left = [(i, (i - 1) % ny) for i in range(ny)]
    from_minus = lax.ppermute(x, "y", right)
    from_plus = lax.ppermute(x, "y", left)
    half = x.shape[0] // 2
    opp_a = lax.ppermute(from_minus[:half], "y", right)
    opp_b = lax.ppermute(from_plus[half:], "y", left)
    opposite = jnp.concatenate([opp_a, opp_b], axis=0)
    return jnp.stack([x, from_plus, opposite, from_minus])


def gather_mdl(x):
    mdl_index = lax.axis_index("mdl")
    n_mdl = lax.axis_size("mdl")
    other = lax.ppermute(x, "mdl", [(m, m ^ 1) for m in range(n_mdl)])
    pair = jnp.where(
        mdl_index % 2 == 0,
        jnp.concatenate([x, other], axis=1),
        jnp.concatenate([other, x], axis=1),
    )
    other = lax.ppermute(pair, "mdl", [(m, m ^ 2) for m in range(n_mdl)])
    return jnp.where(
        mdl_index // 2 == 0,
        jnp.concatenate([pair, other], axis=1),
        jnp.concatenate([other, pair], axis=1),
    )


def body(
    tokens,
    norm_gain,
    w_query,
    key_matrix,
    value_matrix,
    w_gate,
    q_gain,
    k_gain,
    w_out,
    prompt_lengths,
    segment_ids,
    tenant_ranges,
    key_mask,
    cache_slot,
):
    local_rows = tokens.shape[0]
    weight_rows = w_query.shape[0]
    q_cols = w_query.shape[1]
    kv_cols = key_matrix.shape[1]
    g_cols = w_gate.shape[1]
    seq_size = lax.axis_size(SEQ_PARTS)
    stream = local_rows * seq_size
    request_count = prompt_lengths.shape[0]

    mask_cols = local_rows // weight_rows
    mask_block = key_mask.astype(jnp.bfloat16).reshape(weight_rows, mask_cols)
    mask_block = jnp.pad(mask_block, ((0, 0), (0, 128 - mask_cols)))
    packed = jnp.concatenate([w_query, key_matrix, value_matrix, w_out.T, mask_block], axis=1)
    packed = lax.all_gather(packed, "xh", axis=0, tiled=True)
    packed = lax.all_gather(packed, "y", axis=0, tiled=True)
    packed, gate_in = lax.optimization_barrier((packed, w_gate))
    gate_ring = ring_y_kernel(gather_xh_z(gate_in), 1)
    gathered = lax.all_gather(packed, "z", axis=0, tiled=True)
    gathered, gate_ring = lax.optimization_barrier((gathered, gate_ring))
    proj_cols = q_cols + 2 * kv_cols
    w_proj = gathered[:, :proj_cols]
    w_out_t = gathered[:, proj_cols : proj_cols + w_out.shape[0]]
    all_mask = gathered[:, proj_cols + w_out.shape[0] : proj_cols + w_out.shape[0] + mask_cols]
    all_mask = all_mask.reshape(stream)
    w_gate_perm = gate_ring.reshape(-1, g_cols)

    wide_tokens = tokens.astype(jnp.float32)
    full_width = tokens.shape[1] * lax.axis_size("mdl")
    square_total = lax.psum(jnp.sum(wide_tokens * wide_tokens, axis=1), "mdl")
    scaled = (
        wide_tokens
        * lax.rsqrt(square_total / full_width + epsilon)[:, None]
        * norm_gain.astype(jnp.float32)
    )
    normalized_input = gather_mdl(scaled.astype(jnp.bfloat16))
    projected = jnp.dot(normalized_input, w_proj, preferred_element_type=jnp.float32)
    query_rows = projected[:, :q_cols]
    unprojected_keys = projected[:, q_cols : q_cols + kv_cols]
    values_raw = projected[:, q_cols + kv_cols : q_cols + 2 * kv_cols]
    my_y = lax.axis_index("y")
    input_perm = normalized_input.reshape(local_rows, 8, 4, 2, weight_rows)
    input_perm = jnp.roll(input_perm, -my_y, axis=2)
    input_perm = input_perm.transpose(0, 2, 1, 3, 4).reshape(local_rows, -1)
    gate_logits = jnp.dot(input_perm, w_gate_perm, preferred_element_type=jnp.float32)

    device_seq = lax.axis_index(SEQ_PARTS)
    token_ids = device_seq * local_rows + jnp.arange(local_rows, dtype=jnp.int32)
    starts = jnp.cumsum(prompt_lengths) - prompt_lengths
    ends = starts + prompt_lengths
    requests = jnp.arange(request_count, dtype=jnp.int32)
    member = (requests[:, None] > tenant_ranges[None, :, 0]) & (
        requests[:, None] < tenant_ranges[None, :, 1]
    )
    shared_of = jnp.sum(jnp.where(member, tenant_ranges[None, :, 0] + 3, 0), axis=1) - 3
    onehot = segment_ids[:, None] == requests[None, :]
    seg_start = jnp.sum(jnp.where(onehot, starts[None, :], 0), axis=1)
    shared_req = jnp.sum(jnp.where(onehot, shared_of[None, :], 0), axis=1)
    position = token_ids - seg_start

    query_heads = q_cols // HEAD_SIZE
    kv_heads = kv_cols // HEAD_SIZE
    group = query_heads // kv_heads
    q_rot = (
        rotate(head_norm(query_rows.reshape(local_rows, query_heads, HEAD_SIZE), q_gain), position)
        .astype(jnp.bfloat16)
        .reshape(local_rows, kv_heads, group, HEAD_SIZE)
    )
    k_rot = (
        rotate(head_norm(unprojected_keys.reshape(local_rows, kv_heads, HEAD_SIZE), k_gain), position)
        .astype(jnp.bfloat16)
        .reshape(local_rows, kv_cols)
    )
    values_flat = values_raw.astype(jnp.bfloat16)
    kv_pair = lax.all_gather(jnp.concatenate([k_rot, values_flat], axis=1), "xh", axis=0, tiled=True)
    v_part = lax.all_gather(kv_pair[:, kv_cols:], "z", axis=0, tiled=True)
    k_part = ring_y_kernel(kv_pair[:, :kv_cols], 2).reshape(-1, kv_cols)
    k_part, v_part = lax.optimization_barrier((k_part, v_part))
    k_all = lax.all_gather(k_part, "z", axis=0, tiled=True)
    v_ring = ring_y_kernel(v_part, 3).reshape(-1, kv_cols)

    def k_row_of(token):
        block = token // local_rows
        rel = (block // 2 % 4 - my_y) % 4
        place = ((block // 8) * 4 + rel) * 2 + block % 2
        return place * local_rows + token % local_rows

    def v_row_of(token):
        block = token // local_rows
        rel = (block // 2 % 4 - my_y) % 4
        place = (block // 8) * 2 + block % 2
        return (rel * 16 + place) * local_rows + token % local_rows

    n_blocks = stream // KEY_BLOCK
    block_ids = jnp.arange(n_blocks, dtype=jnp.int32)
    last_block = (device_seq * local_rows + local_rows - 1) // KEY_BLOCK
    first_block = jnp.min(seg_start) // KEY_BLOCK
    needed = (block_ids >= first_block) & (block_ids <= last_block)
    lo = tenant_ranges[:, 0]
    hi = tenant_ranges[:, 1]
    used = jnp.any(
        (segment_ids[:, None] > lo[None, :]) & (segment_ids[:, None] < hi[None, :]), axis=0
    )
    lo_start = jnp.sum(jnp.where(requests[None, :] == lo[:, None], starts[None, :], 0), axis=1)
    lo_end = jnp.sum(jnp.where(requests[None, :] == lo[:, None], ends[None, :], 0), axis=1)
    in_prompt = (
        used[:, None]
        & (block_ids[None, :] >= (lo_start // KEY_BLOCK)[:, None])
        & (block_ids[None, :] <= ((lo_end - 1) // KEY_BLOCK)[:, None])
    )
    needed = needed | jnp.any(in_prompt, axis=0)
    n_needed = jnp.sum(needed.astype(jnp.int32))
    (block_list,) = jnp.nonzero(needed, size=n_blocks, fill_value=0)
    block_list = block_list.astype(jnp.int32)

    row_segs = segment_ids
    row_shared = shared_req
    scale_factor = HEAD_SIZE ** (-0.5)
    head_shape = (local_rows, kv_heads, group)

    def key_block(i, loop_state):
        old_top, old_totals, old_summed = loop_state
        block = block_list[i]
        offset = block * KEY_BLOCK
        keys_part = lax.dynamic_slice_in_dim(k_all, k_row_of(offset), KEY_BLOCK, 0).reshape(
            KEY_BLOCK, kv_heads, HEAD_SIZE
        )
        values_part = lax.dynamic_slice_in_dim(v_ring, v_row_of(offset), KEY_BLOCK, 0).reshape(
            KEY_BLOCK, kv_heads, HEAD_SIZE
        )
        mask_part = lax.dynamic_slice_in_dim(all_mask, offset, KEY_BLOCK, 0)
        columns = offset + jnp.arange(KEY_BLOCK, dtype=jnp.int32)
        col_segs = jnp.sum((columns[:, None] >= ends[None, :]).astype(jnp.int32), axis=1)
        live = mask_part == 1
        own = col_segs[None, :] == row_segs[:, None]
        other = col_segs[None, :] == row_shared[:, None]
        earlier = columns[None, :] <= token_ids[:, None]
        diagonal = columns[None, :] == token_ids[:, None]
        visible = diagonal | (earlier & live[None, :] & (own | other))
        allowed = visible[:, None, None, :]
        scores = (
            jnp.einsum("qhgd,khd->qhgk", q_rot, keys_part, preferred_element_type=jnp.float32)
            * scale_factor
        )
        scores = jnp.where(allowed, scores, masked_score)
        new_top = jnp.maximum(old_top, jnp.max(scores, axis=-1))
        factor = jnp.exp(old_top - new_top)
        raw_weights = jnp.where(allowed, jnp.exp(scores - new_top[..., None]), 0.0)
        new_totals = old_totals * factor + jnp.sum(raw_weights, axis=-1)
        new_summed = old_summed * factor[..., None] + jnp.einsum(
            "qhgk,khd->qhgd",
            raw_weights.astype(jnp.bfloat16),
            values_part,
            preferred_element_type=jnp.float32,
        )
        return (new_top, new_totals, new_summed)

    start_state = (
        jnp.full(head_shape, masked_score, jnp.float32),
        jnp.zeros(head_shape, jnp.float32),
        jnp.zeros(head_shape + (HEAD_SIZE,), jnp.float32),
    )
    top_now, totals, summed = lax.fori_loop(0, n_needed, key_block, start_state)

    my_request = jnp.sum(jnp.where(cache_slot == device_seq, requests, 0))
    my_start = jnp.sum(jnp.where(requests == my_request, starts, 0))
    my_length = jnp.sum(jnp.where(requests == my_request, prompt_lengths, 0))
    offsets = jnp.arange(LMAX, dtype=jnp.int32)
    wanted = my_start + offsets
    in_window = ((wanted < stream) & (offsets < my_length))[:, None]
    source = jnp.clip(wanted, 0, stream - 1)
    zero = jnp.zeros((), jnp.bfloat16)
    cache_k = jnp.where(in_window, jnp.take(k_all, k_row_of(source), axis=0), zero)
    cache_v = jnp.where(in_window, jnp.take(v_ring, v_row_of(source), axis=0), zero)

    attended = (summed / totals[..., None]).reshape(local_rows, query_heads * HEAD_SIZE)
    gated_heads = (attended * jax.nn.sigmoid(gate_logits)).astype(jnp.bfloat16)
    partial_out = lax.dot_general(
        gated_heads,
        w_out_t,
        (((1,), (1,)), ((), ())),
        preferred_element_type=jnp.float32,
    )
    mdl_index = lax.axis_index("mdl")
    n_mdl = lax.axis_size("mdl")
    x_lo = mdl_index // 2
    core = mdl_index % 2
    half = partial_out.shape[1] // 2
    quarter = half // 2
    mine = lax.dynamic_slice_in_dim(partial_out, x_lo * half, half, 1)
    theirs = lax.dynamic_slice_in_dim(partial_out, (1 - x_lo) * half, half, 1)
    across = lax.ppermute(
        theirs.astype(jnp.bfloat16), "mdl", [(m, m ^ 2) for m in range(n_mdl)]
    )
    half_sum = mine + across.astype(jnp.float32)
    mine = lax.dynamic_slice_in_dim(half_sum, core * quarter, quarter, 1)
    theirs = lax.dynamic_slice_in_dim(half_sum, (1 - core) * quarter, quarter, 1)
    branch_sum = mine + lax.ppermute(theirs, "mdl", [(m, m ^ 1) for m in range(n_mdl)])
    layer_out = (wide_tokens + branch_sum).astype(jnp.bfloat16)
    return (layer_out, cache_k[None], cache_v[None])


def solution(mesh):
    seq = SEQ_PARTS
    split = Mesh(mesh.devices.reshape(8, 4, 2, mesh.shape["mdl"]), SEQ_PARTS + ("mdl",))
    placed = (
        P(seq, "mdl"),
        P("mdl"),
        P(seq, "mdl"),
        P(seq, "mdl"),
        P(seq, "mdl"),
        P(seq, "mdl"),
        P(),
        P(),
        P("mdl", seq),
        P(),
        P(seq),
        P(),
        P(seq),
        P(),
    )
    return jax.shard_map(
        body,
        mesh=split,
        in_specs=placed,
        out_specs=(P(seq, "mdl"), P(seq, None, "mdl"), P(seq, None, "mdl")),
        check_vma=False,
    )
```

```python
import jax
import jax.numpy as jnp
from jax import lax
from jax.experimental import pallas as pl
from jax.experimental.pallas import tpu as pltpu
from jax.sharding import Mesh
from jax.sharding import PartitionSpec as P

HEAD_SIZE = 128
LMAX = 512
KEY_BLOCK = 256


epsilon = 1e-06
rope_base = 1000000.0
masked_score = -1e30


def head_norm(values, gain_vector):
    return (
        values
        * lax.rsqrt(jnp.mean(values * values, axis=-1, keepdims=True) + epsilon)
        * gain_vector
    )


def rotate(values, position):
    half_width = values.shape[-1] // 2
    frequency = rope_base ** (-2.0 * jnp.arange(half_width, dtype=jnp.float32) / values.shape[-1])
    angles = position.astype(jnp.float32)[:, None] * frequency[None, :]
    cosine = jnp.cos(angles)[:, None, :]
    sine_part = jnp.sin(angles)[:, None, :]
    former = values[..., :half_width]
    latter = values[..., half_width:]
    return jnp.concatenate(
        [former * cosine - latter * sine_part, latter * cosine + former * sine_part], axis=-1
    )


SEQ_PARTS = ("z", "y", "xh")
MESH_ID = pl.DeviceIdType.MESH
AXES = SEQ_PARTS + ("mdl",)


def _ring_kernel(x_ref, out_ref, send_sem, recv_sem, local_sem):
    ny = 4
    me = {name: lax.axis_index(name) for name in AXES}
    my_y = me["y"]

    def dev(yy):
        return tuple(yy if name == "y" else me[name] for name in AXES)

    plus = dev(lax.rem(my_y + 1, ny))
    minus = dev(lax.rem(my_y + ny - 1, ny))
    barrier = pltpu.get_barrier_semaphore()
    for d in (plus, minus):
        pl.semaphore_signal(barrier, inc=1, device_id=d, device_id_type=MESH_ID)
    pl.semaphore_wait(barrier, 2)

    rows = x_ref.shape[0]
    half = rows // 2
    to_minus = pltpu.make_async_remote_copy(
        src_ref=x_ref, dst_ref=out_ref.at[1], send_sem=send_sem.at[0], recv_sem=recv_sem.at[0],
        device_id=minus, device_id_type=MESH_ID)
    to_plus = pltpu.make_async_remote_copy(
        src_ref=x_ref, dst_ref=out_ref.at[3], send_sem=send_sem.at[1], recv_sem=recv_sem.at[1],
        device_id=plus, device_id_type=MESH_ID)
    own = pltpu.make_async_copy(x_ref, out_ref.at[0], local_sem.at[0])
    to_minus.start()
    to_plus.start()
    own.start()
    to_minus.wait_recv()
    on_minus = pltpu.make_async_remote_copy(
        src_ref=out_ref.at[1, pl.ds(0, half)], dst_ref=out_ref.at[2, pl.ds(0, half)],
        send_sem=send_sem.at[2], recv_sem=recv_sem.at[2], device_id=minus, device_id_type=MESH_ID)
    on_minus.start()
    to_plus.wait_recv()
    on_plus = pltpu.make_async_remote_copy(
        src_ref=out_ref.at[3, pl.ds(half, rows - half)], dst_ref=out_ref.at[2, pl.ds(half, rows - half)],
        send_sem=send_sem.at[3], recv_sem=recv_sem.at[3], device_id=plus, device_id_type=MESH_ID)
    on_plus.start()
    to_minus.wait_send()
    to_plus.wait_send()
    own.wait()
    on_minus.wait_send()
    on_plus.wait_send()
    on_minus.wait_recv()
    on_plus.wait_recv()


def ring_y_kernel(x, collective_id):
    rows, width = x.shape
    return pl.pallas_call(
        _ring_kernel,
        out_shape=jax.ShapeDtypeStruct((4, rows, width), x.dtype),
        in_specs=[pl.BlockSpec(memory_space=pl.ANY)],
        out_specs=pl.BlockSpec(memory_space=pl.ANY),
        scratch_shapes=[
            pltpu.SemaphoreType.DMA((4,)),
            pltpu.SemaphoreType.DMA((4,)),
            pltpu.SemaphoreType.DMA((1,)),
        ],
        compiler_params=pltpu.CompilerParams(collective_id=collective_id, has_side_effects=True),
    )(x)


def gather_seq(x):
    for name in reversed(SEQ_PARTS):
        x = lax.all_gather(x, name, axis=0, tiled=True)
    return x


def gather_xh_z(x):
    x = lax.all_gather(x, "xh", axis=0, tiled=True)
    return lax.all_gather(x, "z", axis=0, tiled=True)


def ring_y(x):
    ny = 4
    right = [(i, (i + 1) % ny) for i in range(ny)]
    left = [(i, (i - 1) % ny) for i in range(ny)]
    from_minus = lax.ppermute(x, "y", right)
    from_plus = lax.ppermute(x, "y", left)
    half = x.shape[0] // 2
    opp_a = lax.ppermute(from_minus[:half], "y", right)
    opp_b = lax.ppermute(from_plus[half:], "y", left)
    opposite = jnp.concatenate([opp_a, opp_b], axis=0)
    return jnp.stack([x, from_plus, opposite, from_minus])


def gather_mdl(x):
    mdl_index = lax.axis_index("mdl")
    n_mdl = lax.axis_size("mdl")
    other = lax.ppermute(x, "mdl", [(m, m ^ 1) for m in range(n_mdl)])
    pair = jnp.where(
        mdl_index % 2 == 0,
        jnp.concatenate([x, other], axis=1),
        jnp.concatenate([other, x], axis=1),
    )
    other = lax.ppermute(pair, "mdl", [(m, m ^ 2) for m in range(n_mdl)])
    return jnp.where(
        mdl_index // 2 == 0,
        jnp.concatenate([pair, other], axis=1),
        jnp.concatenate([other, pair], axis=1),
    )


def body(
    tokens,
    norm_gain,
    w_query,
    key_matrix,
    value_matrix,
    w_gate,
    q_gain,
    k_gain,
    w_out,
    prompt_lengths,
    segment_ids,
    tenant_ranges,
    key_mask,
    cache_slot,
):
    local_rows = tokens.shape[0]
    weight_rows = w_query.shape[0]
    q_cols = w_query.shape[1]
    kv_cols = key_matrix.shape[1]
    g_cols = w_gate.shape[1]
    seq_size = lax.axis_size(SEQ_PARTS)
    stream = local_rows * seq_size
    request_count = prompt_lengths.shape[0]

    mask_cols = local_rows // weight_rows
    mask_block = key_mask.astype(jnp.bfloat16).reshape(weight_rows, mask_cols)
    mask_block = jnp.pad(mask_block, ((0, 0), (0, 128 - mask_cols)))
    packed = jnp.concatenate([w_query, key_matrix, value_matrix, w_out.T, mask_block], axis=1)
    packed = lax.all_gather(packed, "xh", axis=0, tiled=True)
    packed = lax.all_gather(packed, "y", axis=0, tiled=True)
    packed, gate_in = lax.optimization_barrier((packed, w_gate))
    gate_ring = ring_y_kernel(gather_xh_z(gate_in), 1)
    gathered = lax.all_gather(packed, "z", axis=0, tiled=True)
    gathered, gate_ring = lax.optimization_barrier((gathered, gate_ring))
    proj_cols = q_cols + 2 * kv_cols
    w_proj = gathered[:, :proj_cols]
    w_out_t = gathered[:, proj_cols : proj_cols + w_out.shape[0]]
    all_mask = gathered[:, proj_cols + w_out.shape[0] : proj_cols + w_out.shape[0] + mask_cols]
    all_mask = all_mask.reshape(stream)
    w_gate_perm = gate_ring.reshape(-1, g_cols)

    wide_tokens = tokens.astype(jnp.float32)
    full_width = tokens.shape[1] * lax.axis_size("mdl")
    square_total = lax.psum(jnp.sum(wide_tokens * wide_tokens, axis=1), "mdl")
    scaled = (
        wide_tokens
        * lax.rsqrt(square_total / full_width + epsilon)[:, None]
        * norm_gain.astype(jnp.float32)
    )
    normalized_input = gather_mdl(scaled.astype(jnp.bfloat16))
    projected = jnp.dot(normalized_input, w_proj, preferred_element_type=jnp.float32)
    query_rows = projected[:, :q_cols]
    unprojected_keys = projected[:, q_cols : q_cols + kv_cols]
    values_raw = projected[:, q_cols + kv_cols : q_cols + 2 * kv_cols]
    my_y = lax.axis_index("y")
    input_perm = normalized_input.reshape(local_rows, 8, 4, 2, weight_rows)
    input_perm = jnp.roll(input_perm, -my_y, axis=2)
    input_perm = input_perm.transpose(0, 2, 1, 3, 4).reshape(local_rows, -1)
    gate_logits = jnp.dot(input_perm, w_gate_perm, preferred_element_type=jnp.float32)

    device_seq = lax.axis_index(SEQ_PARTS)
    token_ids = device_seq * local_rows + jnp.arange(local_rows, dtype=jnp.int32)
    starts = jnp.cumsum(prompt_lengths) - prompt_lengths
    ends = starts + prompt_lengths
    requests = jnp.arange(request_count, dtype=jnp.int32)
    member = (requests[:, None] > tenant_ranges[None, :, 0]) & (
        requests[:, None] < tenant_ranges[None, :, 1]
    )
    shared_of = jnp.sum(jnp.where(member, tenant_ranges[None, :, 0] + 3, 0), axis=1) - 3
    onehot = segment_ids[:, None] == requests[None, :]
    seg_start = jnp.sum(jnp.where(onehot, starts[None, :], 0), axis=1)
    shared_req = jnp.sum(jnp.where(onehot, shared_of[None, :], 0), axis=1)
    position = token_ids - seg_start

    query_heads = q_cols // HEAD_SIZE
    kv_heads = kv_cols // HEAD_SIZE
    group = query_heads // kv_heads
    q_rot = (
        rotate(head_norm(query_rows.reshape(local_rows, query_heads, HEAD_SIZE), q_gain), position)
        .astype(jnp.bfloat16)
        .reshape(local_rows, kv_heads, group, HEAD_SIZE)
    )
    k_rot = (
        rotate(head_norm(unprojected_keys.reshape(local_rows, kv_heads, HEAD_SIZE), k_gain), position)
        .astype(jnp.bfloat16)
        .reshape(local_rows, kv_cols)
    )
    values_flat = values_raw.astype(jnp.bfloat16)
    kv_pair = lax.all_gather(jnp.concatenate([k_rot, values_flat], axis=1), "xh", axis=0, tiled=True)
    v_part = lax.all_gather(kv_pair[:, kv_cols:], "z", axis=0, tiled=True)
    k_part = ring_y_kernel(kv_pair[:, :kv_cols], 2).reshape(-1, kv_cols)
    k_part, v_part = lax.optimization_barrier((k_part, v_part))
    k_all = lax.all_gather(k_part, "z", axis=0, tiled=True)
    v_ring = ring_y_kernel(v_part, 3).reshape(-1, kv_cols)

    def k_row_of(token):
        block = token // local_rows
        rel = (block // 2 % 4 - my_y) % 4
        place = ((block // 8) * 4 + rel) * 2 + block % 2
        return place * local_rows + token % local_rows

    def v_row_of(token):
        block = token // local_rows
        rel = (block // 2 % 4 - my_y) % 4
        place = (block // 8) * 2 + block % 2
        return (rel * 16 + place) * local_rows + token % local_rows

    n_blocks = stream // KEY_BLOCK
    block_ids = jnp.arange(n_blocks, dtype=jnp.int32)
    last_block = (device_seq * local_rows + local_rows - 1) // KEY_BLOCK
    first_block = jnp.min(seg_start) // KEY_BLOCK
    needed = (block_ids >= first_block) & (block_ids <= last_block)
    lo = tenant_ranges[:, 0]
    hi = tenant_ranges[:, 1]
    used = jnp.any(
        (segment_ids[:, None] > lo[None, :]) & (segment_ids[:, None] < hi[None, :]), axis=0
    )
    lo_start = jnp.sum(jnp.where(requests[None, :] == lo[:, None], starts[None, :], 0), axis=1)
    lo_end = jnp.sum(jnp.where(requests[None, :] == lo[:, None], ends[None, :], 0), axis=1)
    in_prompt = (
        used[:, None]
        & (block_ids[None, :] >= (lo_start // KEY_BLOCK)[:, None])
        & (block_ids[None, :] <= ((lo_end - 1) // KEY_BLOCK)[:, None])
    )
    needed = needed | jnp.any(in_prompt, axis=0)
    n_needed = jnp.sum(needed.astype(jnp.int32))
    (block_list,) = jnp.nonzero(needed, size=n_blocks, fill_value=0)
    block_list = block_list.astype(jnp.int32)

    row_segs = segment_ids
    row_shared = shared_req
    scale_factor = HEAD_SIZE ** (-0.5)
    head_shape = (local_rows, kv_heads, group)

    stream_ids = jnp.arange(stream, dtype=jnp.int32)
    key_segs = jnp.sum((stream_ids[:, None] >= ends[None, :]).astype(jnp.int32), axis=1)
    key_tags = jnp.where(all_mask == 1, key_segs, -2)

    def key_block(i, loop_state):
        old_top, old_totals, old_summed = loop_state
        block = block_list[i]
        offset = block * KEY_BLOCK
        keys_part = lax.dynamic_slice_in_dim(k_all, k_row_of(offset), KEY_BLOCK, 0).reshape(
            KEY_BLOCK, kv_heads, HEAD_SIZE
        )
        values_part = lax.dynamic_slice_in_dim(v_ring, v_row_of(offset), KEY_BLOCK, 0).reshape(
            KEY_BLOCK, kv_heads, HEAD_SIZE
        )
        tag_part = lax.dynamic_slice_in_dim(key_tags, offset, KEY_BLOCK, 0)
        columns = offset + jnp.arange(KEY_BLOCK, dtype=jnp.int32)
        own = tag_part[None, :] == row_segs[:, None]
        other = tag_part[None, :] == row_shared[:, None]
        earlier = columns[None, :] <= token_ids[:, None]
        diagonal = columns[None, :] == token_ids[:, None]
        visible = diagonal | (earlier & (own | other))
        allowed = visible[:, None, None, :]
        scores = (
            jnp.einsum("qhgd,khd->qhgk", q_rot, keys_part, preferred_element_type=jnp.float32)
            * scale_factor
        )
        scores = jnp.where(allowed, scores, masked_score)
        new_top = jnp.maximum(old_top, jnp.max(scores, axis=-1))
        factor = jnp.exp(old_top - new_top)
        raw_weights = jnp.where(allowed, jnp.exp(scores - new_top[..., None]), 0.0)
        new_totals = old_totals * factor + jnp.sum(raw_weights, axis=-1)
        new_summed = old_summed * factor[..., None] + jnp.einsum(
            "qhgk,khd->qhgd",
            raw_weights.astype(jnp.bfloat16),
            values_part,
            preferred_element_type=jnp.float32,
        )
        return (new_top, new_totals, new_summed)

    start_state = (
        jnp.full(head_shape, masked_score, jnp.float32),
        jnp.zeros(head_shape, jnp.float32),
        jnp.zeros(head_shape + (HEAD_SIZE,), jnp.float32),
    )
    top_now, totals, summed = lax.fori_loop(0, n_needed, key_block, start_state)

    my_request = jnp.sum(jnp.where(cache_slot == device_seq, requests, 0))
    my_start = jnp.sum(jnp.where(requests == my_request, starts, 0))
    my_length = jnp.sum(jnp.where(requests == my_request, prompt_lengths, 0))
    offsets = jnp.arange(LMAX, dtype=jnp.int32)
    wanted = my_start + offsets
    in_window = ((wanted < stream) & (offsets < my_length))[:, None]
    zero = jnp.zeros((), jnp.bfloat16)
    first = my_start // KEY_BLOCK
    shift = my_start % KEY_BLOCK
    spans = [jnp.clip(first + j, 0, n_blocks - 1) * KEY_BLOCK for j in range(3)]

    def cache_of(table, row_of):
        pieces = [lax.dynamic_slice_in_dim(table, row_of(b), KEY_BLOCK, 0) for b in spans]
        window = lax.dynamic_slice_in_dim(jnp.concatenate(pieces, axis=0), shift, LMAX, 0)
        return jnp.where(in_window, window, zero)

    cache_k = cache_of(k_all, k_row_of)
    cache_v = cache_of(v_ring, v_row_of)

    attended = (summed / totals[..., None]).reshape(local_rows, query_heads * HEAD_SIZE)
    gated_heads = (attended * jax.nn.sigmoid(gate_logits)).astype(jnp.bfloat16)
    partial_out = lax.dot_general(
        gated_heads,
        w_out_t,
        (((1,), (1,)), ((), ())),
        preferred_element_type=jnp.float32,
    )
    mdl_index = lax.axis_index("mdl")
    n_mdl = lax.axis_size("mdl")
    x_lo = mdl_index // 2
    core = mdl_index % 2
    half = partial_out.shape[1] // 2
    quarter = half // 2
    mine = lax.dynamic_slice_in_dim(partial_out, x_lo * half, half, 1)
    theirs = lax.dynamic_slice_in_dim(partial_out, (1 - x_lo) * half, half, 1)
    across = lax.ppermute(
        theirs.astype(jnp.bfloat16), "mdl", [(m, m ^ 2) for m in range(n_mdl)]
    )
    half_sum = mine + across.astype(jnp.float32)
    mine = lax.dynamic_slice_in_dim(half_sum, core * quarter, quarter, 1)
    theirs = lax.dynamic_slice_in_dim(half_sum, (1 - core) * quarter, quarter, 1)
    branch_sum = mine + lax.ppermute(theirs, "mdl", [(m, m ^ 1) for m in range(n_mdl)])
    layer_out = (wide_tokens + branch_sum).astype(jnp.bfloat16)
    return (layer_out, cache_k[None], cache_v[None])


def solution(mesh):
    seq = SEQ_PARTS
    split = Mesh(mesh.devices.reshape(8, 4, 2, mesh.shape["mdl"]), SEQ_PARTS + ("mdl",))
    placed = (
        P(seq, "mdl"),
        P("mdl"),
        P(seq, "mdl"),
        P(seq, "mdl"),
        P(seq, "mdl"),
        P(seq, "mdl"),
        P(),
        P(),
        P("mdl", seq),
        P(),
        P(seq),
        P(),
        P(seq),
        P(),
    )
    return jax.shard_map(
        body,
        mesh=split,
        in_specs=placed,
        out_specs=(P(seq, "mdl"), P(seq, None, "mdl"), P(seq, None, "mdl")),
        check_vma=False,
    )
```

```python
import jax
import jax.numpy as jnp
from jax import lax
from jax.experimental import pallas as pl
from jax.experimental.pallas import tpu as pltpu
from jax.sharding import Mesh
from jax.sharding import PartitionSpec as P

HEAD_SIZE = 128
LMAX = 512
KEY_BLOCK = 256
BATCH_BLOCKS = 8


epsilon = 1e-06
rope_base = 1000000.0
masked_score = -1e30


def head_norm(values, gain_vector):
    return (
        values
        * lax.rsqrt(jnp.mean(values * values, axis=-1, keepdims=True) + epsilon)
        * gain_vector
    )


def rotate(values, position):
    half_width = values.shape[-1] // 2
    frequency = rope_base ** (-2.0 * jnp.arange(half_width, dtype=jnp.float32) / values.shape[-1])
    angles = position.astype(jnp.float32)[:, None] * frequency[None, :]
    cosine = jnp.cos(angles)[:, None, :]
    sine_part = jnp.sin(angles)[:, None, :]
    former = values[..., :half_width]
    latter = values[..., half_width:]
    return jnp.concatenate(
        [former * cosine - latter * sine_part, latter * cosine + former * sine_part], axis=-1
    )


SEQ_PARTS = ("z", "y", "xh")
MESH_ID = pl.DeviceIdType.MESH
AXES = SEQ_PARTS + ("mdl",)


def _ring_kernel(x_ref, out_ref, send_sem, recv_sem, local_sem):
    ny = 4
    me = {name: lax.axis_index(name) for name in AXES}
    my_y = me["y"]

    def dev(yy):
        return tuple(yy if name == "y" else me[name] for name in AXES)

    plus = dev(lax.rem(my_y + 1, ny))
    minus = dev(lax.rem(my_y + ny - 1, ny))
    barrier = pltpu.get_barrier_semaphore()
    for d in (plus, minus):
        pl.semaphore_signal(barrier, inc=1, device_id=d, device_id_type=MESH_ID)
    pl.semaphore_wait(barrier, 2)

    rows = x_ref.shape[0]
    half = rows // 2
    to_minus = pltpu.make_async_remote_copy(
        src_ref=x_ref, dst_ref=out_ref.at[1], send_sem=send_sem.at[0], recv_sem=recv_sem.at[0],
        device_id=minus, device_id_type=MESH_ID)
    to_plus = pltpu.make_async_remote_copy(
        src_ref=x_ref, dst_ref=out_ref.at[3], send_sem=send_sem.at[1], recv_sem=recv_sem.at[1],
        device_id=plus, device_id_type=MESH_ID)
    own = pltpu.make_async_copy(x_ref, out_ref.at[0], local_sem.at[0])
    to_minus.start()
    to_plus.start()
    own.start()
    to_minus.wait_recv()
    on_minus = pltpu.make_async_remote_copy(
        src_ref=out_ref.at[1, pl.ds(0, half)], dst_ref=out_ref.at[2, pl.ds(0, half)],
        send_sem=send_sem.at[2], recv_sem=recv_sem.at[2], device_id=minus, device_id_type=MESH_ID)
    on_minus.start()
    to_plus.wait_recv()
    on_plus = pltpu.make_async_remote_copy(
        src_ref=out_ref.at[3, pl.ds(half, rows - half)], dst_ref=out_ref.at[2, pl.ds(half, rows - half)],
        send_sem=send_sem.at[3], recv_sem=recv_sem.at[3], device_id=plus, device_id_type=MESH_ID)
    on_plus.start()
    to_minus.wait_send()
    to_plus.wait_send()
    own.wait()
    on_minus.wait_send()
    on_plus.wait_send()
    on_minus.wait_recv()
    on_plus.wait_recv()


def ring_y_kernel(x, collective_id):
    rows, width = x.shape
    return pl.pallas_call(
        _ring_kernel,
        out_shape=jax.ShapeDtypeStruct((4, rows, width), x.dtype),
        in_specs=[pl.BlockSpec(memory_space=pl.ANY)],
        out_specs=pl.BlockSpec(memory_space=pl.ANY),
        scratch_shapes=[
            pltpu.SemaphoreType.DMA((4,)),
            pltpu.SemaphoreType.DMA((4,)),
            pltpu.SemaphoreType.DMA((1,)),
        ],
        compiler_params=pltpu.CompilerParams(collective_id=collective_id, has_side_effects=True),
    )(x)


def gather_seq(x):
    for name in reversed(SEQ_PARTS):
        x = lax.all_gather(x, name, axis=0, tiled=True)
    return x


def gather_xh_z(x):
    x = lax.all_gather(x, "xh", axis=0, tiled=True)
    return lax.all_gather(x, "z", axis=0, tiled=True)


def ring_y(x):
    ny = 4
    right = [(i, (i + 1) % ny) for i in range(ny)]
    left = [(i, (i - 1) % ny) for i in range(ny)]
    from_minus = lax.ppermute(x, "y", right)
    from_plus = lax.ppermute(x, "y", left)
    half = x.shape[0] // 2
    opp_a = lax.ppermute(from_minus[:half], "y", right)
    opp_b = lax.ppermute(from_plus[half:], "y", left)
    opposite = jnp.concatenate([opp_a, opp_b], axis=0)
    return jnp.stack([x, from_plus, opposite, from_minus])


def gather_mdl(x):
    mdl_index = lax.axis_index("mdl")
    n_mdl = lax.axis_size("mdl")
    other = lax.ppermute(x, "mdl", [(m, m ^ 1) for m in range(n_mdl)])
    pair = jnp.where(
        mdl_index % 2 == 0,
        jnp.concatenate([x, other], axis=1),
        jnp.concatenate([other, x], axis=1),
    )
    other = lax.ppermute(pair, "mdl", [(m, m ^ 2) for m in range(n_mdl)])
    return jnp.where(
        mdl_index // 2 == 0,
        jnp.concatenate([pair, other], axis=1),
        jnp.concatenate([other, pair], axis=1),
    )


def body(
    tokens,
    norm_gain,
    w_query,
    key_matrix,
    value_matrix,
    w_gate,
    q_gain,
    k_gain,
    w_out,
    prompt_lengths,
    segment_ids,
    tenant_ranges,
    key_mask,
    cache_slot,
):
    local_rows = tokens.shape[0]
    weight_rows = w_query.shape[0]
    q_cols = w_query.shape[1]
    kv_cols = key_matrix.shape[1]
    g_cols = w_gate.shape[1]
    seq_size = lax.axis_size(SEQ_PARTS)
    stream = local_rows * seq_size
    request_count = prompt_lengths.shape[0]

    mask_cols = local_rows // weight_rows
    mask_block = key_mask.astype(jnp.bfloat16).reshape(weight_rows, mask_cols)
    mask_block = jnp.pad(mask_block, ((0, 0), (0, 128 - mask_cols)))
    packed = jnp.concatenate([w_query, key_matrix, value_matrix, w_out.T, mask_block], axis=1)
    packed = lax.all_gather(packed, "xh", axis=0, tiled=True)
    packed = lax.all_gather(packed, "y", axis=0, tiled=True)
    packed, gate_in = lax.optimization_barrier((packed, w_gate))
    gate_ring = ring_y_kernel(gather_xh_z(gate_in), 1)
    gathered = lax.all_gather(packed, "z", axis=0, tiled=True)
    gathered, gate_ring = lax.optimization_barrier((gathered, gate_ring))
    proj_cols = q_cols + 2 * kv_cols
    w_proj = gathered[:, :proj_cols]
    w_out_t = gathered[:, proj_cols : proj_cols + w_out.shape[0]]
    all_mask = gathered[:, proj_cols + w_out.shape[0] : proj_cols + w_out.shape[0] + mask_cols]
    all_mask = all_mask.reshape(stream)
    w_gate_perm = gate_ring.reshape(-1, g_cols)

    wide_tokens = tokens.astype(jnp.float32)
    full_width = tokens.shape[1] * lax.axis_size("mdl")
    square_total = lax.psum(jnp.sum(wide_tokens * wide_tokens, axis=1), "mdl")
    scaled = (
        wide_tokens
        * lax.rsqrt(square_total / full_width + epsilon)[:, None]
        * norm_gain.astype(jnp.float32)
    )
    normalized_input = gather_mdl(scaled.astype(jnp.bfloat16))
    projected = jnp.dot(normalized_input, w_proj, preferred_element_type=jnp.float32)
    query_rows = projected[:, :q_cols]
    unprojected_keys = projected[:, q_cols : q_cols + kv_cols]
    values_raw = projected[:, q_cols + kv_cols : q_cols + 2 * kv_cols]
    my_y = lax.axis_index("y")
    input_perm = normalized_input.reshape(local_rows, 8, 4, 2, weight_rows)
    input_perm = jnp.roll(input_perm, -my_y, axis=2)
    input_perm = input_perm.transpose(0, 2, 1, 3, 4).reshape(local_rows, -1)
    gate_logits = jnp.dot(input_perm, w_gate_perm, preferred_element_type=jnp.float32)

    device_seq = lax.axis_index(SEQ_PARTS)
    token_ids = device_seq * local_rows + jnp.arange(local_rows, dtype=jnp.int32)
    starts = jnp.cumsum(prompt_lengths) - prompt_lengths
    ends = starts + prompt_lengths
    requests = jnp.arange(request_count, dtype=jnp.int32)
    member = (requests[:, None] > tenant_ranges[None, :, 0]) & (
        requests[:, None] < tenant_ranges[None, :, 1]
    )
    shared_of = jnp.sum(jnp.where(member, tenant_ranges[None, :, 0] + 3, 0), axis=1) - 3
    onehot = segment_ids[:, None] == requests[None, :]
    seg_start = jnp.sum(jnp.where(onehot, starts[None, :], 0), axis=1)
    shared_req = jnp.sum(jnp.where(onehot, shared_of[None, :], 0), axis=1)
    position = token_ids - seg_start

    query_heads = q_cols // HEAD_SIZE
    kv_heads = kv_cols // HEAD_SIZE
    group = query_heads // kv_heads
    q_rot = (
        rotate(head_norm(query_rows.reshape(local_rows, query_heads, HEAD_SIZE), q_gain), position)
        .astype(jnp.bfloat16)
        .reshape(local_rows, kv_heads, group, HEAD_SIZE)
    )
    k_rot = (
        rotate(head_norm(unprojected_keys.reshape(local_rows, kv_heads, HEAD_SIZE), k_gain), position)
        .astype(jnp.bfloat16)
        .reshape(local_rows, kv_cols)
    )
    values_flat = values_raw.astype(jnp.bfloat16)
    kv_pair = lax.all_gather(jnp.concatenate([k_rot, values_flat], axis=1), "xh", axis=0, tiled=True)
    v_part = lax.all_gather(kv_pair[:, kv_cols:], "z", axis=0, tiled=True)
    k_part = ring_y_kernel(kv_pair[:, :kv_cols], 2).reshape(-1, kv_cols)
    k_part, v_part = lax.optimization_barrier((k_part, v_part))
    k_all = lax.all_gather(k_part, "z", axis=0, tiled=True)
    v_ring = ring_y_kernel(v_part, 3).reshape(-1, kv_cols)

    def k_row_of(token):
        block = token // local_rows
        rel = (block // 2 % 4 - my_y) % 4
        place = ((block // 8) * 4 + rel) * 2 + block % 2
        return place * local_rows + token % local_rows

    def v_row_of(token):
        block = token // local_rows
        rel = (block // 2 % 4 - my_y) % 4
        place = (block // 8) * 2 + block % 2
        return (rel * 16 + place) * local_rows + token % local_rows

    n_blocks = stream // KEY_BLOCK
    block_ids = jnp.arange(n_blocks, dtype=jnp.int32)
    last_block = (device_seq * local_rows + local_rows - 1) // KEY_BLOCK
    first_block = jnp.min(seg_start) // KEY_BLOCK
    needed = (block_ids >= first_block) & (block_ids <= last_block)
    lo = tenant_ranges[:, 0]
    hi = tenant_ranges[:, 1]
    used = jnp.any(
        (segment_ids[:, None] > lo[None, :]) & (segment_ids[:, None] < hi[None, :]), axis=0
    )
    lo_start = jnp.sum(jnp.where(requests[None, :] == lo[:, None], starts[None, :], 0), axis=1)
    lo_end = jnp.sum(jnp.where(requests[None, :] == lo[:, None], ends[None, :], 0), axis=1)
    in_prompt = (
        used[:, None]
        & (block_ids[None, :] >= (lo_start // KEY_BLOCK)[:, None])
        & (block_ids[None, :] <= ((lo_end - 1) // KEY_BLOCK)[:, None])
    )
    needed = needed | jnp.any(in_prompt, axis=0)
    n_needed = jnp.sum(needed.astype(jnp.int32))
    (block_list,) = jnp.nonzero(needed, size=n_blocks, fill_value=0)
    block_list = block_list.astype(jnp.int32)

    row_segs = segment_ids
    row_shared = shared_req
    scale_factor = HEAD_SIZE ** (-0.5)
    head_shape = (local_rows, kv_heads, group)

    stream_ids = jnp.arange(stream, dtype=jnp.int32)
    key_segs = jnp.sum((stream_ids[:, None] >= ends[None, :]).astype(jnp.int32), axis=1)
    key_tags = jnp.where(all_mask == 1, key_segs, -2)

    def key_block(i, loop_state):
        old_top, old_totals, old_summed = loop_state
        block = block_list[i]
        offset = block * KEY_BLOCK
        keys_part = lax.dynamic_slice_in_dim(k_all, k_row_of(offset), KEY_BLOCK, 0).reshape(
            KEY_BLOCK, kv_heads, HEAD_SIZE
        )
        values_part = lax.dynamic_slice_in_dim(v_ring, v_row_of(offset), KEY_BLOCK, 0).reshape(
            KEY_BLOCK, kv_heads, HEAD_SIZE
        )
        tag_part = lax.dynamic_slice_in_dim(key_tags, offset, KEY_BLOCK, 0)
        columns = offset + jnp.arange(KEY_BLOCK, dtype=jnp.int32)
        own = tag_part[None, :] == row_segs[:, None]
        other = tag_part[None, :] == row_shared[:, None]
        earlier = columns[None, :] <= token_ids[:, None]
        diagonal = columns[None, :] == token_ids[:, None]
        visible = diagonal | (earlier & (own | other))
        allowed = visible[:, None, None, :]
        scores = (
            jnp.einsum("qhgd,khd->qhgk", q_rot, keys_part, preferred_element_type=jnp.float32)
            * scale_factor
        )
        scores = jnp.where(allowed, scores, masked_score)
        new_top = jnp.maximum(old_top, jnp.max(scores, axis=-1))
        factor = jnp.exp(old_top - new_top)
        raw_weights = jnp.where(allowed, jnp.exp(scores - new_top[..., None]), 0.0)
        new_totals = old_totals * factor + jnp.sum(raw_weights, axis=-1)
        new_summed = old_summed * factor[..., None] + jnp.einsum(
            "qhgk,khd->qhgd",
            raw_weights.astype(jnp.bfloat16),
            values_part,
            preferred_element_type=jnp.float32,
        )
        return (new_top, new_totals, new_summed)

    slots = block_list[:BATCH_BLOCKS]
    slot_live = jnp.arange(BATCH_BLOCKS, dtype=jnp.int32) < n_needed
    slot_offsets = slots * KEY_BLOCK
    keys_b = jnp.stack(
        [lax.dynamic_slice_in_dim(k_all, k_row_of(o), KEY_BLOCK, 0) for o in slot_offsets]
    ).reshape(BATCH_BLOCKS * KEY_BLOCK, kv_heads, HEAD_SIZE)
    values_b = jnp.stack(
        [lax.dynamic_slice_in_dim(v_ring, v_row_of(o), KEY_BLOCK, 0) for o in slot_offsets]
    ).reshape(BATCH_BLOCKS * KEY_BLOCK, kv_heads, HEAD_SIZE)
    tags_b = jnp.stack(
        [lax.dynamic_slice_in_dim(key_tags, o, KEY_BLOCK, 0) for o in slot_offsets]
    ).reshape(-1)
    columns_b = (slot_offsets[:, None] + jnp.arange(KEY_BLOCK, dtype=jnp.int32)[None, :]).reshape(-1)
    live_b = jnp.repeat(slot_live, KEY_BLOCK)
    visible_b = live_b[None, :] & (
        (columns_b[None, :] == token_ids[:, None])
        | (
            (columns_b[None, :] <= token_ids[:, None])
            & ((tags_b[None, :] == row_segs[:, None]) | (tags_b[None, :] == row_shared[:, None]))
        )
    )
    allowed_b = visible_b[:, None, None, :]
    scores_b = (
        jnp.einsum("qhgd,khd->qhgk", q_rot, keys_b, preferred_element_type=jnp.float32)
        * scale_factor
    )
    scores_b = jnp.where(allowed_b, scores_b, masked_score)
    top_b = jnp.max(scores_b, axis=-1)
    raw_b = jnp.where(allowed_b, jnp.exp(scores_b - top_b[..., None]), 0.0)
    totals_b = jnp.sum(raw_b, axis=-1)
    summed_b = jnp.einsum(
        "qhgk,khd->qhgd", raw_b.astype(jnp.bfloat16), values_b, preferred_element_type=jnp.float32
    )
    start_state = (top_b, totals_b, summed_b)
    top_now, totals, summed = lax.fori_loop(
        jnp.minimum(n_needed, BATCH_BLOCKS), n_needed, key_block, start_state
    )

    my_request = jnp.sum(jnp.where(cache_slot == device_seq, requests, 0))
    my_start = jnp.sum(jnp.where(requests == my_request, starts, 0))
    my_length = jnp.sum(jnp.where(requests == my_request, prompt_lengths, 0))
    offsets = jnp.arange(LMAX, dtype=jnp.int32)
    wanted = my_start + offsets
    in_window = ((wanted < stream) & (offsets < my_length))[:, None]
    zero = jnp.zeros((), jnp.bfloat16)
    first = my_start // KEY_BLOCK
    shift = my_start % KEY_BLOCK
    spans = [jnp.clip(first + j, 0, n_blocks - 1) * KEY_BLOCK for j in range(3)]

    def cache_of(table, row_of):
        pieces = [lax.dynamic_slice_in_dim(table, row_of(b), KEY_BLOCK, 0) for b in spans]
        window = lax.dynamic_slice_in_dim(jnp.concatenate(pieces, axis=0), shift, LMAX, 0)
        return jnp.where(in_window, window, zero)

    cache_k = cache_of(k_all, k_row_of)
    cache_v = cache_of(v_ring, v_row_of)

    attended = (summed / totals[..., None]).reshape(local_rows, query_heads * HEAD_SIZE)
    gated_heads = (attended * jax.nn.sigmoid(gate_logits)).astype(jnp.bfloat16)
    partial_out = lax.dot_general(
        gated_heads,
        w_out_t,
        (((1,), (1,)), ((), ())),
        preferred_element_type=jnp.float32,
    )
    mdl_index = lax.axis_index("mdl")
    n_mdl = lax.axis_size("mdl")
    x_lo = mdl_index // 2
    core = mdl_index % 2
    half = partial_out.shape[1] // 2
    quarter = half // 2
    mine = lax.dynamic_slice_in_dim(partial_out, x_lo * half, half, 1)
    theirs = lax.dynamic_slice_in_dim(partial_out, (1 - x_lo) * half, half, 1)
    across = lax.ppermute(
        theirs.astype(jnp.bfloat16), "mdl", [(m, m ^ 2) for m in range(n_mdl)]
    )
    half_sum = mine + across.astype(jnp.float32)
    mine = lax.dynamic_slice_in_dim(half_sum, core * quarter, quarter, 1)
    theirs = lax.dynamic_slice_in_dim(half_sum, (1 - core) * quarter, quarter, 1)
    branch_sum = mine + lax.ppermute(theirs, "mdl", [(m, m ^ 1) for m in range(n_mdl)])
    layer_out = (wide_tokens + branch_sum).astype(jnp.bfloat16)
    return (layer_out, cache_k[None], cache_v[None])


def solution(mesh):
    seq = SEQ_PARTS
    split = Mesh(mesh.devices.reshape(8, 4, 2, mesh.shape["mdl"]), SEQ_PARTS + ("mdl",))
    placed = (
        P(seq, "mdl"),
        P("mdl"),
        P(seq, "mdl"),
        P(seq, "mdl"),
        P(seq, "mdl"),
        P(seq, "mdl"),
        P(),
        P(),
        P("mdl", seq),
        P(),
        P(seq),
        P(),
        P(seq),
        P(),
    )
    return jax.shard_map(
        body,
        mesh=split,
        in_specs=placed,
        out_specs=(P(seq, "mdl"), P(seq, None, "mdl"), P(seq, None, "mdl")),
        check_vma=False,
    )
```

```python
import jax
import jax.numpy as jnp
from jax import lax
from jax.experimental import pallas as pl
from jax.experimental.pallas import tpu as pltpu
from jax.sharding import Mesh
from jax.sharding import PartitionSpec as P

HEAD_SIZE = 128
LMAX = 512
KEY_BLOCK = 256


epsilon = 1e-06
rope_base = 1000000.0
masked_score = -1e30


def head_norm(values, gain_vector):
    return (
        values
        * lax.rsqrt(jnp.mean(values * values, axis=-1, keepdims=True) + epsilon)
        * gain_vector
    )


def rotate(values, position):
    half_width = values.shape[-1] // 2
    frequency = rope_base ** (-2.0 * jnp.arange(half_width, dtype=jnp.float32) / values.shape[-1])
    angles = position.astype(jnp.float32)[:, None] * frequency[None, :]
    cosine = jnp.cos(angles)[:, None, :]
    sine_part = jnp.sin(angles)[:, None, :]
    former = values[..., :half_width]
    latter = values[..., half_width:]
    return jnp.concatenate(
        [former * cosine - latter * sine_part, latter * cosine + former * sine_part], axis=-1
    )


SEQ_PARTS = ("z", "y", "xh")
MESH_ID = pl.DeviceIdType.MESH
AXES = SEQ_PARTS + ("mdl",)


def _ring_kernel(x_ref, out_ref, send_sem, recv_sem, local_sem):
    ny = 4
    me = {name: lax.axis_index(name) for name in AXES}
    my_y = me["y"]

    def dev(yy):
        return tuple(yy if name == "y" else me[name] for name in AXES)

    plus = dev(lax.rem(my_y + 1, ny))
    minus = dev(lax.rem(my_y + ny - 1, ny))
    barrier = pltpu.get_barrier_semaphore()
    for d in (plus, minus):
        pl.semaphore_signal(barrier, inc=1, device_id=d, device_id_type=MESH_ID)
    pl.semaphore_wait(barrier, 2)

    rows = x_ref.shape[0]
    half = rows // 2
    to_minus = pltpu.make_async_remote_copy(
        src_ref=x_ref, dst_ref=out_ref.at[1], send_sem=send_sem.at[0], recv_sem=recv_sem.at[0],
        device_id=minus, device_id_type=MESH_ID)
    to_plus = pltpu.make_async_remote_copy(
        src_ref=x_ref, dst_ref=out_ref.at[3], send_sem=send_sem.at[1], recv_sem=recv_sem.at[1],
        device_id=plus, device_id_type=MESH_ID)
    own = pltpu.make_async_copy(x_ref, out_ref.at[0], local_sem.at[0])
    to_minus.start()
    to_plus.start()
    own.start()
    to_minus.wait_recv()
    on_minus = pltpu.make_async_remote_copy(
        src_ref=out_ref.at[1, pl.ds(0, half)], dst_ref=out_ref.at[2, pl.ds(0, half)],
        send_sem=send_sem.at[2], recv_sem=recv_sem.at[2], device_id=minus, device_id_type=MESH_ID)
    on_minus.start()
    to_plus.wait_recv()
    on_plus = pltpu.make_async_remote_copy(
        src_ref=out_ref.at[3, pl.ds(half, rows - half)], dst_ref=out_ref.at[2, pl.ds(half, rows - half)],
        send_sem=send_sem.at[3], recv_sem=recv_sem.at[3], device_id=plus, device_id_type=MESH_ID)
    on_plus.start()
    to_minus.wait_send()
    to_plus.wait_send()
    own.wait()
    on_minus.wait_send()
    on_plus.wait_send()
    on_minus.wait_recv()
    on_plus.wait_recv()


def ring_y_kernel(x, collective_id):
    rows, width = x.shape
    return pl.pallas_call(
        _ring_kernel,
        out_shape=jax.ShapeDtypeStruct((4, rows, width), x.dtype),
        in_specs=[pl.BlockSpec(memory_space=pl.ANY)],
        out_specs=pl.BlockSpec(memory_space=pl.ANY),
        scratch_shapes=[
            pltpu.SemaphoreType.DMA((4,)),
            pltpu.SemaphoreType.DMA((4,)),
            pltpu.SemaphoreType.DMA((1,)),
        ],
        compiler_params=pltpu.CompilerParams(collective_id=collective_id, has_side_effects=True),
    )(x)


def gather_seq(x):
    for name in reversed(SEQ_PARTS):
        x = lax.all_gather(x, name, axis=0, tiled=True)
    return x


def gather_xh_z(x):
    x = lax.all_gather(x, "xh", axis=0, tiled=True)
    return lax.all_gather(x, "z", axis=0, tiled=True)


def ring_y(x):
    ny = 4
    right = [(i, (i + 1) % ny) for i in range(ny)]
    left = [(i, (i - 1) % ny) for i in range(ny)]
    from_minus = lax.ppermute(x, "y", right)
    from_plus = lax.ppermute(x, "y", left)
    half = x.shape[0] // 2
    opp_a = lax.ppermute(from_minus[:half], "y", right)
    opp_b = lax.ppermute(from_plus[half:], "y", left)
    opposite = jnp.concatenate([opp_a, opp_b], axis=0)
    return jnp.stack([x, from_plus, opposite, from_minus])


def gather_mdl(x):
    mdl_index = lax.axis_index("mdl")
    n_mdl = lax.axis_size("mdl")
    other = lax.ppermute(x, "mdl", [(m, m ^ 1) for m in range(n_mdl)])
    pair = jnp.where(
        mdl_index % 2 == 0,
        jnp.concatenate([x, other], axis=1),
        jnp.concatenate([other, x], axis=1),
    )
    other = lax.ppermute(pair, "mdl", [(m, m ^ 2) for m in range(n_mdl)])
    return jnp.where(
        mdl_index // 2 == 0,
        jnp.concatenate([pair, other], axis=1),
        jnp.concatenate([other, pair], axis=1),
    )


def body(
    tokens,
    norm_gain,
    w_query,
    key_matrix,
    value_matrix,
    w_gate,
    q_gain,
    k_gain,
    w_out,
    prompt_lengths,
    segment_ids,
    tenant_ranges,
    key_mask,
    cache_slot,
):
    local_rows = tokens.shape[0]
    weight_rows = w_query.shape[0]
    q_cols = w_query.shape[1]
    kv_cols = key_matrix.shape[1]
    g_cols = w_gate.shape[1]
    seq_size = lax.axis_size(SEQ_PARTS)
    stream = local_rows * seq_size
    request_count = prompt_lengths.shape[0]

    mask_cols = local_rows // weight_rows
    mask_block = key_mask.astype(jnp.bfloat16).reshape(weight_rows, mask_cols)
    mask_block = jnp.pad(mask_block, ((0, 0), (0, 128 - mask_cols)))
    packed = jnp.concatenate([w_query, key_matrix, value_matrix, w_out.T, mask_block], axis=1)
    packed = lax.all_gather(packed, "xh", axis=0, tiled=True)
    packed = lax.all_gather(packed, "y", axis=0, tiled=True)
    packed, gate_in = lax.optimization_barrier((packed, w_gate))
    gate_ring = ring_y_kernel(gather_xh_z(gate_in), 1)
    gathered = lax.all_gather(packed, "z", axis=0, tiled=True)
    gathered, gate_ring = lax.optimization_barrier((gathered, gate_ring))
    proj_cols = q_cols + 2 * kv_cols
    w_proj = gathered[:, :proj_cols]
    w_out_t = gathered[:, proj_cols : proj_cols + w_out.shape[0]]
    all_mask = gathered[:, proj_cols + w_out.shape[0] : proj_cols + w_out.shape[0] + mask_cols]
    all_mask = all_mask.reshape(stream)
    w_gate_perm = gate_ring.reshape(-1, g_cols)

    wide_tokens = tokens.astype(jnp.float32)
    full_width = tokens.shape[1] * lax.axis_size("mdl")
    square_total = lax.psum(jnp.sum(wide_tokens * wide_tokens, axis=1), "mdl")
    scaled = (
        wide_tokens
        * lax.rsqrt(square_total / full_width + epsilon)[:, None]
        * norm_gain.astype(jnp.float32)
    )
    normalized_input = gather_mdl(scaled.astype(jnp.bfloat16))
    projected = jnp.dot(normalized_input, w_proj, preferred_element_type=jnp.float32)
    query_rows = projected[:, :q_cols]
    unprojected_keys = projected[:, q_cols : q_cols + kv_cols]
    values_raw = projected[:, q_cols + kv_cols : q_cols + 2 * kv_cols]
    my_y = lax.axis_index("y")
    input_perm = normalized_input.reshape(local_rows, 8, 4, 2, weight_rows)
    input_perm = jnp.roll(input_perm, -my_y, axis=2)
    input_perm = input_perm.transpose(0, 2, 1, 3, 4).reshape(local_rows, -1)
    gate_logits = jnp.dot(input_perm, w_gate_perm, preferred_element_type=jnp.float32)

    device_seq = lax.axis_index(SEQ_PARTS)
    token_ids = device_seq * local_rows + jnp.arange(local_rows, dtype=jnp.int32)
    starts = jnp.cumsum(prompt_lengths) - prompt_lengths
    ends = starts + prompt_lengths
    requests = jnp.arange(request_count, dtype=jnp.int32)
    member = (requests[:, None] > tenant_ranges[None, :, 0]) & (
        requests[:, None] < tenant_ranges[None, :, 1]
    )
    shared_of = jnp.sum(jnp.where(member, tenant_ranges[None, :, 0] + 3, 0), axis=1) - 3
    onehot = segment_ids[:, None] == requests[None, :]
    seg_start = jnp.sum(jnp.where(onehot, starts[None, :], 0), axis=1)
    shared_req = jnp.sum(jnp.where(onehot, shared_of[None, :], 0), axis=1)
    position = token_ids - seg_start

    query_heads = q_cols // HEAD_SIZE
    kv_heads = kv_cols // HEAD_SIZE
    group = query_heads // kv_heads
    q_rot = (
        rotate(head_norm(query_rows.reshape(local_rows, query_heads, HEAD_SIZE), q_gain), position)
        .astype(jnp.bfloat16)
        .reshape(local_rows, kv_heads, group, HEAD_SIZE)
    )
    k_rot = (
        rotate(head_norm(unprojected_keys.reshape(local_rows, kv_heads, HEAD_SIZE), k_gain), position)
        .astype(jnp.bfloat16)
        .reshape(local_rows, kv_cols)
    )
    values_flat = values_raw.astype(jnp.bfloat16)
    kv_pair = lax.all_gather(jnp.concatenate([k_rot, values_flat], axis=1), "xh", axis=0, tiled=True)
    v_part = lax.all_gather(kv_pair[:, kv_cols:], "z", axis=0, tiled=True)
    k_part = ring_y_kernel(kv_pair[:, :kv_cols], 2).reshape(-1, kv_cols)
    k_part, v_part = lax.optimization_barrier((k_part, v_part))
    k_all = lax.all_gather(k_part, "z", axis=0, tiled=True)
    v_ring = ring_y_kernel(v_part, 3).reshape(-1, kv_cols)

    def k_row_of(token):
        block = token // local_rows
        rel = (block // 2 % 4 - my_y) % 4
        place = ((block // 8) * 4 + rel) * 2 + block % 2
        return place * local_rows + token % local_rows

    def v_row_of(token):
        block = token // local_rows
        rel = (block // 2 % 4 - my_y) % 4
        place = (block // 8) * 2 + block % 2
        return (rel * 16 + place) * local_rows + token % local_rows

    n_blocks = stream // KEY_BLOCK
    block_ids = jnp.arange(n_blocks, dtype=jnp.int32)
    last_block = (device_seq * local_rows + local_rows - 1) // KEY_BLOCK
    first_block = jnp.min(seg_start) // KEY_BLOCK
    needed = (block_ids >= first_block) & (block_ids <= last_block)
    lo = tenant_ranges[:, 0]
    hi = tenant_ranges[:, 1]
    used = jnp.any(
        (segment_ids[:, None] > lo[None, :]) & (segment_ids[:, None] < hi[None, :]), axis=0
    )
    lo_start = jnp.sum(jnp.where(requests[None, :] == lo[:, None], starts[None, :], 0), axis=1)
    lo_end = jnp.sum(jnp.where(requests[None, :] == lo[:, None], ends[None, :], 0), axis=1)
    in_prompt = (
        used[:, None]
        & (block_ids[None, :] >= (lo_start // KEY_BLOCK)[:, None])
        & (block_ids[None, :] <= ((lo_end - 1) // KEY_BLOCK)[:, None])
    )
    needed = needed | jnp.any(in_prompt, axis=0)
    n_needed = jnp.sum(needed.astype(jnp.int32))
    (block_list,) = jnp.nonzero(needed, size=n_blocks, fill_value=0)
    block_list = block_list.astype(jnp.int32)

    row_segs = segment_ids
    row_shared = shared_req
    scale_factor = HEAD_SIZE ** (-0.5)
    head_shape = (local_rows, kv_heads, group)

    stream_ids = jnp.arange(stream, dtype=jnp.int32)
    key_segs = jnp.sum((stream_ids[:, None] >= ends[None, :]).astype(jnp.int32), axis=1)
    key_tags = jnp.where(all_mask == 1, key_segs, -2)

    def key_block(i, loop_state):
        old_top, old_totals, old_summed = loop_state
        block = block_list[i]
        offset = block * KEY_BLOCK
        keys_part = lax.dynamic_slice_in_dim(k_all, k_row_of(offset), KEY_BLOCK, 0).reshape(
            KEY_BLOCK, kv_heads, HEAD_SIZE
        )
        values_part = lax.dynamic_slice_in_dim(v_ring, v_row_of(offset), KEY_BLOCK, 0).reshape(
            KEY_BLOCK, kv_heads, HEAD_SIZE
        )
        tag_part = lax.dynamic_slice_in_dim(key_tags, offset, KEY_BLOCK, 0)
        columns = offset + jnp.arange(KEY_BLOCK, dtype=jnp.int32)
        own = tag_part[None, :] == row_segs[:, None]
        other = tag_part[None, :] == row_shared[:, None]
        earlier = columns[None, :] <= token_ids[:, None]
        diagonal = columns[None, :] == token_ids[:, None]
        visible = diagonal | (earlier & (own | other))
        allowed = visible[:, None, None, :]
        scores = (
            jnp.einsum("qhgd,khd->qhgk", q_rot, keys_part, preferred_element_type=jnp.float32)
            * scale_factor
        )
        scores = jnp.where(allowed, scores, masked_score)
        new_top = jnp.maximum(old_top, jnp.max(scores, axis=-1))
        factor = jnp.exp(old_top - new_top)
        raw_weights = jnp.where(allowed, jnp.exp(scores - new_top[..., None]), 0.0)
        new_totals = old_totals * factor + jnp.sum(raw_weights, axis=-1)
        new_summed = old_summed * factor[..., None] + jnp.einsum(
            "qhgk,khd->qhgd",
            raw_weights.astype(jnp.bfloat16),
            values_part,
            preferred_element_type=jnp.float32,
        )
        return (new_top, new_totals, new_summed)

    start_state = (
        jnp.full(head_shape, masked_score, jnp.float32),
        jnp.zeros(head_shape, jnp.float32),
        jnp.zeros(head_shape + (HEAD_SIZE,), jnp.float32),
    )
    top_now, totals, summed = lax.fori_loop(0, n_needed, key_block, start_state)

    my_request = jnp.sum(jnp.where(cache_slot == device_seq, requests, 0))
    my_start = jnp.sum(jnp.where(requests == my_request, starts, 0))
    my_length = jnp.sum(jnp.where(requests == my_request, prompt_lengths, 0))
    offsets = jnp.arange(LMAX, dtype=jnp.int32)
    wanted = my_start + offsets
    in_window = ((wanted < stream) & (offsets < my_length))[:, None]
    zero = jnp.zeros((), jnp.bfloat16)
    first = my_start // KEY_BLOCK
    shift = my_start % KEY_BLOCK
    spans = [jnp.clip(first + j, 0, n_blocks - 1) * KEY_BLOCK for j in range(3)]

    def cache_of(table, row_of):
        pieces = [lax.dynamic_slice_in_dim(table, row_of(b), KEY_BLOCK, 0) for b in spans]
        window = lax.dynamic_slice_in_dim(jnp.concatenate(pieces, axis=0), shift, LMAX, 0)
        return jnp.where(in_window, window, zero)

    cache_k = cache_of(k_all, k_row_of)
    cache_v = cache_of(v_ring, v_row_of)

    attended = (summed / totals[..., None]).reshape(local_rows, query_heads * HEAD_SIZE)
    gated_heads = (attended * jax.nn.sigmoid(gate_logits)).astype(jnp.bfloat16)
    partial_out = lax.dot_general(
        gated_heads,
        w_out_t,
        (((1,), (1,)), ((), ())),
        preferred_element_type=jnp.float32,
    )
    mdl_index = lax.axis_index("mdl")
    n_mdl = lax.axis_size("mdl")
    x_lo = mdl_index // 2
    core = mdl_index % 2
    quarter = partial_out.shape[1] // 4

    def cols_of(block):
        return lax.dynamic_slice_in_dim(partial_out, block * quarter, quarter, 1)

    mine = jnp.concatenate([cols_of(core), cols_of(2 + core)], axis=1)
    theirs = jnp.concatenate([cols_of(1 - core), cols_of(3 - core)], axis=1)
    pair_sum = mine + lax.ppermute(theirs, "mdl", [(m, m ^ 1) for m in range(n_mdl)])
    mine = lax.dynamic_slice_in_dim(pair_sum, x_lo * quarter, quarter, 1)
    theirs = lax.dynamic_slice_in_dim(pair_sum, (1 - x_lo) * quarter, quarter, 1)
    across = lax.ppermute(
        theirs.astype(jnp.bfloat16), "mdl", [(m, m ^ 2) for m in range(n_mdl)]
    )
    branch_sum = mine + across.astype(jnp.float32)
    layer_out = (wide_tokens + branch_sum).astype(jnp.bfloat16)
    return (layer_out, cache_k[None], cache_v[None])


def solution(mesh):
    seq = SEQ_PARTS
    split = Mesh(mesh.devices.reshape(8, 4, 2, mesh.shape["mdl"]), SEQ_PARTS + ("mdl",))
    placed = (
        P(seq, "mdl"),
        P("mdl"),
        P(seq, "mdl"),
        P(seq, "mdl"),
        P(seq, "mdl"),
        P(seq, "mdl"),
        P(),
        P(),
        P("mdl", seq),
        P(),
        P(seq),
        P(),
        P(seq),
        P(),
    )
    return jax.shard_map(
        body,
        mesh=split,
        in_specs=placed,
        out_specs=(P(seq, "mdl"), P(seq, None, "mdl"), P(seq, None, "mdl")),
        check_vma=False,
    )
```

```python
import jax
import jax.numpy as jnp
from jax import lax
from jax.experimental import pallas as pl
from jax.experimental.pallas import tpu as pltpu
from jax.sharding import Mesh
from jax.sharding import PartitionSpec as P

HEAD_SIZE = 128
LMAX = 512
KEY_BLOCK = 256


epsilon = 1e-06
rope_base = 1000000.0
masked_score = -1e30


def head_norm(values, gain_vector):
    return (
        values
        * lax.rsqrt(jnp.mean(values * values, axis=-1, keepdims=True) + epsilon)
        * gain_vector
    )


def rotate(values, position):
    half_width = values.shape[-1] // 2
    frequency = rope_base ** (-2.0 * jnp.arange(half_width, dtype=jnp.float32) / values.shape[-1])
    angles = position.astype(jnp.float32)[:, None] * frequency[None, :]
    cosine = jnp.cos(angles)[:, None, :]
    sine_part = jnp.sin(angles)[:, None, :]
    former = values[..., :half_width]
    latter = values[..., half_width:]
    return jnp.concatenate(
        [former * cosine - latter * sine_part, latter * cosine + former * sine_part], axis=-1
    )


SEQ_PARTS = ("z", "y", "xh")
MESH_ID = pl.DeviceIdType.MESH
AXES = SEQ_PARTS + ("mdl",)


def _ring_kernel(x_ref, out_ref, send_sem, recv_sem, local_sem):
    ny = 4
    me = {name: lax.axis_index(name) for name in AXES}
    my_y = me["y"]

    def dev(yy):
        return tuple(yy if name == "y" else me[name] for name in AXES)

    plus = dev(lax.rem(my_y + 1, ny))
    minus = dev(lax.rem(my_y + ny - 1, ny))
    barrier = pltpu.get_barrier_semaphore()
    for d in (plus, minus):
        pl.semaphore_signal(barrier, inc=1, device_id=d, device_id_type=MESH_ID)
    pl.semaphore_wait(barrier, 2)

    rows = x_ref.shape[0]
    half = rows // 2
    to_minus = pltpu.make_async_remote_copy(
        src_ref=x_ref, dst_ref=out_ref.at[1], send_sem=send_sem.at[0], recv_sem=recv_sem.at[0],
        device_id=minus, device_id_type=MESH_ID)
    to_plus = pltpu.make_async_remote_copy(
        src_ref=x_ref, dst_ref=out_ref.at[3], send_sem=send_sem.at[1], recv_sem=recv_sem.at[1],
        device_id=plus, device_id_type=MESH_ID)
    own = pltpu.make_async_copy(x_ref, out_ref.at[0], local_sem.at[0])
    to_minus.start()
    to_plus.start()
    own.start()
    to_minus.wait_recv()
    on_minus = pltpu.make_async_remote_copy(
        src_ref=out_ref.at[1, pl.ds(0, half)], dst_ref=out_ref.at[2, pl.ds(0, half)],
        send_sem=send_sem.at[2], recv_sem=recv_sem.at[2], device_id=minus, device_id_type=MESH_ID)
    on_minus.start()
    to_plus.wait_recv()
    on_plus = pltpu.make_async_remote_copy(
        src_ref=out_ref.at[3, pl.ds(half, rows - half)], dst_ref=out_ref.at[2, pl.ds(half, rows - half)],
        send_sem=send_sem.at[3], recv_sem=recv_sem.at[3], device_id=plus, device_id_type=MESH_ID)
    on_plus.start()
    to_minus.wait_send()
    to_plus.wait_send()
    own.wait()
    on_minus.wait_send()
    on_plus.wait_send()
    on_minus.wait_recv()
    on_plus.wait_recv()


def ring_y_kernel(x, collective_id):
    rows, width = x.shape
    return pl.pallas_call(
        _ring_kernel,
        out_shape=jax.ShapeDtypeStruct((4, rows, width), x.dtype),
        in_specs=[pl.BlockSpec(memory_space=pl.ANY)],
        out_specs=pl.BlockSpec(memory_space=pl.ANY),
        scratch_shapes=[
            pltpu.SemaphoreType.DMA((4,)),
            pltpu.SemaphoreType.DMA((4,)),
            pltpu.SemaphoreType.DMA((1,)),
        ],
        compiler_params=pltpu.CompilerParams(collective_id=collective_id, has_side_effects=True),
    )(x)


def gather_seq(x):
    for name in reversed(SEQ_PARTS):
        x = lax.all_gather(x, name, axis=0, tiled=True)
    return x


def gather_xh_z(x):
    x = lax.all_gather(x, "xh", axis=0, tiled=True)
    return lax.all_gather(x, "z", axis=0, tiled=True)


def ring_y(x):
    ny = 4
    right = [(i, (i + 1) % ny) for i in range(ny)]
    left = [(i, (i - 1) % ny) for i in range(ny)]
    from_minus = lax.ppermute(x, "y", right)
    from_plus = lax.ppermute(x, "y", left)
    half = x.shape[0] // 2
    opp_a = lax.ppermute(from_minus[:half], "y", right)
    opp_b = lax.ppermute(from_plus[half:], "y", left)
    opposite = jnp.concatenate([opp_a, opp_b], axis=0)
    return jnp.stack([x, from_plus, opposite, from_minus])


def gather_mdl(x):
    mdl_index = lax.axis_index("mdl")
    n_mdl = lax.axis_size("mdl")
    other = lax.ppermute(x, "mdl", [(m, m ^ 1) for m in range(n_mdl)])
    pair = jnp.where(
        mdl_index % 2 == 0,
        jnp.concatenate([x, other], axis=1),
        jnp.concatenate([other, x], axis=1),
    )
    other = lax.ppermute(pair, "mdl", [(m, m ^ 2) for m in range(n_mdl)])
    return jnp.where(
        mdl_index // 2 == 0,
        jnp.concatenate([pair, other], axis=1),
        jnp.concatenate([other, pair], axis=1),
    )


def body(
    tokens,
    norm_gain,
    w_query,
    key_matrix,
    value_matrix,
    w_gate,
    q_gain,
    k_gain,
    w_out,
    prompt_lengths,
    segment_ids,
    tenant_ranges,
    key_mask,
    cache_slot,
):
    local_rows = tokens.shape[0]
    weight_rows = w_query.shape[0]
    q_cols = w_query.shape[1]
    kv_cols = key_matrix.shape[1]
    g_cols = w_gate.shape[1]
    seq_size = lax.axis_size(SEQ_PARTS)
    stream = local_rows * seq_size
    request_count = prompt_lengths.shape[0]

    mask_cols = local_rows // weight_rows
    mask_block = key_mask.astype(jnp.bfloat16).reshape(weight_rows, mask_cols)
    mask_block = jnp.pad(mask_block, ((0, 0), (0, 128 - mask_cols)))
    packed = jnp.concatenate([w_query, key_matrix, value_matrix, w_out.T, mask_block], axis=1)
    packed = lax.all_gather(packed, "xh", axis=0, tiled=True)
    packed = lax.all_gather(packed, "y", axis=0, tiled=True)
    packed, gate_in = lax.optimization_barrier((packed, w_gate))
    gate_ring = ring_y_kernel(gather_xh_z(gate_in), 1)
    gathered = lax.all_gather(packed, "z", axis=0, tiled=True)
    gathered, gate_ring = lax.optimization_barrier((gathered, gate_ring))
    proj_cols = q_cols + 2 * kv_cols
    w_proj = gathered[:, :proj_cols]
    w_out_t = gathered[:, proj_cols : proj_cols + w_out.shape[0]]
    all_mask = gathered[:, proj_cols + w_out.shape[0] : proj_cols + w_out.shape[0] + mask_cols]
    all_mask = all_mask.reshape(stream)
    w_gate_perm = gate_ring.reshape(-1, g_cols)

    wide_tokens = tokens.astype(jnp.float32)
    full_width = tokens.shape[1] * lax.axis_size("mdl")
    square_part = jnp.sum(wide_tokens * wide_tokens, axis=1)
    n_mdl_in = lax.axis_size("mdl")
    square_part = square_part + lax.ppermute(
        square_part, "mdl", [(m, m ^ 1) for m in range(n_mdl_in)]
    )
    square_total = square_part + lax.ppermute(
        square_part, "mdl", [(m, m ^ 2) for m in range(n_mdl_in)]
    )
    scaled = (
        wide_tokens
        * lax.rsqrt(square_total / full_width + epsilon)[:, None]
        * norm_gain.astype(jnp.float32)
    )
    normalized_input = gather_mdl(scaled.astype(jnp.bfloat16))
    projected = jnp.dot(normalized_input, w_proj, preferred_element_type=jnp.float32)
    query_rows = projected[:, :q_cols]
    unprojected_keys = projected[:, q_cols : q_cols + kv_cols]
    values_raw = projected[:, q_cols + kv_cols : q_cols + 2 * kv_cols]
    my_y = lax.axis_index("y")
    input_perm = normalized_input.reshape(local_rows, 8, 4, 2, weight_rows)
    input_perm = jnp.roll(input_perm, -my_y, axis=2)
    input_perm = input_perm.transpose(0, 2, 1, 3, 4).reshape(local_rows, -1)
    gate_logits = jnp.dot(input_perm, w_gate_perm, preferred_element_type=jnp.float32)

    device_seq = lax.axis_index(SEQ_PARTS)
    token_ids = device_seq * local_rows + jnp.arange(local_rows, dtype=jnp.int32)
    starts = jnp.cumsum(prompt_lengths) - prompt_lengths
    ends = starts + prompt_lengths
    requests = jnp.arange(request_count, dtype=jnp.int32)
    member = (requests[:, None] > tenant_ranges[None, :, 0]) & (
        requests[:, None] < tenant_ranges[None, :, 1]
    )
    shared_of = jnp.sum(jnp.where(member, tenant_ranges[None, :, 0] + 3, 0), axis=1) - 3
    onehot = segment_ids[:, None] == requests[None, :]
    seg_start = jnp.sum(jnp.where(onehot, starts[None, :], 0), axis=1)
    shared_req = jnp.sum(jnp.where(onehot, shared_of[None, :], 0), axis=1)
    position = token_ids - seg_start

    query_heads = q_cols // HEAD_SIZE
    kv_heads = kv_cols // HEAD_SIZE
    group = query_heads // kv_heads
    q_rot = (
        rotate(head_norm(query_rows.reshape(local_rows, query_heads, HEAD_SIZE), q_gain), position)
        .astype(jnp.bfloat16)
        .reshape(local_rows, kv_heads, group, HEAD_SIZE)
    )
    k_rot = (
        rotate(head_norm(unprojected_keys.reshape(local_rows, kv_heads, HEAD_SIZE), k_gain), position)
        .astype(jnp.bfloat16)
        .reshape(local_rows, kv_cols)
    )
    values_flat = values_raw.astype(jnp.bfloat16)
    kv_pair = lax.all_gather(jnp.concatenate([k_rot, values_flat], axis=1), "xh", axis=0, tiled=True)
    v_part = lax.all_gather(kv_pair[:, kv_cols:], "z", axis=0, tiled=True)
    k_part = ring_y_kernel(kv_pair[:, :kv_cols], 2).reshape(-1, kv_cols)
    k_part, v_part = lax.optimization_barrier((k_part, v_part))
    k_all = lax.all_gather(k_part, "z", axis=0, tiled=True)
    v_ring = ring_y_kernel(v_part, 3).reshape(-1, kv_cols)

    def k_row_of(token):
        block = token // local_rows
        rel = (block // 2 % 4 - my_y) % 4
        place = ((block // 8) * 4 + rel) * 2 + block % 2
        return place * local_rows + token % local_rows

    def v_row_of(token):
        block = token // local_rows
        rel = (block // 2 % 4 - my_y) % 4
        place = (block // 8) * 2 + block % 2
        return (rel * 16 + place) * local_rows + token % local_rows

    n_blocks = stream // KEY_BLOCK
    block_ids = jnp.arange(n_blocks, dtype=jnp.int32)
    last_block = (device_seq * local_rows + local_rows - 1) // KEY_BLOCK
    first_block = jnp.min(seg_start) // KEY_BLOCK
    needed = (block_ids >= first_block) & (block_ids <= last_block)
    lo = tenant_ranges[:, 0]
    hi = tenant_ranges[:, 1]
    used = jnp.any(
        (segment_ids[:, None] > lo[None, :]) & (segment_ids[:, None] < hi[None, :]), axis=0
    )
    lo_start = jnp.sum(jnp.where(requests[None, :] == lo[:, None], starts[None, :], 0), axis=1)
    lo_end = jnp.sum(jnp.where(requests[None, :] == lo[:, None], ends[None, :], 0), axis=1)
    in_prompt = (
        used[:, None]
        & (block_ids[None, :] >= (lo_start // KEY_BLOCK)[:, None])
        & (block_ids[None, :] <= ((lo_end - 1) // KEY_BLOCK)[:, None])
    )
    needed = needed | jnp.any(in_prompt, axis=0)
    n_needed = jnp.sum(needed.astype(jnp.int32))
    (block_list,) = jnp.nonzero(needed, size=n_blocks, fill_value=0)
    block_list = block_list.astype(jnp.int32)

    row_segs = segment_ids
    row_shared = shared_req
    scale_factor = HEAD_SIZE ** (-0.5)
    head_shape = (local_rows, kv_heads, group)

    stream_ids = jnp.arange(stream, dtype=jnp.int32)
    key_segs = jnp.sum((stream_ids[:, None] >= ends[None, :]).astype(jnp.int32), axis=1)
    key_tags = jnp.where(all_mask == 1, key_segs, -2)

    def key_block(i, loop_state):
        old_top, old_totals, old_summed = loop_state
        block = block_list[i]
        offset = block * KEY_BLOCK
        keys_part = lax.dynamic_slice_in_dim(k_all, k_row_of(offset), KEY_BLOCK, 0).reshape(
            KEY_BLOCK, kv_heads, HEAD_SIZE
        )
        values_part = lax.dynamic_slice_in_dim(v_ring, v_row_of(offset), KEY_BLOCK, 0).reshape(
            KEY_BLOCK, kv_heads, HEAD_SIZE
        )
        tag_part = lax.dynamic_slice_in_dim(key_tags, offset, KEY_BLOCK, 0)
        columns = offset + jnp.arange(KEY_BLOCK, dtype=jnp.int32)
        own = tag_part[None, :] == row_segs[:, None]
        other = tag_part[None, :] == row_shared[:, None]
        earlier = columns[None, :] <= token_ids[:, None]
        diagonal = columns[None, :] == token_ids[:, None]
        visible = diagonal | (earlier & (own | other))
        allowed = visible[:, None, None, :]
        scores = (
            jnp.einsum("qhgd,khd->qhgk", q_rot, keys_part, preferred_element_type=jnp.float32)
            * scale_factor
        )
        scores = jnp.where(allowed, scores, masked_score)
        new_top = jnp.maximum(old_top, jnp.max(scores, axis=-1))
        factor = jnp.exp(old_top - new_top)
        raw_weights = jnp.where(allowed, jnp.exp(scores - new_top[..., None]), 0.0)
        new_totals = old_totals * factor + jnp.sum(raw_weights, axis=-1)
        new_summed = old_summed * factor[..., None] + jnp.einsum(
            "qhgk,khd->qhgd",
            raw_weights.astype(jnp.bfloat16),
            values_part,
            preferred_element_type=jnp.float32,
        )
        return (new_top, new_totals, new_summed)

    start_state = (
        jnp.full(head_shape, masked_score, jnp.float32),
        jnp.zeros(head_shape, jnp.float32),
        jnp.zeros(head_shape + (HEAD_SIZE,), jnp.float32),
    )
    top_now, totals, summed = lax.fori_loop(0, n_needed, key_block, start_state)

    my_request = jnp.sum(jnp.where(cache_slot == device_seq, requests, 0))
    my_start = jnp.sum(jnp.where(requests == my_request, starts, 0))
    my_length = jnp.sum(jnp.where(requests == my_request, prompt_lengths, 0))
    offsets = jnp.arange(LMAX, dtype=jnp.int32)
    wanted = my_start + offsets
    in_window = ((wanted < stream) & (offsets < my_length))[:, None]
    zero = jnp.zeros((), jnp.bfloat16)
    first = my_start // KEY_BLOCK
    shift = my_start % KEY_BLOCK
    spans = [jnp.clip(first + j, 0, n_blocks - 1) * KEY_BLOCK for j in range(3)]

    def cache_of(table, row_of):
        pieces = [lax.dynamic_slice_in_dim(table, row_of(b), KEY_BLOCK, 0) for b in spans]
        window = lax.dynamic_slice_in_dim(jnp.concatenate(pieces, axis=0), shift, LMAX, 0)
        return jnp.where(in_window, window, zero)

    cache_k = cache_of(k_all, k_row_of)
    cache_v = cache_of(v_ring, v_row_of)

    attended = (summed / totals[..., None]).reshape(local_rows, query_heads * HEAD_SIZE)
    gated_heads = (attended * jax.nn.sigmoid(gate_logits)).astype(jnp.bfloat16)
    partial_out = lax.dot_general(
        gated_heads,
        w_out_t,
        (((1,), (1,)), ((), ())),
        preferred_element_type=jnp.float32,
    )
    mdl_index = lax.axis_index("mdl")
    n_mdl = lax.axis_size("mdl")
    x_lo = mdl_index // 2
    core = mdl_index % 2
    quarter = partial_out.shape[1] // 4

    def cols_of(block):
        return lax.dynamic_slice_in_dim(partial_out, block * quarter, quarter, 1)

    mine = jnp.concatenate([cols_of(core), cols_of(2 + core)], axis=1)
    theirs = jnp.concatenate([cols_of(1 - core), cols_of(3 - core)], axis=1)
    pair_sum = mine + lax.ppermute(theirs, "mdl", [(m, m ^ 1) for m in range(n_mdl)])
    mine = lax.dynamic_slice_in_dim(pair_sum, x_lo * quarter, quarter, 1)
    theirs = lax.dynamic_slice_in_dim(pair_sum, (1 - x_lo) * quarter, quarter, 1)
    across = lax.ppermute(
        theirs.astype(jnp.bfloat16), "mdl", [(m, m ^ 2) for m in range(n_mdl)]
    )
    branch_sum = mine + across.astype(jnp.float32)
    layer_out = (wide_tokens + branch_sum).astype(jnp.bfloat16)
    return (layer_out, cache_k[None], cache_v[None])


def solution(mesh):
    seq = SEQ_PARTS
    split = Mesh(mesh.devices.reshape(8, 4, 2, mesh.shape["mdl"]), SEQ_PARTS + ("mdl",))
    placed = (
        P(seq, "mdl"),
        P("mdl"),
        P(seq, "mdl"),
        P(seq, "mdl"),
        P(seq, "mdl"),
        P(seq, "mdl"),
        P(),
        P(),
        P("mdl", seq),
        P(),
        P(seq),
        P(),
        P(seq),
        P(),
    )
    return jax.shard_map(
        body,
        mesh=split,
        in_specs=placed,
        out_specs=(P(seq, "mdl"), P(seq, None, "mdl"), P(seq, None, "mdl")),
        check_vma=False,
    )
```

```python
import jax
import jax.numpy as jnp
from jax import lax
from jax.experimental import pallas as pl
from jax.experimental.pallas import tpu as pltpu
from jax.sharding import Mesh
from jax.sharding import PartitionSpec as P

HEAD_SIZE = 128
LMAX = 512
KEY_BLOCK = 256


epsilon = 1e-06
rope_base = 1000000.0
masked_score = -1e30


def head_norm(values, gain_vector):
    return (
        values
        * lax.rsqrt(jnp.mean(values * values, axis=-1, keepdims=True) + epsilon)
        * gain_vector
    )


def rotate(values, position):
    half_width = values.shape[-1] // 2
    frequency = rope_base ** (-2.0 * jnp.arange(half_width, dtype=jnp.float32) / values.shape[-1])
    angles = position.astype(jnp.float32)[:, None] * frequency[None, :]
    cosine = jnp.cos(angles)[:, None, :]
    sine_part = jnp.sin(angles)[:, None, :]
    former = values[..., :half_width]
    latter = values[..., half_width:]
    return jnp.concatenate(
        [former * cosine - latter * sine_part, latter * cosine + former * sine_part], axis=-1
    )


SEQ_PARTS = ("z", "y", "xh")
MESH_ID = pl.DeviceIdType.MESH
AXES = SEQ_PARTS + ("mdl",)


def _ring_kernel(x_ref, out_ref, send_sem, recv_sem, local_sem):
    ny = 4
    me = {name: lax.axis_index(name) for name in AXES}
    my_y = me["y"]

    def dev(yy):
        return tuple(yy if name == "y" else me[name] for name in AXES)

    plus = dev(lax.rem(my_y + 1, ny))
    minus = dev(lax.rem(my_y + ny - 1, ny))
    barrier = pltpu.get_barrier_semaphore()
    for d in (plus, minus):
        pl.semaphore_signal(barrier, inc=1, device_id=d, device_id_type=MESH_ID)
    pl.semaphore_wait(barrier, 2)

    rows = x_ref.shape[0]
    half = rows // 2
    to_minus = pltpu.make_async_remote_copy(
        src_ref=x_ref, dst_ref=out_ref.at[1], send_sem=send_sem.at[0], recv_sem=recv_sem.at[0],
        device_id=minus, device_id_type=MESH_ID)
    to_plus = pltpu.make_async_remote_copy(
        src_ref=x_ref, dst_ref=out_ref.at[3], send_sem=send_sem.at[1], recv_sem=recv_sem.at[1],
        device_id=plus, device_id_type=MESH_ID)
    own = pltpu.make_async_copy(x_ref, out_ref.at[0], local_sem.at[0])
    to_minus.start()
    to_plus.start()
    own.start()
    to_minus.wait_recv()
    on_minus = pltpu.make_async_remote_copy(
        src_ref=out_ref.at[1, pl.ds(0, half)], dst_ref=out_ref.at[2, pl.ds(0, half)],
        send_sem=send_sem.at[2], recv_sem=recv_sem.at[2], device_id=minus, device_id_type=MESH_ID)
    on_minus.start()
    to_plus.wait_recv()
    on_plus = pltpu.make_async_remote_copy(
        src_ref=out_ref.at[3, pl.ds(half, rows - half)], dst_ref=out_ref.at[2, pl.ds(half, rows - half)],
        send_sem=send_sem.at[3], recv_sem=recv_sem.at[3], device_id=plus, device_id_type=MESH_ID)
    on_plus.start()
    to_minus.wait_send()
    to_plus.wait_send()
    own.wait()
    on_minus.wait_send()
    on_plus.wait_send()
    on_minus.wait_recv()
    on_plus.wait_recv()


def ring_y_kernel(x, collective_id):
    rows, width = x.shape
    return pl.pallas_call(
        _ring_kernel,
        out_shape=jax.ShapeDtypeStruct((4, rows, width), x.dtype),
        in_specs=[pl.BlockSpec(memory_space=pl.ANY)],
        out_specs=pl.BlockSpec(memory_space=pl.ANY),
        scratch_shapes=[
            pltpu.SemaphoreType.DMA((4,)),
            pltpu.SemaphoreType.DMA((4,)),
            pltpu.SemaphoreType.DMA((1,)),
        ],
        compiler_params=pltpu.CompilerParams(collective_id=collective_id, has_side_effects=True),
    )(x)


def gather_seq(x):
    for name in reversed(SEQ_PARTS):
        x = lax.all_gather(x, name, axis=0, tiled=True)
    return x


def gather_xh(x):
    other = lax.ppermute(x, "xh", [(0, 1), (1, 0)])
    return jnp.where(
        lax.axis_index("xh") == 0,
        jnp.concatenate([x, other], axis=0),
        jnp.concatenate([other, x], axis=0),
    )


def gather_xh_z(x):
    x = gather_xh(x)
    return lax.all_gather(x, "z", axis=0, tiled=True)


def ring_y(x):
    ny = 4
    right = [(i, (i + 1) % ny) for i in range(ny)]
    left = [(i, (i - 1) % ny) for i in range(ny)]
    from_minus = lax.ppermute(x, "y", right)
    from_plus = lax.ppermute(x, "y", left)
    half = x.shape[0] // 2
    opp_a = lax.ppermute(from_minus[:half], "y", right)
    opp_b = lax.ppermute(from_plus[half:], "y", left)
    opposite = jnp.concatenate([opp_a, opp_b], axis=0)
    return jnp.stack([x, from_plus, opposite, from_minus])


def gather_mdl(x):
    mdl_index = lax.axis_index("mdl")
    n_mdl = lax.axis_size("mdl")
    other = lax.ppermute(x, "mdl", [(m, m ^ 1) for m in range(n_mdl)])
    pair = jnp.where(
        mdl_index % 2 == 0,
        jnp.concatenate([x, other], axis=1),
        jnp.concatenate([other, x], axis=1),
    )
    other = lax.ppermute(pair, "mdl", [(m, m ^ 2) for m in range(n_mdl)])
    return jnp.where(
        mdl_index // 2 == 0,
        jnp.concatenate([pair, other], axis=1),
        jnp.concatenate([other, pair], axis=1),
    )


def body(
    tokens,
    norm_gain,
    w_query,
    key_matrix,
    value_matrix,
    w_gate,
    q_gain,
    k_gain,
    w_out,
    prompt_lengths,
    segment_ids,
    tenant_ranges,
    key_mask,
    cache_slot,
):
    local_rows = tokens.shape[0]
    weight_rows = w_query.shape[0]
    q_cols = w_query.shape[1]
    kv_cols = key_matrix.shape[1]
    g_cols = w_gate.shape[1]
    seq_size = lax.axis_size(SEQ_PARTS)
    stream = local_rows * seq_size
    request_count = prompt_lengths.shape[0]

    mask_cols = local_rows // weight_rows
    mask_block = key_mask.astype(jnp.bfloat16).reshape(weight_rows, mask_cols)
    mask_block = jnp.pad(mask_block, ((0, 0), (0, 128 - mask_cols)))
    packed = jnp.concatenate([w_query, key_matrix, value_matrix, w_out.T, mask_block], axis=1)
    packed = gather_xh(packed)
    packed = lax.all_gather(packed, "y", axis=0, tiled=True)
    packed, gate_in = lax.optimization_barrier((packed, w_gate))
    gate_ring = ring_y_kernel(gather_xh_z(gate_in), 1)
    gathered = lax.all_gather(packed, "z", axis=0, tiled=True)
    gathered, gate_ring = lax.optimization_barrier((gathered, gate_ring))
    proj_cols = q_cols + 2 * kv_cols
    w_proj = gathered[:, :proj_cols]
    w_out_t = gathered[:, proj_cols : proj_cols + w_out.shape[0]]
    all_mask = gathered[:, proj_cols + w_out.shape[0] : proj_cols + w_out.shape[0] + mask_cols]
    all_mask = all_mask.reshape(stream)
    w_gate_perm = gate_ring.reshape(-1, g_cols)

    wide_tokens = tokens.astype(jnp.float32)
    full_width = tokens.shape[1] * lax.axis_size("mdl")
    square_part = jnp.sum(wide_tokens * wide_tokens, axis=1)
    n_mdl_in = lax.axis_size("mdl")
    square_part = square_part + lax.ppermute(
        square_part, "mdl", [(m, m ^ 1) for m in range(n_mdl_in)]
    )
    square_total = square_part + lax.ppermute(
        square_part, "mdl", [(m, m ^ 2) for m in range(n_mdl_in)]
    )
    scaled = (
        wide_tokens
        * lax.rsqrt(square_total / full_width + epsilon)[:, None]
        * norm_gain.astype(jnp.float32)
    )
    normalized_input = gather_mdl(scaled.astype(jnp.bfloat16))
    projected = jnp.dot(normalized_input, w_proj, preferred_element_type=jnp.float32)
    query_rows = projected[:, :q_cols]
    unprojected_keys = projected[:, q_cols : q_cols + kv_cols]
    values_raw = projected[:, q_cols + kv_cols : q_cols + 2 * kv_cols]
    my_y = lax.axis_index("y")
    input_perm = normalized_input.reshape(local_rows, 8, 4, 2, weight_rows)
    input_perm = jnp.roll(input_perm, -my_y, axis=2)
    input_perm = input_perm.transpose(0, 2, 1, 3, 4).reshape(local_rows, -1)
    gate_logits = jnp.dot(input_perm, w_gate_perm, preferred_element_type=jnp.float32)

    device_seq = lax.axis_index(SEQ_PARTS)
    token_ids = device_seq * local_rows + jnp.arange(local_rows, dtype=jnp.int32)
    starts = jnp.cumsum(prompt_lengths) - prompt_lengths
    ends = starts + prompt_lengths
    requests = jnp.arange(request_count, dtype=jnp.int32)
    member = (requests[:, None] > tenant_ranges[None, :, 0]) & (
        requests[:, None] < tenant_ranges[None, :, 1]
    )
    shared_of = jnp.sum(jnp.where(member, tenant_ranges[None, :, 0] + 3, 0), axis=1) - 3
    onehot = segment_ids[:, None] == requests[None, :]
    seg_start = jnp.sum(jnp.where(onehot, starts[None, :], 0), axis=1)
    shared_req = jnp.sum(jnp.where(onehot, shared_of[None, :], 0), axis=1)
    position = token_ids - seg_start

    query_heads = q_cols // HEAD_SIZE
    kv_heads = kv_cols // HEAD_SIZE
    group = query_heads // kv_heads
    q_rot = (
        rotate(head_norm(query_rows.reshape(local_rows, query_heads, HEAD_SIZE), q_gain), position)
        .astype(jnp.bfloat16)
        .reshape(local_rows, kv_heads, group, HEAD_SIZE)
    )
    k_rot = (
        rotate(head_norm(unprojected_keys.reshape(local_rows, kv_heads, HEAD_SIZE), k_gain), position)
        .astype(jnp.bfloat16)
        .reshape(local_rows, kv_cols)
    )
    values_flat = values_raw.astype(jnp.bfloat16)
    kv_pair = gather_xh(jnp.concatenate([k_rot, values_flat], axis=1))
    v_part = lax.all_gather(kv_pair[:, kv_cols:], "z", axis=0, tiled=True)
    k_part = ring_y_kernel(kv_pair[:, :kv_cols], 2).reshape(-1, kv_cols)
    k_part, v_part = lax.optimization_barrier((k_part, v_part))
    k_all = lax.all_gather(k_part, "z", axis=0, tiled=True)
    v_ring = ring_y_kernel(v_part, 3).reshape(-1, kv_cols)

    def k_row_of(token):
        block = token // local_rows
        rel = (block // 2 % 4 - my_y) % 4
        place = ((block // 8) * 4 + rel) * 2 + block % 2
        return place * local_rows + token % local_rows

    def v_row_of(token):
        block = token // local_rows
        rel = (block // 2 % 4 - my_y) % 4
        place = (block // 8) * 2 + block % 2
        return (rel * 16 + place) * local_rows + token % local_rows

    n_blocks = stream // KEY_BLOCK
    block_ids = jnp.arange(n_blocks, dtype=jnp.int32)
    last_block = (device_seq * local_rows + local_rows - 1) // KEY_BLOCK
    first_block = jnp.min(seg_start) // KEY_BLOCK
    needed = (block_ids >= first_block) & (block_ids <= last_block)
    lo = tenant_ranges[:, 0]
    hi = tenant_ranges[:, 1]
    used = jnp.any(
        (segment_ids[:, None] > lo[None, :]) & (segment_ids[:, None] < hi[None, :]), axis=0
    )
    lo_start = jnp.sum(jnp.where(requests[None, :] == lo[:, None], starts[None, :], 0), axis=1)
    lo_end = jnp.sum(jnp.where(requests[None, :] == lo[:, None], ends[None, :], 0), axis=1)
    in_prompt = (
        used[:, None]
        & (block_ids[None, :] >= (lo_start // KEY_BLOCK)[:, None])
        & (block_ids[None, :] <= ((lo_end - 1) // KEY_BLOCK)[:, None])
    )
    needed = needed | jnp.any(in_prompt, axis=0)
    n_needed = jnp.sum(needed.astype(jnp.int32))
    (block_list,) = jnp.nonzero(needed, size=n_blocks, fill_value=0)
    block_list = block_list.astype(jnp.int32)

    row_segs = segment_ids
    row_shared = shared_req
    scale_factor = HEAD_SIZE ** (-0.5)
    head_shape = (local_rows, kv_heads, group)

    stream_ids = jnp.arange(stream, dtype=jnp.int32)
    key_segs = jnp.sum((stream_ids[:, None] >= ends[None, :]).astype(jnp.int32), axis=1)
    key_tags = jnp.where(all_mask == 1, key_segs, -2)

    def key_block(i, loop_state):
        old_top, old_totals, old_summed = loop_state
        block = block_list[i]
        offset = block * KEY_BLOCK
        keys_part = lax.dynamic_slice_in_dim(k_all, k_row_of(offset), KEY_BLOCK, 0).reshape(
            KEY_BLOCK, kv_heads, HEAD_SIZE
        )
        values_part = lax.dynamic_slice_in_dim(v_ring, v_row_of(offset), KEY_BLOCK, 0).reshape(
            KEY_BLOCK, kv_heads, HEAD_SIZE
        )
        tag_part = lax.dynamic_slice_in_dim(key_tags, offset, KEY_BLOCK, 0)
        columns = offset + jnp.arange(KEY_BLOCK, dtype=jnp.int32)
        own = tag_part[None, :] == row_segs[:, None]
        other = tag_part[None, :] == row_shared[:, None]
        earlier = columns[None, :] <= token_ids[:, None]
        diagonal = columns[None, :] == token_ids[:, None]
        visible = diagonal | (earlier & (own | other))
        allowed = visible[:, None, None, :]
        scores = (
            jnp.einsum("qhgd,khd->qhgk", q_rot, keys_part, preferred_element_type=jnp.float32)
            * scale_factor
        )
        scores = jnp.where(allowed, scores, masked_score)
        new_top = jnp.maximum(old_top, jnp.max(scores, axis=-1))
        factor = jnp.exp(old_top - new_top)
        raw_weights = jnp.where(allowed, jnp.exp(scores - new_top[..., None]), 0.0)
        new_totals = old_totals * factor + jnp.sum(raw_weights, axis=-1)
        new_summed = old_summed * factor[..., None] + jnp.einsum(
            "qhgk,khd->qhgd",
            raw_weights.astype(jnp.bfloat16),
            values_part,
            preferred_element_type=jnp.float32,
        )
        return (new_top, new_totals, new_summed)

    start_state = (
        jnp.full(head_shape, masked_score, jnp.float32),
        jnp.zeros(head_shape, jnp.float32),
        jnp.zeros(head_shape + (HEAD_SIZE,), jnp.float32),
    )
    top_now, totals, summed = lax.fori_loop(0, n_needed, key_block, start_state)

    my_request = jnp.sum(jnp.where(cache_slot == device_seq, requests, 0))
    my_start = jnp.sum(jnp.where(requests == my_request, starts, 0))
    my_length = jnp.sum(jnp.where(requests == my_request, prompt_lengths, 0))
    offsets = jnp.arange(LMAX, dtype=jnp.int32)
    wanted = my_start + offsets
    in_window = ((wanted < stream) & (offsets < my_length))[:, None]
    zero = jnp.zeros((), jnp.bfloat16)
    first = my_start // KEY_BLOCK
    shift = my_start % KEY_BLOCK
    spans = [jnp.clip(first + j, 0, n_blocks - 1) * KEY_BLOCK for j in range(3)]

    def cache_of(table, row_of):
        pieces = [lax.dynamic_slice_in_dim(table, row_of(b), KEY_BLOCK, 0) for b in spans]
        window = lax.dynamic_slice_in_dim(jnp.concatenate(pieces, axis=0), shift, LMAX, 0)
        return jnp.where(in_window, window, zero)

    cache_k = cache_of(k_all, k_row_of)
    cache_v = cache_of(v_ring, v_row_of)

    attended = (summed / totals[..., None]).reshape(local_rows, query_heads * HEAD_SIZE)
    gated_heads = (attended * jax.nn.sigmoid(gate_logits)).astype(jnp.bfloat16)
    partial_out = lax.dot_general(
        gated_heads,
        w_out_t,
        (((1,), (1,)), ((), ())),
        preferred_element_type=jnp.float32,
    )
    mdl_index = lax.axis_index("mdl")
    n_mdl = lax.axis_size("mdl")
    x_lo = mdl_index // 2
    core = mdl_index % 2
    quarter = partial_out.shape[1] // 4

    def cols_of(block):
        return lax.dynamic_slice_in_dim(partial_out, block * quarter, quarter, 1)

    mine = jnp.concatenate([cols_of(core), cols_of(2 + core)], axis=1)
    theirs = jnp.concatenate([cols_of(1 - core), cols_of(3 - core)], axis=1)
    pair_sum = mine + lax.ppermute(theirs, "mdl", [(m, m ^ 1) for m in range(n_mdl)])
    mine = lax.dynamic_slice_in_dim(pair_sum, x_lo * quarter, quarter, 1)
    theirs = lax.dynamic_slice_in_dim(pair_sum, (1 - x_lo) * quarter, quarter, 1)
    across = lax.ppermute(
        theirs.astype(jnp.bfloat16), "mdl", [(m, m ^ 2) for m in range(n_mdl)]
    )
    branch_sum = mine + across.astype(jnp.float32)
    layer_out = (wide_tokens + branch_sum).astype(jnp.bfloat16)
    return (layer_out, cache_k[None], cache_v[None])


def solution(mesh):
    seq = SEQ_PARTS
    split = Mesh(mesh.devices.reshape(8, 4, 2, mesh.shape["mdl"]), SEQ_PARTS + ("mdl",))
    placed = (
        P(seq, "mdl"),
        P("mdl"),
        P(seq, "mdl"),
        P(seq, "mdl"),
        P(seq, "mdl"),
        P(seq, "mdl"),
        P(),
        P(),
        P("mdl", seq),
        P(),
        P(seq),
        P(),
        P(seq),
        P(),
    )
    return jax.shard_map(
        body,
        mesh=split,
        in_specs=placed,
        out_specs=(P(seq, "mdl"), P(seq, None, "mdl"), P(seq, None, "mdl")),
        check_vma=False,
    )
```

```python
import jax
import jax.numpy as jnp
from jax import lax
from jax.experimental import pallas as pl
from jax.experimental.pallas import tpu as pltpu
from jax.sharding import Mesh
from jax.sharding import PartitionSpec as P

HEAD_SIZE = 128
LMAX = 512
KEY_BLOCK = 256
BATCH_BLOCKS = 3


epsilon = 1e-06
rope_base = 1000000.0
masked_score = -1e30


def head_norm(values, gain_vector):
    return (
        values
        * lax.rsqrt(jnp.mean(values * values, axis=-1, keepdims=True) + epsilon)
        * gain_vector
    )


def rotate(values, position):
    half_width = values.shape[-1] // 2
    frequency = rope_base ** (-2.0 * jnp.arange(half_width, dtype=jnp.float32) / values.shape[-1])
    angles = position.astype(jnp.float32)[:, None] * frequency[None, :]
    cosine = jnp.cos(angles)[:, None, :]
    sine_part = jnp.sin(angles)[:, None, :]
    former = values[..., :half_width]
    latter = values[..., half_width:]
    return jnp.concatenate(
        [former * cosine - latter * sine_part, latter * cosine + former * sine_part], axis=-1
    )


SEQ_PARTS = ("z", "y", "xh")
MESH_ID = pl.DeviceIdType.MESH
AXES = SEQ_PARTS + ("mdl",)


def _ring_kernel(x_ref, out_ref, send_sem, recv_sem, local_sem):
    ny = 4
    me = {name: lax.axis_index(name) for name in AXES}
    my_y = me["y"]

    def dev(yy):
        return tuple(yy if name == "y" else me[name] for name in AXES)

    plus = dev(lax.rem(my_y + 1, ny))
    minus = dev(lax.rem(my_y + ny - 1, ny))
    barrier = pltpu.get_barrier_semaphore()
    for d in (plus, minus):
        pl.semaphore_signal(barrier, inc=1, device_id=d, device_id_type=MESH_ID)
    pl.semaphore_wait(barrier, 2)

    rows = x_ref.shape[0]
    half = rows // 2
    to_minus = pltpu.make_async_remote_copy(
        src_ref=x_ref, dst_ref=out_ref.at[1], send_sem=send_sem.at[0], recv_sem=recv_sem.at[0],
        device_id=minus, device_id_type=MESH_ID)
    to_plus = pltpu.make_async_remote_copy(
        src_ref=x_ref, dst_ref=out_ref.at[3], send_sem=send_sem.at[1], recv_sem=recv_sem.at[1],
        device_id=plus, device_id_type=MESH_ID)
    own = pltpu.make_async_copy(x_ref, out_ref.at[0], local_sem.at[0])
    to_minus.start()
    to_plus.start()
    own.start()
    to_minus.wait_recv()
    on_minus = pltpu.make_async_remote_copy(
        src_ref=out_ref.at[1, pl.ds(0, half)], dst_ref=out_ref.at[2, pl.ds(0, half)],
        send_sem=send_sem.at[2], recv_sem=recv_sem.at[2], device_id=minus, device_id_type=MESH_ID)
    on_minus.start()
    to_plus.wait_recv()
    on_plus = pltpu.make_async_remote_copy(
        src_ref=out_ref.at[3, pl.ds(half, rows - half)], dst_ref=out_ref.at[2, pl.ds(half, rows - half)],
        send_sem=send_sem.at[3], recv_sem=recv_sem.at[3], device_id=plus, device_id_type=MESH_ID)
    on_plus.start()
    to_minus.wait_send()
    to_plus.wait_send()
    own.wait()
    on_minus.wait_send()
    on_plus.wait_send()
    on_minus.wait_recv()
    on_plus.wait_recv()


def ring_y_kernel(x, collective_id):
    rows, width = x.shape
    return pl.pallas_call(
        _ring_kernel,
        out_shape=jax.ShapeDtypeStruct((4, rows, width), x.dtype),
        in_specs=[pl.BlockSpec(memory_space=pl.ANY)],
        out_specs=pl.BlockSpec(memory_space=pl.ANY),
        scratch_shapes=[
            pltpu.SemaphoreType.DMA((4,)),
            pltpu.SemaphoreType.DMA((4,)),
            pltpu.SemaphoreType.DMA((1,)),
        ],
        compiler_params=pltpu.CompilerParams(collective_id=collective_id, has_side_effects=True),
    )(x)


def gather_seq(x):
    for name in reversed(SEQ_PARTS):
        x = lax.all_gather(x, name, axis=0, tiled=True)
    return x


def gather_xh_z(x):
    x = lax.all_gather(x, "xh", axis=0, tiled=True)
    return lax.all_gather(x, "z", axis=0, tiled=True)


def ring_y(x):
    ny = 4
    right = [(i, (i + 1) % ny) for i in range(ny)]
    left = [(i, (i - 1) % ny) for i in range(ny)]
    from_minus = lax.ppermute(x, "y", right)
    from_plus = lax.ppermute(x, "y", left)
    half = x.shape[0] // 2
    opp_a = lax.ppermute(from_minus[:half], "y", right)
    opp_b = lax.ppermute(from_plus[half:], "y", left)
    opposite = jnp.concatenate([opp_a, opp_b], axis=0)
    return jnp.stack([x, from_plus, opposite, from_minus])


def gather_mdl(x):
    mdl_index = lax.axis_index("mdl")
    n_mdl = lax.axis_size("mdl")
    other = lax.ppermute(x, "mdl", [(m, m ^ 1) for m in range(n_mdl)])
    pair = jnp.where(
        mdl_index % 2 == 0,
        jnp.concatenate([x, other], axis=1),
        jnp.concatenate([other, x], axis=1),
    )
    other = lax.ppermute(pair, "mdl", [(m, m ^ 2) for m in range(n_mdl)])
    return jnp.where(
        mdl_index // 2 == 0,
        jnp.concatenate([pair, other], axis=1),
        jnp.concatenate([other, pair], axis=1),
    )


def body(
    tokens,
    norm_gain,
    w_query,
    key_matrix,
    value_matrix,
    w_gate,
    q_gain,
    k_gain,
    w_out,
    prompt_lengths,
    segment_ids,
    tenant_ranges,
    key_mask,
    cache_slot,
):
    local_rows = tokens.shape[0]
    weight_rows = w_query.shape[0]
    q_cols = w_query.shape[1]
    kv_cols = key_matrix.shape[1]
    g_cols = w_gate.shape[1]
    seq_size = lax.axis_size(SEQ_PARTS)
    stream = local_rows * seq_size
    request_count = prompt_lengths.shape[0]

    mask_cols = local_rows // weight_rows
    mask_block = key_mask.astype(jnp.bfloat16).reshape(weight_rows, mask_cols)
    mask_block = jnp.pad(mask_block, ((0, 0), (0, 128 - mask_cols)))
    packed = jnp.concatenate([w_query, key_matrix, value_matrix, w_out.T, mask_block], axis=1)
    packed = lax.all_gather(packed, "xh", axis=0, tiled=True)
    packed = lax.all_gather(packed, "y", axis=0, tiled=True)
    packed, gate_in = lax.optimization_barrier((packed, w_gate))
    gate_ring = ring_y_kernel(gather_xh_z(gate_in), 1)
    gathered = lax.all_gather(packed, "z", axis=0, tiled=True)
    gathered, gate_ring = lax.optimization_barrier((gathered, gate_ring))
    proj_cols = q_cols + 2 * kv_cols
    w_proj = gathered[:, :proj_cols]
    w_out_t = gathered[:, proj_cols : proj_cols + w_out.shape[0]]
    all_mask = gathered[:, proj_cols + w_out.shape[0] : proj_cols + w_out.shape[0] + mask_cols]
    all_mask = all_mask.reshape(stream)
    w_gate_perm = gate_ring.reshape(-1, g_cols)

    wide_tokens = tokens.astype(jnp.float32)
    full_width = tokens.shape[1] * lax.axis_size("mdl")
    square_part = jnp.sum(wide_tokens * wide_tokens, axis=1)
    n_mdl_in = lax.axis_size("mdl")
    square_part = square_part + lax.ppermute(
        square_part, "mdl", [(m, m ^ 1) for m in range(n_mdl_in)]
    )
    square_total = square_part + lax.ppermute(
        square_part, "mdl", [(m, m ^ 2) for m in range(n_mdl_in)]
    )
    scaled = (
        wide_tokens
        * lax.rsqrt(square_total / full_width + epsilon)[:, None]
        * norm_gain.astype(jnp.float32)
    )
    normalized_input = gather_mdl(scaled.astype(jnp.bfloat16))
    projected = jnp.dot(normalized_input, w_proj, preferred_element_type=jnp.float32)
    query_rows = projected[:, :q_cols]
    unprojected_keys = projected[:, q_cols : q_cols + kv_cols]
    values_raw = projected[:, q_cols + kv_cols : q_cols + 2 * kv_cols]
    my_y = lax.axis_index("y")
    input_perm = normalized_input.reshape(local_rows, 8, 4, 2, weight_rows)
    input_perm = jnp.roll(input_perm, -my_y, axis=2)
    input_perm = input_perm.transpose(0, 2, 1, 3, 4).reshape(local_rows, -1)
    gate_logits = jnp.dot(input_perm, w_gate_perm, preferred_element_type=jnp.float32)

    device_seq = lax.axis_index(SEQ_PARTS)
    token_ids = device_seq * local_rows + jnp.arange(local_rows, dtype=jnp.int32)
    starts = jnp.cumsum(prompt_lengths) - prompt_lengths
    ends = starts + prompt_lengths
    requests = jnp.arange(request_count, dtype=jnp.int32)
    member = (requests[:, None] > tenant_ranges[None, :, 0]) & (
        requests[:, None] < tenant_ranges[None, :, 1]
    )
    shared_of = jnp.sum(jnp.where(member, tenant_ranges[None, :, 0] + 3, 0), axis=1) - 3
    onehot = segment_ids[:, None] == requests[None, :]
    seg_start = jnp.sum(jnp.where(onehot, starts[None, :], 0), axis=1)
    shared_req = jnp.sum(jnp.where(onehot, shared_of[None, :], 0), axis=1)
    position = token_ids - seg_start

    query_heads = q_cols // HEAD_SIZE
    kv_heads = kv_cols // HEAD_SIZE
    group = query_heads // kv_heads
    q_rot = (
        rotate(head_norm(query_rows.reshape(local_rows, query_heads, HEAD_SIZE), q_gain), position)
        .astype(jnp.bfloat16)
        .reshape(local_rows, kv_heads, group, HEAD_SIZE)
    )
    k_rot = (
        rotate(head_norm(unprojected_keys.reshape(local_rows, kv_heads, HEAD_SIZE), k_gain), position)
        .astype(jnp.bfloat16)
        .reshape(local_rows, kv_cols)
    )
    values_flat = values_raw.astype(jnp.bfloat16)
    kv_pair = lax.all_gather(jnp.concatenate([k_rot, values_flat], axis=1), "xh", axis=0, tiled=True)
    v_part = lax.all_gather(kv_pair[:, kv_cols:], "z", axis=0, tiled=True)
    k_part = ring_y_kernel(kv_pair[:, :kv_cols], 2).reshape(-1, kv_cols)
    k_part, v_part = lax.optimization_barrier((k_part, v_part))
    k_all = lax.all_gather(k_part, "z", axis=0, tiled=True)
    v_ring = ring_y_kernel(v_part, 3).reshape(-1, kv_cols)

    def k_row_of(token):
        block = token // local_rows
        rel = (block // 2 % 4 - my_y) % 4
        place = ((block // 8) * 4 + rel) * 2 + block % 2
        return place * local_rows + token % local_rows

    def v_row_of(token):
        block = token // local_rows
        rel = (block // 2 % 4 - my_y) % 4
        place = (block // 8) * 2 + block % 2
        return (rel * 16 + place) * local_rows + token % local_rows

    n_blocks = stream // KEY_BLOCK
    block_ids = jnp.arange(n_blocks, dtype=jnp.int32)
    last_block = (device_seq * local_rows + local_rows - 1) // KEY_BLOCK
    first_block = jnp.min(seg_start) // KEY_BLOCK
    needed = (block_ids >= first_block) & (block_ids <= last_block)
    lo = tenant_ranges[:, 0]
    hi = tenant_ranges[:, 1]
    used = jnp.any(
        (segment_ids[:, None] > lo[None, :]) & (segment_ids[:, None] < hi[None, :]), axis=0
    )
    lo_start = jnp.sum(jnp.where(requests[None, :] == lo[:, None], starts[None, :], 0), axis=1)
    lo_end = jnp.sum(jnp.where(requests[None, :] == lo[:, None], ends[None, :], 0), axis=1)
    in_prompt = (
        used[:, None]
        & (block_ids[None, :] >= (lo_start // KEY_BLOCK)[:, None])
        & (block_ids[None, :] <= ((lo_end - 1) // KEY_BLOCK)[:, None])
    )
    needed = needed | jnp.any(in_prompt, axis=0)
    n_needed = jnp.sum(needed.astype(jnp.int32))
    (block_list,) = jnp.nonzero(needed, size=n_blocks, fill_value=0)
    block_list = block_list.astype(jnp.int32)

    row_segs = segment_ids
    row_shared = shared_req
    scale_factor = HEAD_SIZE ** (-0.5)
    head_shape = (local_rows, kv_heads, group)

    stream_ids = jnp.arange(stream, dtype=jnp.int32)
    key_segs = jnp.sum((stream_ids[:, None] >= ends[None, :]).astype(jnp.int32), axis=1)
    key_tags = jnp.where(all_mask == 1, key_segs, -2)

    def key_block(i, loop_state):
        old_top, old_totals, old_summed = loop_state
        block = block_list[i]
        offset = block * KEY_BLOCK
        keys_part = lax.dynamic_slice_in_dim(k_all, k_row_of(offset), KEY_BLOCK, 0).reshape(
            KEY_BLOCK, kv_heads, HEAD_SIZE
        )
        values_part = lax.dynamic_slice_in_dim(v_ring, v_row_of(offset), KEY_BLOCK, 0).reshape(
            KEY_BLOCK, kv_heads, HEAD_SIZE
        )
        tag_part = lax.dynamic_slice_in_dim(key_tags, offset, KEY_BLOCK, 0)
        columns = offset + jnp.arange(KEY_BLOCK, dtype=jnp.int32)
        own = tag_part[None, :] == row_segs[:, None]
        other = tag_part[None, :] == row_shared[:, None]
        earlier = columns[None, :] <= token_ids[:, None]
        diagonal = columns[None, :] == token_ids[:, None]
        visible = diagonal | (earlier & (own | other))
        allowed = visible[:, None, None, :]
        scores = (
            jnp.einsum("qhgd,khd->qhgk", q_rot, keys_part, preferred_element_type=jnp.float32)
            * scale_factor
        )
        scores = jnp.where(allowed, scores, masked_score)
        new_top = jnp.maximum(old_top, jnp.max(scores, axis=-1))
        factor = jnp.exp(old_top - new_top)
        raw_weights = jnp.where(allowed, jnp.exp(scores - new_top[..., None]), 0.0)
        new_totals = old_totals * factor + jnp.sum(raw_weights, axis=-1)
        new_summed = old_summed * factor[..., None] + jnp.einsum(
            "qhgk,khd->qhgd",
            raw_weights.astype(jnp.bfloat16),
            values_part,
            preferred_element_type=jnp.float32,
        )
        return (new_top, new_totals, new_summed)

    slots = block_list[:BATCH_BLOCKS]
    slot_live = jnp.arange(BATCH_BLOCKS, dtype=jnp.int32) < n_needed
    slot_offsets = slots * KEY_BLOCK
    keys_b = jnp.stack(
        [lax.dynamic_slice_in_dim(k_all, k_row_of(o), KEY_BLOCK, 0) for o in slot_offsets]
    ).reshape(BATCH_BLOCKS * KEY_BLOCK, kv_heads, HEAD_SIZE)
    values_b = jnp.stack(
        [lax.dynamic_slice_in_dim(v_ring, v_row_of(o), KEY_BLOCK, 0) for o in slot_offsets]
    ).reshape(BATCH_BLOCKS * KEY_BLOCK, kv_heads, HEAD_SIZE)
    tags_b = jnp.stack(
        [lax.dynamic_slice_in_dim(key_tags, o, KEY_BLOCK, 0) for o in slot_offsets]
    ).reshape(-1)
    columns_b = (slot_offsets[:, None] + jnp.arange(KEY_BLOCK, dtype=jnp.int32)[None, :]).reshape(-1)
    live_b = jnp.repeat(slot_live, KEY_BLOCK)
    visible_b = live_b[None, :] & (
        (columns_b[None, :] == token_ids[:, None])
        | (
            (columns_b[None, :] <= token_ids[:, None])
            & ((tags_b[None, :] == row_segs[:, None]) | (tags_b[None, :] == row_shared[:, None]))
        )
    )
    allowed_b = visible_b[:, None, None, :]
    scores_b = (
        jnp.einsum("qhgd,khd->qhgk", q_rot, keys_b, preferred_element_type=jnp.float32)
        * scale_factor
    )
    scores_b = jnp.where(allowed_b, scores_b, masked_score)
    top_b = jnp.max(scores_b, axis=-1)
    raw_b = jnp.where(allowed_b, jnp.exp(scores_b - top_b[..., None]), 0.0)
    totals_b = jnp.sum(raw_b, axis=-1)
    summed_b = jnp.einsum(
        "qhgk,khd->qhgd", raw_b.astype(jnp.bfloat16), values_b, preferred_element_type=jnp.float32
    )
    start_state = (top_b, totals_b, summed_b)
    top_now, totals, summed = lax.fori_loop(
        jnp.minimum(n_needed, BATCH_BLOCKS), n_needed, key_block, start_state
    )

    my_request = jnp.sum(jnp.where(cache_slot == device_seq, requests, 0))
    my_start = jnp.sum(jnp.where(requests == my_request, starts, 0))
    my_length = jnp.sum(jnp.where(requests == my_request, prompt_lengths, 0))
    offsets = jnp.arange(LMAX, dtype=jnp.int32)
    wanted = my_start + offsets
    in_window = ((wanted < stream) & (offsets < my_length))[:, None]
    zero = jnp.zeros((), jnp.bfloat16)
    first = my_start // KEY_BLOCK
    shift = my_start % KEY_BLOCK
    spans = [jnp.clip(first + j, 0, n_blocks - 1) * KEY_BLOCK for j in range(3)]

    def cache_of(table, row_of):
        pieces = [lax.dynamic_slice_in_dim(table, row_of(b), KEY_BLOCK, 0) for b in spans]
        window = lax.dynamic_slice_in_dim(jnp.concatenate(pieces, axis=0), shift, LMAX, 0)
        return jnp.where(in_window, window, zero)

    cache_k = cache_of(k_all, k_row_of)
    cache_v = cache_of(v_ring, v_row_of)

    attended = (summed / totals[..., None]).reshape(local_rows, query_heads * HEAD_SIZE)
    gated_heads = (attended * jax.nn.sigmoid(gate_logits)).astype(jnp.bfloat16)
    partial_out = lax.dot_general(
        gated_heads,
        w_out_t,
        (((1,), (1,)), ((), ())),
        preferred_element_type=jnp.float32,
    )
    mdl_index = lax.axis_index("mdl")
    n_mdl = lax.axis_size("mdl")
    x_lo = mdl_index // 2
    core = mdl_index % 2
    quarter = partial_out.shape[1] // 4

    def cols_of(block):
        return lax.dynamic_slice_in_dim(partial_out, block * quarter, quarter, 1)

    mine = jnp.concatenate([cols_of(core), cols_of(2 + core)], axis=1)
    theirs = jnp.concatenate([cols_of(1 - core), cols_of(3 - core)], axis=1)
    pair_sum = mine + lax.ppermute(theirs, "mdl", [(m, m ^ 1) for m in range(n_mdl)])
    mine = lax.dynamic_slice_in_dim(pair_sum, x_lo * quarter, quarter, 1)
    theirs = lax.dynamic_slice_in_dim(pair_sum, (1 - x_lo) * quarter, quarter, 1)
    across = lax.ppermute(
        theirs.astype(jnp.bfloat16), "mdl", [(m, m ^ 2) for m in range(n_mdl)]
    )
    branch_sum = mine + across.astype(jnp.float32)
    layer_out = (wide_tokens + branch_sum).astype(jnp.bfloat16)
    return (layer_out, cache_k[None], cache_v[None])


def solution(mesh):
    seq = SEQ_PARTS
    split = Mesh(mesh.devices.reshape(8, 4, 2, mesh.shape["mdl"]), SEQ_PARTS + ("mdl",))
    placed = (
        P(seq, "mdl"),
        P("mdl"),
        P(seq, "mdl"),
        P(seq, "mdl"),
        P(seq, "mdl"),
        P(seq, "mdl"),
        P(),
        P(),
        P("mdl", seq),
        P(),
        P(seq),
        P(),
        P(seq),
        P(),
    )
    return jax.shard_map(
        body,
        mesh=split,
        in_specs=placed,
        out_specs=(P(seq, "mdl"), P(seq, None, "mdl"), P(seq, None, "mdl")),
        check_vma=False,
    )
```

```python
import jax
import jax.numpy as jnp
from jax import lax
from jax.experimental import pallas as pl
from jax.experimental.pallas import tpu as pltpu
from jax.sharding import Mesh
from jax.sharding import PartitionSpec as P

HEAD_SIZE = 128
LMAX = 512
KEY_BLOCK = 256
BATCH_BLOCKS = 5


epsilon = 1e-06
rope_base = 1000000.0
masked_score = -1e30


def head_norm(values, gain_vector):
    return (
        values
        * lax.rsqrt(jnp.mean(values * values, axis=-1, keepdims=True) + epsilon)
        * gain_vector
    )


def rotate(values, position):
    half_width = values.shape[-1] // 2
    frequency = rope_base ** (-2.0 * jnp.arange(half_width, dtype=jnp.float32) / values.shape[-1])
    angles = position.astype(jnp.float32)[:, None] * frequency[None, :]
    cosine = jnp.cos(angles)[:, None, :]
    sine_part = jnp.sin(angles)[:, None, :]
    former = values[..., :half_width]
    latter = values[..., half_width:]
    return jnp.concatenate(
        [former * cosine - latter * sine_part, latter * cosine + former * sine_part], axis=-1
    )


SEQ_PARTS = ("z", "y", "xh")
MESH_ID = pl.DeviceIdType.MESH
AXES = SEQ_PARTS + ("mdl",)


def _ring_kernel(x_ref, out_ref, send_sem, recv_sem, local_sem):
    ny = 4
    me = {name: lax.axis_index(name) for name in AXES}
    my_y = me["y"]

    def dev(yy):
        return tuple(yy if name == "y" else me[name] for name in AXES)

    plus = dev(lax.rem(my_y + 1, ny))
    minus = dev(lax.rem(my_y + ny - 1, ny))
    barrier = pltpu.get_barrier_semaphore()
    for d in (plus, minus):
        pl.semaphore_signal(barrier, inc=1, device_id=d, device_id_type=MESH_ID)
    pl.semaphore_wait(barrier, 2)

    rows = x_ref.shape[0]
    half = rows // 2
    to_minus = pltpu.make_async_remote_copy(
        src_ref=x_ref, dst_ref=out_ref.at[1], send_sem=send_sem.at[0], recv_sem=recv_sem.at[0],
        device_id=minus, device_id_type=MESH_ID)
    to_plus = pltpu.make_async_remote_copy(
        src_ref=x_ref, dst_ref=out_ref.at[3], send_sem=send_sem.at[1], recv_sem=recv_sem.at[1],
        device_id=plus, device_id_type=MESH_ID)
    own = pltpu.make_async_copy(x_ref, out_ref.at[0], local_sem.at[0])
    to_minus.start()
    to_plus.start()
    own.start()
    to_minus.wait_recv()
    on_minus = pltpu.make_async_remote_copy(
        src_ref=out_ref.at[1, pl.ds(0, half)], dst_ref=out_ref.at[2, pl.ds(0, half)],
        send_sem=send_sem.at[2], recv_sem=recv_sem.at[2], device_id=minus, device_id_type=MESH_ID)
    on_minus.start()
    to_plus.wait_recv()
    on_plus = pltpu.make_async_remote_copy(
        src_ref=out_ref.at[3, pl.ds(half, rows - half)], dst_ref=out_ref.at[2, pl.ds(half, rows - half)],
        send_sem=send_sem.at[3], recv_sem=recv_sem.at[3], device_id=plus, device_id_type=MESH_ID)
    on_plus.start()
    to_minus.wait_send()
    to_plus.wait_send()
    own.wait()
    on_minus.wait_send()
    on_plus.wait_send()
    on_minus.wait_recv()
    on_plus.wait_recv()


def ring_y_kernel(x, collective_id):
    rows, width = x.shape
    return pl.pallas_call(
        _ring_kernel,
        out_shape=jax.ShapeDtypeStruct((4, rows, width), x.dtype),
        in_specs=[pl.BlockSpec(memory_space=pl.ANY)],
        out_specs=pl.BlockSpec(memory_space=pl.ANY),
        scratch_shapes=[
            pltpu.SemaphoreType.DMA((4,)),
            pltpu.SemaphoreType.DMA((4,)),
            pltpu.SemaphoreType.DMA((1,)),
        ],
        compiler_params=pltpu.CompilerParams(collective_id=collective_id, has_side_effects=True),
    )(x)


def gather_seq(x):
    for name in reversed(SEQ_PARTS):
        x = lax.all_gather(x, name, axis=0, tiled=True)
    return x


def gather_xh_z(x):
    x = lax.all_gather(x, "xh", axis=0, tiled=True)
    return lax.all_gather(x, "z", axis=0, tiled=True)


def ring_y(x):
    ny = 4
    right = [(i, (i + 1) % ny) for i in range(ny)]
    left = [(i, (i - 1) % ny) for i in range(ny)]
    from_minus = lax.ppermute(x, "y", right)
    from_plus = lax.ppermute(x, "y", left)
    half = x.shape[0] // 2
    opp_a = lax.ppermute(from_minus[:half], "y", right)
    opp_b = lax.ppermute(from_plus[half:], "y", left)
    opposite = jnp.concatenate([opp_a, opp_b], axis=0)
    return jnp.stack([x, from_plus, opposite, from_minus])


def gather_mdl(x):
    mdl_index = lax.axis_index("mdl")
    n_mdl = lax.axis_size("mdl")
    other = lax.ppermute(x, "mdl", [(m, m ^ 1) for m in range(n_mdl)])
    pair = jnp.where(
        mdl_index % 2 == 0,
        jnp.concatenate([x, other], axis=1),
        jnp.concatenate([other, x], axis=1),
    )
    other = lax.ppermute(pair, "mdl", [(m, m ^ 2) for m in range(n_mdl)])
    return jnp.where(
        mdl_index // 2 == 0,
        jnp.concatenate([pair, other], axis=1),
        jnp.concatenate([other, pair], axis=1),
    )


def body(
    tokens,
    norm_gain,
    w_query,
    key_matrix,
    value_matrix,
    w_gate,
    q_gain,
    k_gain,
    w_out,
    prompt_lengths,
    segment_ids,
    tenant_ranges,
    key_mask,
    cache_slot,
):
    local_rows = tokens.shape[0]
    weight_rows = w_query.shape[0]
    q_cols = w_query.shape[1]
    kv_cols = key_matrix.shape[1]
    g_cols = w_gate.shape[1]
    seq_size = lax.axis_size(SEQ_PARTS)
    stream = local_rows * seq_size
    request_count = prompt_lengths.shape[0]

    mask_cols = local_rows // weight_rows
    mask_block = key_mask.astype(jnp.bfloat16).reshape(weight_rows, mask_cols)
    mask_block = jnp.pad(mask_block, ((0, 0), (0, 128 - mask_cols)))
    packed = jnp.concatenate([w_query, key_matrix, value_matrix, w_out.T, mask_block], axis=1)
    packed = lax.all_gather(packed, "xh", axis=0, tiled=True)
    packed = lax.all_gather(packed, "y", axis=0, tiled=True)
    packed, gate_in = lax.optimization_barrier((packed, w_gate))
    gate_ring = ring_y_kernel(gather_xh_z(gate_in), 1)
    gathered = lax.all_gather(packed, "z", axis=0, tiled=True)
    gathered, gate_ring = lax.optimization_barrier((gathered, gate_ring))
    proj_cols = q_cols + 2 * kv_cols
    w_proj = gathered[:, :proj_cols]
    w_out_t = gathered[:, proj_cols : proj_cols + w_out.shape[0]]
    all_mask = gathered[:, proj_cols + w_out.shape[0] : proj_cols + w_out.shape[0] + mask_cols]
    all_mask = all_mask.reshape(stream)
    w_gate_perm = gate_ring.reshape(-1, g_cols)

    wide_tokens = tokens.astype(jnp.float32)
    full_width = tokens.shape[1] * lax.axis_size("mdl")
    square_part = jnp.sum(wide_tokens * wide_tokens, axis=1)
    n_mdl_in = lax.axis_size("mdl")
    square_part = square_part + lax.ppermute(
        square_part, "mdl", [(m, m ^ 1) for m in range(n_mdl_in)]
    )
    square_total = square_part + lax.ppermute(
        square_part, "mdl", [(m, m ^ 2) for m in range(n_mdl_in)]
    )
    scaled = (
        wide_tokens
        * lax.rsqrt(square_total / full_width + epsilon)[:, None]
        * norm_gain.astype(jnp.float32)
    )
    normalized_input = gather_mdl(scaled.astype(jnp.bfloat16))
    projected = jnp.dot(normalized_input, w_proj, preferred_element_type=jnp.float32)
    query_rows = projected[:, :q_cols]
    unprojected_keys = projected[:, q_cols : q_cols + kv_cols]
    values_raw = projected[:, q_cols + kv_cols : q_cols + 2 * kv_cols]
    my_y = lax.axis_index("y")
    input_perm = normalized_input.reshape(local_rows, 8, 4, 2, weight_rows)
    input_perm = jnp.roll(input_perm, -my_y, axis=2)
    input_perm = input_perm.transpose(0, 2, 1, 3, 4).reshape(local_rows, -1)
    gate_logits = jnp.dot(input_perm, w_gate_perm, preferred_element_type=jnp.float32)

    device_seq = lax.axis_index(SEQ_PARTS)
    token_ids = device_seq * local_rows + jnp.arange(local_rows, dtype=jnp.int32)
    starts = jnp.cumsum(prompt_lengths) - prompt_lengths
    ends = starts + prompt_lengths
    requests = jnp.arange(request_count, dtype=jnp.int32)
    member = (requests[:, None] > tenant_ranges[None, :, 0]) & (
        requests[:, None] < tenant_ranges[None, :, 1]
    )
    shared_of = jnp.sum(jnp.where(member, tenant_ranges[None, :, 0] + 3, 0), axis=1) - 3
    onehot = segment_ids[:, None] == requests[None, :]
    seg_start = jnp.sum(jnp.where(onehot, starts[None, :], 0), axis=1)
    shared_req = jnp.sum(jnp.where(onehot, shared_of[None, :], 0), axis=1)
    position = token_ids - seg_start

    query_heads = q_cols // HEAD_SIZE
    kv_heads = kv_cols // HEAD_SIZE
    group = query_heads // kv_heads
    q_rot = (
        rotate(head_norm(query_rows.reshape(local_rows, query_heads, HEAD_SIZE), q_gain), position)
        .astype(jnp.bfloat16)
        .reshape(local_rows, kv_heads, group, HEAD_SIZE)
    )
    k_rot = (
        rotate(head_norm(unprojected_keys.reshape(local_rows, kv_heads, HEAD_SIZE), k_gain), position)
        .astype(jnp.bfloat16)
        .reshape(local_rows, kv_cols)
    )
    values_flat = values_raw.astype(jnp.bfloat16)
    kv_pair = lax.all_gather(jnp.concatenate([k_rot, values_flat], axis=1), "xh", axis=0, tiled=True)
    v_part = lax.all_gather(kv_pair[:, kv_cols:], "z", axis=0, tiled=True)
    k_part = ring_y_kernel(kv_pair[:, :kv_cols], 2).reshape(-1, kv_cols)
    k_part, v_part = lax.optimization_barrier((k_part, v_part))
    k_all = lax.all_gather(k_part, "z", axis=0, tiled=True)
    v_ring = ring_y_kernel(v_part, 3).reshape(-1, kv_cols)

    def k_row_of(token):
        block = token // local_rows
        rel = (block // 2 % 4 - my_y) % 4
        place = ((block // 8) * 4 + rel) * 2 + block % 2
        return place * local_rows + token % local_rows

    def v_row_of(token):
        block = token // local_rows
        rel = (block // 2 % 4 - my_y) % 4
        place = (block // 8) * 2 + block % 2
        return (rel * 16 + place) * local_rows + token % local_rows

    n_blocks = stream // KEY_BLOCK
    block_ids = jnp.arange(n_blocks, dtype=jnp.int32)
    last_block = (device_seq * local_rows + local_rows - 1) // KEY_BLOCK
    first_block = jnp.min(seg_start) // KEY_BLOCK
    needed = (block_ids >= first_block) & (block_ids <= last_block)
    lo = tenant_ranges[:, 0]
    hi = tenant_ranges[:, 1]
    used = jnp.any(
        (segment_ids[:, None] > lo[None, :]) & (segment_ids[:, None] < hi[None, :]), axis=0
    )
    lo_start = jnp.sum(jnp.where(requests[None, :] == lo[:, None], starts[None, :], 0), axis=1)
    lo_end = jnp.sum(jnp.where(requests[None, :] == lo[:, None], ends[None, :], 0), axis=1)
    in_prompt = (
        used[:, None]
        & (block_ids[None, :] >= (lo_start // KEY_BLOCK)[:, None])
        & (block_ids[None, :] <= ((lo_end - 1) // KEY_BLOCK)[:, None])
    )
    needed = needed | jnp.any(in_prompt, axis=0)
    n_needed = jnp.sum(needed.astype(jnp.int32))
    (block_list,) = jnp.nonzero(needed, size=n_blocks, fill_value=0)
    block_list = block_list.astype(jnp.int32)

    row_segs = segment_ids
    row_shared = shared_req
    scale_factor = HEAD_SIZE ** (-0.5)
    head_shape = (local_rows, kv_heads, group)

    stream_ids = jnp.arange(stream, dtype=jnp.int32)
    key_segs = jnp.sum((stream_ids[:, None] >= ends[None, :]).astype(jnp.int32), axis=1)
    key_tags = jnp.where(all_mask == 1, key_segs, -2)

    def key_block(i, loop_state):
        old_top, old_totals, old_summed = loop_state
        block = block_list[i]
        offset = block * KEY_BLOCK
        keys_part = lax.dynamic_slice_in_dim(k_all, k_row_of(offset), KEY_BLOCK, 0).reshape(
            KEY_BLOCK, kv_heads, HEAD_SIZE
        )
        values_part = lax.dynamic_slice_in_dim(v_ring, v_row_of(offset), KEY_BLOCK, 0).reshape(
            KEY_BLOCK, kv_heads, HEAD_SIZE
        )
        tag_part = lax.dynamic_slice_in_dim(key_tags, offset, KEY_BLOCK, 0)
        columns = offset + jnp.arange(KEY_BLOCK, dtype=jnp.int32)
        own = tag_part[None, :] == row_segs[:, None]
        other = tag_part[None, :] == row_shared[:, None]
        earlier = columns[None, :] <= token_ids[:, None]
        diagonal = columns[None, :] == token_ids[:, None]
        visible = diagonal | (earlier & (own | other))
        allowed = visible[:, None, None, :]
        scores = (
            jnp.einsum("qhgd,khd->qhgk", q_rot, keys_part, preferred_element_type=jnp.float32)
            * scale_factor
        )
        scores = jnp.where(allowed, scores, masked_score)
        new_top = jnp.maximum(old_top, jnp.max(scores, axis=-1))
        factor = jnp.exp(old_top - new_top)
        raw_weights = jnp.where(allowed, jnp.exp(scores - new_top[..., None]), 0.0)
        new_totals = old_totals * factor + jnp.sum(raw_weights, axis=-1)
        new_summed = old_summed * factor[..., None] + jnp.einsum(
            "qhgk,khd->qhgd",
            raw_weights.astype(jnp.bfloat16),
            values_part,
            preferred_element_type=jnp.float32,
        )
        return (new_top, new_totals, new_summed)

    slots = block_list[:BATCH_BLOCKS]
    slot_live = jnp.arange(BATCH_BLOCKS, dtype=jnp.int32) < n_needed
    slot_offsets = slots * KEY_BLOCK
    keys_b = jnp.stack(
        [lax.dynamic_slice_in_dim(k_all, k_row_of(o), KEY_BLOCK, 0) for o in slot_offsets]
    ).reshape(BATCH_BLOCKS * KEY_BLOCK, kv_heads, HEAD_SIZE)
    values_b = jnp.stack(
        [lax.dynamic_slice_in_dim(v_ring, v_row_of(o), KEY_BLOCK, 0) for o in slot_offsets]
    ).reshape(BATCH_BLOCKS * KEY_BLOCK, kv_heads, HEAD_SIZE)
    tags_b = jnp.stack(
        [lax.dynamic_slice_in_dim(key_tags, o, KEY_BLOCK, 0) for o in slot_offsets]
    ).reshape(-1)
    columns_b = (slot_offsets[:, None] + jnp.arange(KEY_BLOCK, dtype=jnp.int32)[None, :]).reshape(-1)
    live_b = jnp.repeat(slot_live, KEY_BLOCK)
    visible_b = live_b[None, :] & (
        (columns_b[None, :] == token_ids[:, None])
        | (
            (columns_b[None, :] <= token_ids[:, None])
            & ((tags_b[None, :] == row_segs[:, None]) | (tags_b[None, :] == row_shared[:, None]))
        )
    )
    allowed_b = visible_b[:, None, None, :]
    scores_b = (
        jnp.einsum("qhgd,khd->qhgk", q_rot, keys_b, preferred_element_type=jnp.float32)
        * scale_factor
    )
    scores_b = jnp.where(allowed_b, scores_b, masked_score)
    top_b = jnp.max(scores_b, axis=-1)
    raw_b = jnp.where(allowed_b, jnp.exp(scores_b - top_b[..., None]), 0.0)
    totals_b = jnp.sum(raw_b, axis=-1)
    summed_b = jnp.einsum(
        "qhgk,khd->qhgd", raw_b.astype(jnp.bfloat16), values_b, preferred_element_type=jnp.float32
    )
    start_state = (top_b, totals_b, summed_b)
    top_now, totals, summed = lax.fori_loop(
        jnp.minimum(n_needed, BATCH_BLOCKS), n_needed, key_block, start_state
    )

    my_request = jnp.sum(jnp.where(cache_slot == device_seq, requests, 0))
    my_start = jnp.sum(jnp.where(requests == my_request, starts, 0))
    my_length = jnp.sum(jnp.where(requests == my_request, prompt_lengths, 0))
    offsets = jnp.arange(LMAX, dtype=jnp.int32)
    wanted = my_start + offsets
    in_window = ((wanted < stream) & (offsets < my_length))[:, None]
    zero = jnp.zeros((), jnp.bfloat16)
    first = my_start // KEY_BLOCK
    shift = my_start % KEY_BLOCK
    spans = [jnp.clip(first + j, 0, n_blocks - 1) * KEY_BLOCK for j in range(3)]

    def cache_of(table, row_of):
        pieces = [lax.dynamic_slice_in_dim(table, row_of(b), KEY_BLOCK, 0) for b in spans]
        window = lax.dynamic_slice_in_dim(jnp.concatenate(pieces, axis=0), shift, LMAX, 0)
        return jnp.where(in_window, window, zero)

    cache_k = cache_of(k_all, k_row_of)
    cache_v = cache_of(v_ring, v_row_of)

    attended = (summed / totals[..., None]).reshape(local_rows, query_heads * HEAD_SIZE)
    gated_heads = (attended * jax.nn.sigmoid(gate_logits)).astype(jnp.bfloat16)
    partial_out = lax.dot_general(
        gated_heads,
        w_out_t,
        (((1,), (1,)), ((), ())),
        preferred_element_type=jnp.float32,
    )
    mdl_index = lax.axis_index("mdl")
    n_mdl = lax.axis_size("mdl")
    x_lo = mdl_index // 2
    core = mdl_index % 2
    quarter = partial_out.shape[1] // 4

    def cols_of(block):
        return lax.dynamic_slice_in_dim(partial_out, block * quarter, quarter, 1)

    mine = jnp.concatenate([cols_of(core), cols_of(2 + core)], axis=1)
    theirs = jnp.concatenate([cols_of(1 - core), cols_of(3 - core)], axis=1)
    pair_sum = mine + lax.ppermute(theirs, "mdl", [(m, m ^ 1) for m in range(n_mdl)])
    mine = lax.dynamic_slice_in_dim(pair_sum, x_lo * quarter, quarter, 1)
    theirs = lax.dynamic_slice_in_dim(pair_sum, (1 - x_lo) * quarter, quarter, 1)
    across = lax.ppermute(
        theirs.astype(jnp.bfloat16), "mdl", [(m, m ^ 2) for m in range(n_mdl)]
    )
    branch_sum = mine + across.astype(jnp.float32)
    layer_out = (wide_tokens + branch_sum).astype(jnp.bfloat16)
    return (layer_out, cache_k[None], cache_v[None])


def solution(mesh):
    seq = SEQ_PARTS
    split = Mesh(mesh.devices.reshape(8, 4, 2, mesh.shape["mdl"]), SEQ_PARTS + ("mdl",))
    placed = (
        P(seq, "mdl"),
        P("mdl"),
        P(seq, "mdl"),
        P(seq, "mdl"),
        P(seq, "mdl"),
        P(seq, "mdl"),
        P(),
        P(),
        P("mdl", seq),
        P(),
        P(seq),
        P(),
        P(seq),
        P(),
    )
    return jax.shard_map(
        body,
        mesh=split,
        in_specs=placed,
        out_specs=(P(seq, "mdl"), P(seq, None, "mdl"), P(seq, None, "mdl")),
        check_vma=False,
    )
```

```python
import jax
import jax.numpy as jnp
from jax import lax
from jax.experimental import pallas as pl
from jax.experimental.pallas import tpu as pltpu
from jax.sharding import Mesh
from jax.sharding import PartitionSpec as P

HEAD_SIZE = 128
LMAX = 512
KEY_BLOCK = 256
BATCH_BLOCKS = 5


epsilon = 1e-06
rope_base = 1000000.0
masked_score = -1e30


def head_norm(values, gain_vector):
    return (
        values
        * lax.rsqrt(jnp.mean(values * values, axis=-1, keepdims=True) + epsilon)
        * gain_vector
    )


def rotate(values, position):
    half_width = values.shape[-1] // 2
    frequency = rope_base ** (-2.0 * jnp.arange(half_width, dtype=jnp.float32) / values.shape[-1])
    angles = position.astype(jnp.float32)[:, None] * frequency[None, :]
    cosine = jnp.cos(angles)[:, None, :]
    sine_part = jnp.sin(angles)[:, None, :]
    former = values[..., :half_width]
    latter = values[..., half_width:]
    return jnp.concatenate(
        [former * cosine - latter * sine_part, latter * cosine + former * sine_part], axis=-1
    )


SEQ_PARTS = ("z", "y", "xh")
MESH_ID = pl.DeviceIdType.MESH
AXES = SEQ_PARTS + ("mdl",)


def _ring_kernel(x_ref, out_ref, send_sem, recv_sem, local_sem):
    ny = 4
    me = {name: lax.axis_index(name) for name in AXES}
    my_y = me["y"]

    def dev(yy):
        return tuple(yy if name == "y" else me[name] for name in AXES)

    plus = dev(lax.rem(my_y + 1, ny))
    minus = dev(lax.rem(my_y + ny - 1, ny))
    barrier = pltpu.get_barrier_semaphore()
    for d in (plus, minus):
        pl.semaphore_signal(barrier, inc=1, device_id=d, device_id_type=MESH_ID)
    pl.semaphore_wait(barrier, 2)

    rows = x_ref.shape[0]
    half = rows // 2
    to_minus = pltpu.make_async_remote_copy(
        src_ref=x_ref, dst_ref=out_ref.at[1], send_sem=send_sem.at[0], recv_sem=recv_sem.at[0],
        device_id=minus, device_id_type=MESH_ID)
    to_plus = pltpu.make_async_remote_copy(
        src_ref=x_ref, dst_ref=out_ref.at[3], send_sem=send_sem.at[1], recv_sem=recv_sem.at[1],
        device_id=plus, device_id_type=MESH_ID)
    own = pltpu.make_async_copy(x_ref, out_ref.at[0], local_sem.at[0])
    to_minus.start()
    to_plus.start()
    to_minus.wait_recv()
    on_minus = pltpu.make_async_remote_copy(
        src_ref=out_ref.at[1, pl.ds(0, half)], dst_ref=out_ref.at[2, pl.ds(0, half)],
        send_sem=send_sem.at[2], recv_sem=recv_sem.at[2], device_id=minus, device_id_type=MESH_ID)
    on_minus.start()
    to_plus.wait_recv()
    on_plus = pltpu.make_async_remote_copy(
        src_ref=out_ref.at[3, pl.ds(half, rows - half)], dst_ref=out_ref.at[2, pl.ds(half, rows - half)],
        send_sem=send_sem.at[3], recv_sem=recv_sem.at[3], device_id=plus, device_id_type=MESH_ID)
    on_plus.start()
    own.start()
    to_minus.wait_send()
    to_plus.wait_send()
    own.wait()
    on_minus.wait_send()
    on_plus.wait_send()
    on_minus.wait_recv()
    on_plus.wait_recv()


def ring_y_kernel(x, collective_id):
    rows, width = x.shape
    return pl.pallas_call(
        _ring_kernel,
        out_shape=jax.ShapeDtypeStruct((4, rows, width), x.dtype),
        in_specs=[pl.BlockSpec(memory_space=pl.ANY)],
        out_specs=pl.BlockSpec(memory_space=pl.ANY),
        scratch_shapes=[
            pltpu.SemaphoreType.DMA((4,)),
            pltpu.SemaphoreType.DMA((4,)),
            pltpu.SemaphoreType.DMA((1,)),
        ],
        compiler_params=pltpu.CompilerParams(collective_id=collective_id, has_side_effects=True),
    )(x)


def gather_seq(x):
    for name in reversed(SEQ_PARTS):
        x = lax.all_gather(x, name, axis=0, tiled=True)
    return x


def gather_xh_z(x):
    x = lax.all_gather(x, "xh", axis=0, tiled=True)
    return lax.all_gather(x, "z", axis=0, tiled=True)


def ring_y(x):
    ny = 4
    right = [(i, (i + 1) % ny) for i in range(ny)]
    left = [(i, (i - 1) % ny) for i in range(ny)]
    from_minus = lax.ppermute(x, "y", right)
    from_plus = lax.ppermute(x, "y", left)
    half = x.shape[0] // 2
    opp_a = lax.ppermute(from_minus[:half], "y", right)
    opp_b = lax.ppermute(from_plus[half:], "y", left)
    opposite = jnp.concatenate([opp_a, opp_b], axis=0)
    return jnp.stack([x, from_plus, opposite, from_minus])


def gather_mdl(x):
    mdl_index = lax.axis_index("mdl")
    n_mdl = lax.axis_size("mdl")
    other = lax.ppermute(x, "mdl", [(m, m ^ 1) for m in range(n_mdl)])
    pair = jnp.where(
        mdl_index % 2 == 0,
        jnp.concatenate([x, other], axis=1),
        jnp.concatenate([other, x], axis=1),
    )
    other = lax.ppermute(pair, "mdl", [(m, m ^ 2) for m in range(n_mdl)])
    return jnp.where(
        mdl_index // 2 == 0,
        jnp.concatenate([pair, other], axis=1),
        jnp.concatenate([other, pair], axis=1),
    )


def body(
    tokens,
    norm_gain,
    w_query,
    key_matrix,
    value_matrix,
    w_gate,
    q_gain,
    k_gain,
    w_out,
    prompt_lengths,
    segment_ids,
    tenant_ranges,
    key_mask,
    cache_slot,
):
    local_rows = tokens.shape[0]
    weight_rows = w_query.shape[0]
    q_cols = w_query.shape[1]
    kv_cols = key_matrix.shape[1]
    g_cols = w_gate.shape[1]
    seq_size = lax.axis_size(SEQ_PARTS)
    stream = local_rows * seq_size
    request_count = prompt_lengths.shape[0]

    mask_cols = local_rows // weight_rows
    mask_block = key_mask.astype(jnp.bfloat16).reshape(weight_rows, mask_cols)
    mask_block = jnp.pad(mask_block, ((0, 0), (0, 128 - mask_cols)))
    packed = jnp.concatenate([w_query, key_matrix, value_matrix, w_out.T, mask_block], axis=1)
    packed = lax.all_gather(packed, "xh", axis=0, tiled=True)
    packed = lax.all_gather(packed, "y", axis=0, tiled=True)
    packed, gate_in = lax.optimization_barrier((packed, w_gate))
    gate_ring = ring_y_kernel(gather_xh_z(gate_in), 1)
    gathered = lax.all_gather(packed, "z", axis=0, tiled=True)
    gathered, gate_ring = lax.optimization_barrier((gathered, gate_ring))
    proj_cols = q_cols + 2 * kv_cols
    w_proj = gathered[:, :proj_cols]
    w_out_t = gathered[:, proj_cols : proj_cols + w_out.shape[0]]
    all_mask = gathered[:, proj_cols + w_out.shape[0] : proj_cols + w_out.shape[0] + mask_cols]
    all_mask = all_mask.reshape(stream)
    w_gate_perm = gate_ring.reshape(-1, g_cols)

    wide_tokens = tokens.astype(jnp.float32)
    full_width = tokens.shape[1] * lax.axis_size("mdl")
    square_part = jnp.sum(wide_tokens * wide_tokens, axis=1)
    n_mdl_in = lax.axis_size("mdl")
    square_part = square_part + lax.ppermute(
        square_part, "mdl", [(m, m ^ 1) for m in range(n_mdl_in)]
    )
    square_total = square_part + lax.ppermute(
        square_part, "mdl", [(m, m ^ 2) for m in range(n_mdl_in)]
    )
    scaled = (
        wide_tokens
        * lax.rsqrt(square_total / full_width + epsilon)[:, None]
        * norm_gain.astype(jnp.float32)
    )
    normalized_input = gather_mdl(scaled.astype(jnp.bfloat16))
    projected = jnp.dot(normalized_input, w_proj, preferred_element_type=jnp.float32)
    query_rows = projected[:, :q_cols]
    unprojected_keys = projected[:, q_cols : q_cols + kv_cols]
    values_raw = projected[:, q_cols + kv_cols : q_cols + 2 * kv_cols]
    my_y = lax.axis_index("y")
    input_perm = normalized_input.reshape(local_rows, 8, 4, 2, weight_rows)
    input_perm = jnp.roll(input_perm, -my_y, axis=2)
    input_perm = input_perm.transpose(0, 2, 1, 3, 4).reshape(local_rows, -1)
    gate_logits = jnp.dot(input_perm, w_gate_perm, preferred_element_type=jnp.float32)

    device_seq = lax.axis_index(SEQ_PARTS)
    token_ids = device_seq * local_rows + jnp.arange(local_rows, dtype=jnp.int32)
    starts = jnp.cumsum(prompt_lengths) - prompt_lengths
    ends = starts + prompt_lengths
    requests = jnp.arange(request_count, dtype=jnp.int32)
    member = (requests[:, None] > tenant_ranges[None, :, 0]) & (
        requests[:, None] < tenant_ranges[None, :, 1]
    )
    shared_of = jnp.sum(jnp.where(member, tenant_ranges[None, :, 0] + 3, 0), axis=1) - 3
    onehot = segment_ids[:, None] == requests[None, :]
    seg_start = jnp.sum(jnp.where(onehot, starts[None, :], 0), axis=1)
    shared_req = jnp.sum(jnp.where(onehot, shared_of[None, :], 0), axis=1)
    position = token_ids - seg_start

    query_heads = q_cols // HEAD_SIZE
    kv_heads = kv_cols // HEAD_SIZE
    group = query_heads // kv_heads
    q_rot = (
        rotate(head_norm(query_rows.reshape(local_rows, query_heads, HEAD_SIZE), q_gain), position)
        .astype(jnp.bfloat16)
        .reshape(local_rows, kv_heads, group, HEAD_SIZE)
    )
    k_rot = (
        rotate(head_norm(unprojected_keys.reshape(local_rows, kv_heads, HEAD_SIZE), k_gain), position)
        .astype(jnp.bfloat16)
        .reshape(local_rows, kv_cols)
    )
    values_flat = values_raw.astype(jnp.bfloat16)
    kv_pair = lax.all_gather(jnp.concatenate([k_rot, values_flat], axis=1), "xh", axis=0, tiled=True)
    v_part = lax.all_gather(kv_pair[:, kv_cols:], "z", axis=0, tiled=True)
    k_part = ring_y_kernel(kv_pair[:, :kv_cols], 2).reshape(-1, kv_cols)
    k_part, v_part = lax.optimization_barrier((k_part, v_part))
    k_all = lax.all_gather(k_part, "z", axis=0, tiled=True)
    v_ring = ring_y_kernel(v_part, 3).reshape(-1, kv_cols)

    def k_row_of(token):
        block = token // local_rows
        rel = (block // 2 % 4 - my_y) % 4
        place = ((block // 8) * 4 + rel) * 2 + block % 2
        return place * local_rows + token % local_rows

    def v_row_of(token):
        block = token // local_rows
        rel = (block // 2 % 4 - my_y) % 4
        place = (block // 8) * 2 + block % 2
        return (rel * 16 + place) * local_rows + token % local_rows

    n_blocks = stream // KEY_BLOCK
    block_ids = jnp.arange(n_blocks, dtype=jnp.int32)
    last_block = (device_seq * local_rows + local_rows - 1) // KEY_BLOCK
    first_block = jnp.min(seg_start) // KEY_BLOCK
    needed = (block_ids >= first_block) & (block_ids <= last_block)
    lo = tenant_ranges[:, 0]
    hi = tenant_ranges[:, 1]
    used = jnp.any(
        (segment_ids[:, None] > lo[None, :]) & (segment_ids[:, None] < hi[None, :]), axis=0
    )
    lo_start = jnp.sum(jnp.where(requests[None, :] == lo[:, None], starts[None, :], 0), axis=1)
    lo_end = jnp.sum(jnp.where(requests[None, :] == lo[:, None], ends[None, :], 0), axis=1)
    in_prompt = (
        used[:, None]
        & (block_ids[None, :] >= (lo_start // KEY_BLOCK)[:, None])
        & (block_ids[None, :] <= ((lo_end - 1) // KEY_BLOCK)[:, None])
    )
    needed = needed | jnp.any(in_prompt, axis=0)
    n_needed = jnp.sum(needed.astype(jnp.int32))
    (block_list,) = jnp.nonzero(needed, size=n_blocks, fill_value=0)
    block_list = block_list.astype(jnp.int32)

    row_segs = segment_ids
    row_shared = shared_req
    scale_factor = HEAD_SIZE ** (-0.5)
    head_shape = (local_rows, kv_heads, group)

    stream_ids = jnp.arange(stream, dtype=jnp.int32)
    key_segs = jnp.sum((stream_ids[:, None] >= ends[None, :]).astype(jnp.int32), axis=1)
    key_tags = jnp.where(all_mask == 1, key_segs, -2)

    def key_block(i, loop_state):
        old_top, old_totals, old_summed = loop_state
        block = block_list[i]
        offset = block * KEY_BLOCK
        keys_part = lax.dynamic_slice_in_dim(k_all, k_row_of(offset), KEY_BLOCK, 0).reshape(
            KEY_BLOCK, kv_heads, HEAD_SIZE
        )
        values_part = lax.dynamic_slice_in_dim(v_ring, v_row_of(offset), KEY_BLOCK, 0).reshape(
            KEY_BLOCK, kv_heads, HEAD_SIZE
        )
        tag_part = lax.dynamic_slice_in_dim(key_tags, offset, KEY_BLOCK, 0)
        columns = offset + jnp.arange(KEY_BLOCK, dtype=jnp.int32)
        own = tag_part[None, :] == row_segs[:, None]
        other = tag_part[None, :] == row_shared[:, None]
        earlier = columns[None, :] <= token_ids[:, None]
        diagonal = columns[None, :] == token_ids[:, None]
        visible = diagonal | (earlier & (own | other))
        allowed = visible[:, None, None, :]
        scores = (
            jnp.einsum("qhgd,khd->qhgk", q_rot, keys_part, preferred_element_type=jnp.float32)
            * scale_factor
        )
        scores = jnp.where(allowed, scores, masked_score)
        new_top = jnp.maximum(old_top, jnp.max(scores, axis=-1))
        factor = jnp.exp(old_top - new_top)
        raw_weights = jnp.where(allowed, jnp.exp(scores - new_top[..., None]), 0.0)
        new_totals = old_totals * factor + jnp.sum(raw_weights, axis=-1)
        new_summed = old_summed * factor[..., None] + jnp.einsum(
            "qhgk,khd->qhgd",
            raw_weights.astype(jnp.bfloat16),
            values_part,
            preferred_element_type=jnp.float32,
        )
        return (new_top, new_totals, new_summed)

    slots = block_list[:BATCH_BLOCKS]
    slot_live = jnp.arange(BATCH_BLOCKS, dtype=jnp.int32) < n_needed
    slot_offsets = slots * KEY_BLOCK
    keys_b = jnp.stack(
        [lax.dynamic_slice_in_dim(k_all, k_row_of(o), KEY_BLOCK, 0) for o in slot_offsets]
    ).reshape(BATCH_BLOCKS * KEY_BLOCK, kv_heads, HEAD_SIZE)
    values_b = jnp.stack(
        [lax.dynamic_slice_in_dim(v_ring, v_row_of(o), KEY_BLOCK, 0) for o in slot_offsets]
    ).reshape(BATCH_BLOCKS * KEY_BLOCK, kv_heads, HEAD_SIZE)
    tags_b = jnp.stack(
        [lax.dynamic_slice_in_dim(key_tags, o, KEY_BLOCK, 0) for o in slot_offsets]
    ).reshape(-1)
    columns_b = (slot_offsets[:, None] + jnp.arange(KEY_BLOCK, dtype=jnp.int32)[None, :]).reshape(-1)
    live_b = jnp.repeat(slot_live, KEY_BLOCK)
    visible_b = live_b[None, :] & (
        (columns_b[None, :] == token_ids[:, None])
        | (
            (columns_b[None, :] <= token_ids[:, None])
            & ((tags_b[None, :] == row_segs[:, None]) | (tags_b[None, :] == row_shared[:, None]))
        )
    )
    allowed_b = visible_b[:, None, None, :]
    scores_b = (
        jnp.einsum("qhgd,khd->qhgk", q_rot, keys_b, preferred_element_type=jnp.float32)
        * scale_factor
    )
    scores_b = jnp.where(allowed_b, scores_b, masked_score)
    top_b = jnp.max(scores_b, axis=-1)
    raw_b = jnp.where(allowed_b, jnp.exp(scores_b - top_b[..., None]), 0.0)
    totals_b = jnp.sum(raw_b, axis=-1)
    summed_b = jnp.einsum(
        "qhgk,khd->qhgd", raw_b.astype(jnp.bfloat16), values_b, preferred_element_type=jnp.float32
    )
    start_state = (top_b, totals_b, summed_b)
    top_now, totals, summed = lax.fori_loop(
        jnp.minimum(n_needed, BATCH_BLOCKS), n_needed, key_block, start_state
    )

    my_request = jnp.sum(jnp.where(cache_slot == device_seq, requests, 0))
    my_start = jnp.sum(jnp.where(requests == my_request, starts, 0))
    my_length = jnp.sum(jnp.where(requests == my_request, prompt_lengths, 0))
    offsets = jnp.arange(LMAX, dtype=jnp.int32)
    wanted = my_start + offsets
    in_window = ((wanted < stream) & (offsets < my_length))[:, None]
    zero = jnp.zeros((), jnp.bfloat16)
    first = my_start // KEY_BLOCK
    shift = my_start % KEY_BLOCK
    spans = [jnp.clip(first + j, 0, n_blocks - 1) * KEY_BLOCK for j in range(3)]

    def cache_of(table, row_of):
        pieces = [lax.dynamic_slice_in_dim(table, row_of(b), KEY_BLOCK, 0) for b in spans]
        window = lax.dynamic_slice_in_dim(jnp.concatenate(pieces, axis=0), shift, LMAX, 0)
        return jnp.where(in_window, window, zero)

    cache_k = cache_of(k_all, k_row_of)
    cache_v = cache_of(v_ring, v_row_of)

    attended = (summed / totals[..., None]).reshape(local_rows, query_heads * HEAD_SIZE)
    gated_heads = (attended * jax.nn.sigmoid(gate_logits)).astype(jnp.bfloat16)
    partial_out = lax.dot_general(
        gated_heads,
        w_out_t,
        (((1,), (1,)), ((), ())),
        preferred_element_type=jnp.float32,
    )
    mdl_index = lax.axis_index("mdl")
    n_mdl = lax.axis_size("mdl")
    x_lo = mdl_index // 2
    core = mdl_index % 2
    quarter = partial_out.shape[1] // 4

    def cols_of(block):
        return lax.dynamic_slice_in_dim(partial_out, block * quarter, quarter, 1)

    mine = jnp.concatenate([cols_of(core), cols_of(2 + core)], axis=1)
    theirs = jnp.concatenate([cols_of(1 - core), cols_of(3 - core)], axis=1)
    pair_sum = mine + lax.ppermute(theirs, "mdl", [(m, m ^ 1) for m in range(n_mdl)])
    mine = lax.dynamic_slice_in_dim(pair_sum, x_lo * quarter, quarter, 1)
    theirs = lax.dynamic_slice_in_dim(pair_sum, (1 - x_lo) * quarter, quarter, 1)
    across = lax.ppermute(
        theirs.astype(jnp.bfloat16), "mdl", [(m, m ^ 2) for m in range(n_mdl)]
    )
    branch_sum = mine + across.astype(jnp.float32)
    layer_out = (wide_tokens + branch_sum).astype(jnp.bfloat16)
    return (layer_out, cache_k[None], cache_v[None])


def solution(mesh):
    seq = SEQ_PARTS
    split = Mesh(mesh.devices.reshape(8, 4, 2, mesh.shape["mdl"]), SEQ_PARTS + ("mdl",))
    placed = (
        P(seq, "mdl"),
        P("mdl"),
        P(seq, "mdl"),
        P(seq, "mdl"),
        P(seq, "mdl"),
        P(seq, "mdl"),
        P(),
        P(),
        P("mdl", seq),
        P(),
        P(seq),
        P(),
        P(seq),
        P(),
    )
    return jax.shard_map(
        body,
        mesh=split,
        in_specs=placed,
        out_specs=(P(seq, "mdl"), P(seq, None, "mdl"), P(seq, None, "mdl")),
        check_vma=False,
    )
```
